512 devices in a mesh: img: 16 (over z, core), proto: 32 (over x, y).
Axes of the slice: x: 4, y: 8, z: 8, core: 2. Of those that a mesh axis runs over, the one named last changes fastest.
Arguments:
- images: bfloat16 [32768, 256], P('img'), may hold values from -24 to 24
- prototypes: bfloat16 [131072, 256], P('proto'), may hold values from -24 to 24
- tile_row: int32 [16, 32, 6], P('img', 'proto'), may hold values from 0 to 3
- tile_proto: int32 [16, 32, 6], P('img', 'proto'), may hold values from 0 to 7
- tile_valid: int32 [16, 32, 6], P('img', 'proto'), may hold values from 0 to 1, as said below
Outputs:
- proto_sums: float32 [131072, 256], P(('proto', 'img'))
- col_potential: float32 [131072], P('proto')
The draws below stay inside these ranges and needn't reach their ends.
Inputs may be any that keep to these rules, and one draw needn't show every extreme that they name: `tile_valid`: on every device the valid slots come before the padded ones, at least one slot is valid, and the valid slots name distinct (row block, prototype block) pairs; some device has all 6 slots valid. Every row block has a valid slot on some device of its img index, and every prototype block on some device of its proto index.
All inputs are finite; a program needn't handle non-finite values.
Results may differ from the reference program's by a relative error of at most 0.012.
Values may be sent and summed in bfloat16 or wider, within the bound.
A program may use at most 64 MiB of HBM per device.

```python
import math
import jax
import jax.numpy as jnp
from jax import lax

E = 256
TILE = 512
RB_DEV = 4
PB_DEV = 8
MAXT = 6
ITERS = 3
IMAGES = 32768
PROTOS = 131072
IMG_SHARDS = 16
PROTO_SHARDS = 32


def tile_layout(key):
    base_key = jax.random.fold_in(key, 101)
    sub_keys = jax.random.split(base_key, 7)
    shards_img = IMG_SHARDS
    shards_pro = PROTO_SHARDS
    pair_count = RB_DEV * PB_DEV
    needed = -(-PB_DEV // shards_img)
    order_img = jax.random.permutation(sub_keys[0], shards_img).astype(jnp.int32)
    order_pro = jax.random.permutation(sub_keys[1], shards_pro).astype(jnp.int32)
    pair_ids = jnp.arange(pair_count, dtype=jnp.int32)
    pair_rows = pair_ids // PB_DEV
    pair_blocks = pair_ids % PB_DEV
    forced = jnp.zeros((shards_img, shards_pro, pair_count), dtype=bool)
    for layer in range(needed):
        want_row = ((order_pro + layer) % RB_DEV)[None, :, None]
        want_block = ((order_img + layer * shards_img) % PB_DEV)[:, None, None]
        forced = forced | (pair_rows[None, None, :] == want_row) & (pair_blocks[None, None, :] == want_block)
    priority = jax.random.randint(sub_keys[2], (shards_img, shards_pro, pair_count), 0, 2 ** 20)
    ranking = jnp.where(forced, 0, 2 ** 29) + priority * 256 + pair_ids[None, None, :]
    picked = jnp.argsort(ranking, axis=-1)[..., :MAXT].astype(jnp.int32)
    first_extra = jax.random.randint(sub_keys[3], (shards_img, shards_pro), 0, MAXT - needed + 1)
    second_extra = jax.random.randint(sub_keys[4], (shards_img, shards_pro), 0, MAXT - needed + 1)
    fullest = jax.random.randint(sub_keys[5], (), 0, shards_img * shards_pro)
    device_ids = jnp.arange(shards_img * shards_pro, dtype=jnp.int32).reshape(shards_img, shards_pro)
    live_count = jnp.where(device_ids == fullest, MAXT, needed + jnp.minimum(first_extra, second_extra))
    slot_ids = jnp.arange(MAXT, dtype=jnp.int32)
    shuffle = jax.random.randint(sub_keys[6], (shards_img, shards_pro, MAXT), 0, 2 ** 20)
    arrange = jnp.where(slot_ids[None, None, :] < live_count[..., None], shuffle * 64 + slot_ids[None, None, :], 2 ** 28 + slot_ids[None, None, :])
    reorder = jnp.argsort(arrange, axis=-1)
    chosen = jnp.take_along_axis(picked, reorder, axis=-1)
    validity = (slot_ids[None, None, :] < live_count[..., None]).astype(jnp.int32)
    return ((chosen // PB_DEV).astype(jnp.int32), (chosen % PB_DEV).astype(jnp.int32), validity)


def embed_rows(key, row_count, salt):
    own_key = jax.random.fold_in(key, salt)
    scale_key, noise_key = jax.random.split(own_key, 2)
    scales = jnp.exp(jax.random.uniform(scale_key, (row_count, 1), jnp.float32, 0.0, math.log(10.0)))
    noise = jnp.clip(jax.random.normal(noise_key, (row_count, E), jnp.float32), -2.5, 2.5)
    return 0.5 * scales * noise


def draw_images(key, part):
    values = embed_rows(key, IMAGES, 201)
    return values.astype(jnp.bfloat16)


def draw_prototypes(key, part):
    values = embed_rows(key, PROTOS, 202)
    return values.astype(jnp.bfloat16)


def draw_tile_row(key, part):
    return tile_layout(key)[0]


def draw_tile_proto(key, part):
    return tile_layout(key)[1]


def draw_tile_valid(key, part):
    return tile_layout(key)[2]


def setup_inputs(seed: int = 0) -> dict:
    arg_keys = jax.random.split(jax.random.key(seed), 6)
    return {
        "images": draw_images(jax.random.fold_in(arg_keys[5], 71), 0),
        "prototypes": draw_prototypes(jax.random.fold_in(arg_keys[5], 71), 0),
        "tile_row": draw_tile_row(jax.random.fold_in(arg_keys[5], 71), 0),
        "tile_proto": draw_tile_proto(jax.random.fold_in(arg_keys[5], 71), 0),
        "tile_valid": draw_tile_valid(jax.random.fold_in(arg_keys[5], 71), 0),
    }


HIGHEST_PRECISION = lax.Precision.HIGHEST


def tile_scores(image_blocks, proto_blocks, img_shard, proto_shard, slot_rows, slot_protos):
    rows_here = image_blocks[img_shard][slot_rows]
    protos_here = proto_blocks[proto_shard][slot_protos]
    products = jnp.einsum("tae,tbe->tab", rows_here.astype(jnp.float32), protos_here.astype(jnp.float32), precision=HIGHEST_PRECISION)
    return products * (float(E) ** -0.5), rows_here


def reference(images, prototypes, tile_row, tile_proto, tile_valid):
    shards_img = IMG_SHARDS
    shards_pro = PROTO_SHARDS
    device_total = shards_img * shards_pro
    image_blocks = images.reshape(shards_img, RB_DEV, TILE, E)
    proto_blocks = prototypes.reshape(shards_pro, PB_DEV, TILE, E)
    rows_all = tile_row.reshape(device_total, MAXT).astype(jnp.int32)
    protos_all = tile_proto.reshape(device_total, MAXT).astype(jnp.int32)
    valid_all = tile_valid.reshape(device_total, MAXT) == 1
    device_ids = jnp.arange(device_total, dtype=jnp.int32)
    row_ids = jnp.arange(RB_DEV, dtype=jnp.int32)
    block_ids = jnp.arange(PB_DEV, dtype=jnp.int32)
    log_ratio = math.log(PROTOS / IMAGES)

    def row_pass(col_pot):
        def per_device(device):
            img_shard = device // shards_pro
            proto_shard = device % shards_pro
            slot_rows = rows_all[device]
            slot_protos = protos_all[device]
            scores, rows_here = tile_scores(image_blocks, proto_blocks, img_shard, proto_shard, slot_rows, slot_protos)
            values = scores + col_pot[proto_shard][slot_protos][:, None, :]
            per_slot = jax.nn.logsumexp(values, axis=2)
            chosen = (slot_rows[None, :] == row_ids[:, None]) & valid_all[device][None, :]
            stacked = jnp.where(chosen[:, :, None], per_slot[None], -jnp.inf)
            return jax.nn.logsumexp(stacked, axis=1)
        partials = lax.map(per_device, device_ids).reshape(shards_img, shards_pro, RB_DEV, TILE)
        return log_ratio - jax.nn.logsumexp(partials, axis=1)

    def col_pass(row_pot):
        def per_device(device):
            img_shard = device // shards_pro
            proto_shard = device % shards_pro
            slot_rows = rows_all[device]
            slot_protos = protos_all[device]
            scores, rows_here = tile_scores(image_blocks, proto_blocks, img_shard, proto_shard, slot_rows, slot_protos)
            values = scores + row_pot[img_shard][slot_rows][:, :, None]
            per_slot = jax.nn.logsumexp(values, axis=1)
            chosen = (slot_protos[None, :] == block_ids[:, None]) & valid_all[device][None, :]
            stacked = jnp.where(chosen[:, :, None], per_slot[None], -jnp.inf)
            return jax.nn.logsumexp(stacked, axis=1)
        partials = lax.map(per_device, device_ids).reshape(shards_img, shards_pro, PB_DEV, TILE)
        return -jax.nn.logsumexp(partials, axis=0)

    col_pot = jnp.zeros((shards_pro, PB_DEV, TILE), jnp.float32)
    row_pot = jnp.zeros((shards_img, RB_DEV, TILE), jnp.float32)
    for iteration in range(ITERS):
        row_pot = row_pass(col_pot)
        col_pot = col_pass(row_pot)

    def add_device(running_sum, device):
        img_shard = device // shards_pro
        proto_shard = device % shards_pro
        slot_rows = rows_all[device]
        slot_protos = protos_all[device]
        valid = valid_all[device]
        scores, rows_here = tile_scores(image_blocks, proto_blocks, img_shard, proto_shard, slot_rows, slot_protos)
        weights = jnp.exp(scores + row_pot[img_shard][slot_rows][:, :, None] + col_pot[proto_shard][slot_protos][:, None, :])
        weights = jnp.where(valid[:, None, None], weights, 0.0).astype(jnp.bfloat16)
        contribution = jnp.einsum("tab,tae->tbe", weights.astype(jnp.float32), rows_here.astype(jnp.float32), precision=HIGHEST_PRECISION)
        block_hits = ((slot_protos[:, None] == block_ids[None, :]) & valid[:, None]).astype(jnp.float32)
        block_term = jnp.einsum("tk,tbe->kbe", block_hits, contribution, precision=HIGHEST_PRECISION)
        rounded = lax.optimization_barrier(block_term.astype(jnp.bfloat16)).astype(jnp.float32)
        return running_sum.at[proto_shard].add(rounded), None

    start_sum = jnp.zeros((shards_pro, PB_DEV, TILE, E), jnp.float32)
    running_sum, unused = lax.scan(add_device, start_sum, device_ids)
    return running_sum.reshape(PROTOS, E), col_pot.reshape(PROTOS)
```

```python
import math

import jax
import jax.numpy as jnp
from jax import lax
from jax.sharding import PartitionSpec as P

E = 256
TILE = 512
RB_DEV = 4
PB_DEV = 8
MAXT = 6
ITERS = 3


far_below = -1e30


def running_top(values_of, live_slots, reduced, slot_blocks, block_count):

    def advance(position, tops):
        local_top = jnp.max(values_of(position), axis=reduced)
        target = slot_blocks[position]
        old_top = lax.dynamic_index_in_dim(tops, target, 0, keepdims=False)
        return lax.dynamic_update_index_in_dim(tops, jnp.maximum(old_top, local_top), target, 0)

    return lax.fori_loop(
        0, live_slots, advance, jnp.full((block_count, TILE), far_below, jnp.float32)
    )


def running_mass(values_of, live_slots, reduced, slot_blocks, tops):

    def advance(position, masses):
        target = slot_blocks[position]
        top_here = lax.dynamic_index_in_dim(tops, target, 0, keepdims=False)
        local_mass = jnp.sum(
            jnp.exp(values_of(position) - jnp.expand_dims(top_here, reduced)), axis=reduced
        )
        old_mass = lax.dynamic_index_in_dim(masses, target, 0, keepdims=False)
        return lax.dynamic_update_index_in_dim(masses, old_mass + local_mass, target, 0)

    return lax.fori_loop(0, live_slots, advance, jnp.zeros_like(tops))


def merge_tops(local_top, local_mass, axis):
    gathered = lax.all_gather(jnp.stack([local_top, local_mass]), axis)
    tops, masses = gathered[:, 0], gathered[:, 1]
    highest = jnp.max(tops, axis=0)
    summed = jnp.sum(masses * jnp.exp(tops - highest[None]), axis=0)
    return highest, summed


def shards(images, prototypes, tile_row, tile_proto, tile_valid):
    img_count = lax.axis_size("img")
    proto_count = lax.axis_size("proto")
    image_blocks = images.reshape(RB_DEV, TILE, E)
    proto_blocks = prototypes.reshape(PB_DEV, TILE, E)
    slot_rows = tile_row.reshape(MAXT)
    slot_protos = tile_proto.reshape(MAXT)
    live_slots = jnp.sum(tile_valid)
    score_scale = float(E) ** (-0.5)
    log_ratio = math.log(PB_DEV * proto_count / (RB_DEV * img_count))

    def fresh_scores(position):
        rows_here = lax.dynamic_index_in_dim(image_blocks, slot_rows[position], 0, keepdims=False)
        protos_here = lax.dynamic_index_in_dim(
            proto_blocks, slot_protos[position], 0, keepdims=False
        )
        products = lax.dot_general(
            rows_here, protos_here, (((1,), (1,)), ((), ())), preferred_element_type=jnp.float32
        )
        return products * score_scale

    def fill_cache(position, cache):
        return lax.dynamic_update_index_in_dim(cache, fresh_scores(position), position, 0)

    score_cache = lax.fori_loop(
        0, live_slots, fill_cache, jnp.zeros((MAXT, TILE, TILE), jnp.float32)
    )

    def scores_at(position):
        return lax.dynamic_index_in_dim(score_cache, position, 0, keepdims=False)

    col_pot = jnp.zeros((PB_DEV, TILE), jnp.float32)
    row_pot = jnp.zeros((RB_DEV, TILE), jnp.float32)
    for iteration in range(ITERS):

        def row_values_of(position):
            return scores_at(position) + lax.dynamic_index_in_dim(
                col_pot, slot_protos[position], 0, keepdims=True
            )

        row_local_top = running_top(row_values_of, live_slots, 1, slot_rows, RB_DEV)
        row_local_mass = running_mass(row_values_of, live_slots, 1, slot_rows, row_local_top)
        row_highest, row_summed = merge_tops(row_local_top, row_local_mass, "proto")
        row_pot = log_ratio - (row_highest + jnp.log(row_summed))

        def values_of(position):
            return (
                scores_at(position)
                + lax.dynamic_index_in_dim(row_pot, slot_rows[position], 0, keepdims=False)[:, None]
            )

        local_top = running_top(values_of, live_slots, 0, slot_protos, PB_DEV)
        local_mass = running_mass(values_of, live_slots, 0, slot_protos, local_top)
        highest, summed = merge_tops(local_top, local_mass, "img")
        col_pot = -(highest + jnp.log(summed))

    def tile_term(position):
        target = slot_protos[position]
        source = slot_rows[position]
        shifted = (
            scores_at(position)
            + lax.dynamic_index_in_dim(row_pot, source, 0, keepdims=False)[:, None]
        )
        weights = jnp.exp(
            shifted + lax.dynamic_index_in_dim(col_pot, target, 0, keepdims=True)
        ).astype(jnp.bfloat16)
        rows_here = lax.dynamic_index_in_dim(image_blocks, source, 0, keepdims=False)
        return lax.dot_general(
            weights, rows_here, (((0,), (0,)), ((), ())), preferred_element_type=jnp.float32
        )

    def add_tile(position, partial_value):
        target = slot_protos[position]
        current = lax.dynamic_index_in_dim(partial_value, target, 0, keepdims=False)
        return lax.dynamic_update_index_in_dim(
            partial_value, current + tile_term(position), target, 0
        )

    partial_value = lax.fori_loop(
        0, live_slots, add_tile, jnp.zeros((PB_DEV, TILE, E), jnp.float32)
    )
    proto_share = lax.psum_scatter(
        partial_value.reshape(PB_DEV * TILE, E).astype(jnp.bfloat16),
        "img",
        scatter_dimension=0,
        tiled=True,
    ).astype(jnp.float32)
    return (proto_share, col_pot.reshape(PB_DEV * TILE))


def solution(mesh):
    return jax.shard_map(
        shards,
        mesh=mesh,
        in_specs=(
            P("img", None),
            P("proto", None),
            P("img", "proto", None),
            P("img", "proto", None),
            P("img", "proto", None),
        ),
        out_specs=(P(("proto", "img"), None), P("proto")),
        check_vma=False,
    )
```

```python
import functools
import math

import jax
import jax.numpy as jnp
from jax import lax
from jax.experimental import pallas as pl
from jax.experimental.pallas import tpu as pltpu
from jax.sharding import PartitionSpec as P

E = 256
TILE = 512
RB_DEV = 4
PB_DEV = 8
MAXT = 6
ITERS = 3


far_below = -1e30


def running_top(values_of, live_slots, reduced, slot_blocks, block_count):

    def advance(position, tops):
        local_top = jnp.max(values_of(position), axis=reduced)
        target = slot_blocks[position]
        old_top = lax.dynamic_index_in_dim(tops, target, 0, keepdims=False)
        return lax.dynamic_update_index_in_dim(tops, jnp.maximum(old_top, local_top), target, 0)

    return lax.fori_loop(
        0, live_slots, advance, jnp.full((block_count, TILE), far_below, jnp.float32)
    )


def running_mass(values_of, live_slots, reduced, slot_blocks, tops):

    def advance(position, masses):
        target = slot_blocks[position]
        top_here = lax.dynamic_index_in_dim(tops, target, 0, keepdims=False)
        local_mass = jnp.sum(
            jnp.exp(values_of(position) - jnp.expand_dims(top_here, reduced)), axis=reduced
        )
        old_mass = lax.dynamic_index_in_dim(masses, target, 0, keepdims=False)
        return lax.dynamic_update_index_in_dim(masses, old_mass + local_mass, target, 0)

    return lax.fori_loop(0, live_slots, advance, jnp.zeros_like(tops))


def gather_kernel(axis, x_ref, out_ref, landed, send_sems, recv_sems):
    count = lax.axis_size(axis)
    me = lax.axis_index(axis)

    def peer_copy(peer, slot):
        return pltpu.make_async_remote_copy(
            src_ref=x_ref,
            dst_ref=landed.at[slot],
            send_sem=send_sems.at[slot],
            recv_sem=recv_sems.at[slot],
            device_id={axis: peer},
            device_id_type=pl.DeviceIdType.MESH,
        )

    landed[me] = x_ref[...]

    def send(step, carry):
        peer = lax.rem(me + step, count)
        peer_copy(peer, me).start()
        return carry

    lax.fori_loop(1, count, send, 0)

    def receive(step, carry):
        peer = lax.rem(me + count - step, count)
        peer_copy(peer, peer).wait_recv()
        return carry

    lax.fori_loop(1, count, receive, 0)

    def drain(step, carry):
        peer = lax.rem(me + step, count)
        peer_copy(peer, me).wait_send()
        return carry

    lax.fori_loop(1, count, drain, 0)
    out_ref[...] = landed[...]


def gather_peers(block, axis):
    count = lax.axis_size(axis)
    shape = (count,) + block.shape
    return pl.pallas_call(
        functools.partial(gather_kernel, axis),
        out_shape=jax.ShapeDtypeStruct(shape, block.dtype),
        in_specs=[pl.BlockSpec(memory_space=pltpu.VMEM)],
        out_specs=pl.BlockSpec(memory_space=pltpu.VMEM),
        scratch_shapes=[
            pltpu.VMEM(shape, block.dtype),
            pltpu.SemaphoreType.DMA((count,)),
            pltpu.SemaphoreType.DMA((count,)),
        ],
        compiler_params=pltpu.CompilerParams(has_side_effects=True),
    )(block)


def merge_tops(local_top, local_mass, axis):
    gathered = gather_peers(jnp.stack([local_top, local_mass]), axis)
    tops, masses = gathered[:, 0], gathered[:, 1]
    highest = jnp.max(tops, axis=0)
    summed = jnp.sum(masses * jnp.exp(tops - highest[None]), axis=0)
    return highest, summed


def shards(images, prototypes, tile_row, tile_proto, tile_valid):
    img_count = lax.axis_size("img")
    proto_count = lax.axis_size("proto")
    image_blocks = images.reshape(RB_DEV, TILE, E)
    proto_blocks = prototypes.reshape(PB_DEV, TILE, E)
    slot_rows = tile_row.reshape(MAXT)
    slot_protos = tile_proto.reshape(MAXT)
    live_slots = jnp.sum(tile_valid)
    score_scale = float(E) ** (-0.5)
    log_ratio = math.log(PB_DEV * proto_count / (RB_DEV * img_count))

    def fresh_scores(position):
        rows_here = lax.dynamic_index_in_dim(image_blocks, slot_rows[position], 0, keepdims=False)
        protos_here = lax.dynamic_index_in_dim(
            proto_blocks, slot_protos[position], 0, keepdims=False
        )
        products = lax.dot_general(
            rows_here, protos_here, (((1,), (1,)), ((), ())), preferred_element_type=jnp.float32
        )
        return products * score_scale

    def fill_cache(position, cache):
        return lax.dynamic_update_index_in_dim(cache, fresh_scores(position), position, 0)

    score_cache = lax.fori_loop(
        0, live_slots, fill_cache, jnp.zeros((MAXT, TILE, TILE), jnp.float32)
    )

    def scores_at(position):
        return lax.dynamic_index_in_dim(score_cache, position, 0, keepdims=False)

    col_pot = jnp.zeros((PB_DEV, TILE), jnp.float32)
    row_pot = jnp.zeros((RB_DEV, TILE), jnp.float32)
    for iteration in range(ITERS):

        def row_values_of(position):
            return scores_at(position) + lax.dynamic_index_in_dim(
                col_pot, slot_protos[position], 0, keepdims=True
            )

        row_local_top = running_top(row_values_of, live_slots, 1, slot_rows, RB_DEV)
        row_local_mass = running_mass(row_values_of, live_slots, 1, slot_rows, row_local_top)
        row_highest, row_summed = merge_tops(row_local_top, row_local_mass, "proto")
        row_pot = log_ratio - (row_highest + jnp.log(row_summed))

        def values_of(position):
            return (
                scores_at(position)
                + lax.dynamic_index_in_dim(row_pot, slot_rows[position], 0, keepdims=False)[:, None]
            )

        local_top = running_top(values_of, live_slots, 0, slot_protos, PB_DEV)
        local_mass = running_mass(values_of, live_slots, 0, slot_protos, local_top)
        highest, summed = merge_tops(local_top, local_mass, "img")
        col_pot = -(highest + jnp.log(summed))

    def tile_term(position):
        target = slot_protos[position]
        source = slot_rows[position]
        shifted = (
            scores_at(position)
            + lax.dynamic_index_in_dim(row_pot, source, 0, keepdims=False)[:, None]
        )
        weights = jnp.exp(
            shifted + lax.dynamic_index_in_dim(col_pot, target, 0, keepdims=True)
        ).astype(jnp.bfloat16)
        rows_here = lax.dynamic_index_in_dim(image_blocks, source, 0, keepdims=False)
        return lax.dot_general(
            weights, rows_here, (((0,), (0,)), ((), ())), preferred_element_type=jnp.float32
        )

    def add_tile(position, partial_value):
        target = slot_protos[position]
        current = lax.dynamic_index_in_dim(partial_value, target, 0, keepdims=False)
        return lax.dynamic_update_index_in_dim(
            partial_value, current + tile_term(position), target, 0
        )

    partial_value = lax.fori_loop(
        0, live_slots, add_tile, jnp.zeros((PB_DEV, TILE, E), jnp.float32)
    )
    proto_share = lax.psum_scatter(
        partial_value.reshape(PB_DEV * TILE, E).astype(jnp.bfloat16),
        "img",
        scatter_dimension=0,
        tiled=True,
    ).astype(jnp.float32)
    return (proto_share, col_pot.reshape(PB_DEV * TILE))


def solution(mesh):
    return jax.shard_map(
        shards,
        mesh=mesh,
        in_specs=(
            P("img", None),
            P("proto", None),
            P("img", "proto", None),
            P("img", "proto", None),
            P("img", "proto", None),
        ),
        out_specs=(P(("proto", "img"), None), P("proto")),
        check_vma=False,
    )
```

```python
import functools
import math

import jax
import jax.numpy as jnp
from jax import lax
from jax.experimental import pallas as pl
from jax.experimental.pallas import tpu as pltpu
from jax.sharding import PartitionSpec as P

E = 256
TILE = 512
RB_DEV = 4
PB_DEV = 8
MAXT = 6
ITERS = 3


far_below = -1e30


def running_top(values_of, live_slots, reduced, slot_blocks, block_count):

    def advance(position, tops):
        local_top = jnp.max(values_of(position), axis=reduced)
        target = slot_blocks[position]
        old_top = lax.dynamic_index_in_dim(tops, target, 0, keepdims=False)
        return lax.dynamic_update_index_in_dim(tops, jnp.maximum(old_top, local_top), target, 0)

    return lax.fori_loop(
        0, live_slots, advance, jnp.full((block_count, TILE), far_below, jnp.float32)
    )


def running_mass(values_of, live_slots, reduced, slot_blocks, tops):

    def advance(position, masses):
        target = slot_blocks[position]
        top_here = lax.dynamic_index_in_dim(tops, target, 0, keepdims=False)
        local_mass = jnp.sum(
            jnp.exp(values_of(position) - jnp.expand_dims(top_here, reduced)), axis=reduced
        )
        old_mass = lax.dynamic_index_in_dim(masses, target, 0, keepdims=False)
        return lax.dynamic_update_index_in_dim(masses, old_mass + local_mass, target, 0)

    return lax.fori_loop(0, live_slots, advance, jnp.zeros_like(tops))


def gather_kernel(axis, x_ref, out_ref, landed, send_sems, recv_sems):
    count = lax.axis_size(axis)
    me = lax.axis_index(axis)

    def peer_copy(peer, slot):
        return pltpu.make_async_remote_copy(
            src_ref=x_ref,
            dst_ref=landed.at[slot],
            send_sem=send_sems.at[slot],
            recv_sem=recv_sems.at[slot],
            device_id={axis: peer},
            device_id_type=pl.DeviceIdType.MESH,
        )

    landed[me] = x_ref[...]

    def send(step, carry):
        peer = lax.rem(me + step, count)
        peer_copy(peer, me).start()
        return carry

    lax.fori_loop(1, count, send, 0)

    def receive(step, carry):
        peer = lax.rem(me + count - step, count)
        peer_copy(peer, peer).wait_recv()
        return carry

    lax.fori_loop(1, count, receive, 0)

    def drain(step, carry):
        peer = lax.rem(me + step, count)
        peer_copy(peer, me).wait_send()
        return carry

    lax.fori_loop(1, count, drain, 0)
    out_ref[...] = landed[...]


def gather_peers(block, axis):
    count = lax.axis_size(axis)
    shape = (count,) + block.shape
    return pl.pallas_call(
        functools.partial(gather_kernel, axis),
        out_shape=jax.ShapeDtypeStruct(shape, block.dtype),
        in_specs=[pl.BlockSpec(memory_space=pltpu.VMEM)],
        out_specs=pl.BlockSpec(memory_space=pltpu.VMEM),
        scratch_shapes=[
            pltpu.VMEM(shape, block.dtype),
            pltpu.SemaphoreType.DMA((count,)),
            pltpu.SemaphoreType.DMA((count,)),
        ],
        compiler_params=pltpu.CompilerParams(has_side_effects=True),
    )(block)


def merge_tops(local_top, local_mass, axis):
    gathered = gather_peers(jnp.stack([local_top, local_mass]), axis)
    tops, masses = gathered[:, 0], gathered[:, 1]
    highest = jnp.max(tops, axis=0)
    summed = jnp.sum(masses * jnp.exp(tops - highest[None]), axis=0)
    return highest, summed


def slot_specs():
    return [pl.BlockSpec(memory_space=pltpu.SMEM)] * 3


def whole_specs(count):
    return [pl.BlockSpec(memory_space=pltpu.VMEM)] * count


def pass_kernel(along_rows, rows_ref, protos_ref, valid_ref, images_ref, prototypes_ref,
                other_ref, top_ref, mass_ref):
    top_ref[...] = jnp.full(top_ref.shape, far_below, jnp.float32)
    mass_ref[...] = jnp.zeros(mass_ref.shape, jnp.float32)
    score_scale = float(E) ** (-0.5)
    for position in range(MAXT):

        @pl.when(valid_ref[position] == 1)
        def _():
            row_block = rows_ref[position]
            proto_block = protos_ref[position]
            rows_here = images_ref[pl.ds(pl.multiple_of(row_block * TILE, TILE), TILE), :]
            protos_here = prototypes_ref[pl.ds(pl.multiple_of(proto_block * TILE, TILE), TILE), :]
            if along_rows:
                first, second, other_block, target = protos_here, rows_here, proto_block, row_block
            else:
                first, second, other_block, target = rows_here, protos_here, row_block, proto_block
            products = lax.dot_general(
                first, second, (((1,), (1,)), ((), ())), preferred_element_type=jnp.float32
            )
            values = products * score_scale + other_ref[other_block]
            local_top = jnp.max(values, axis=0, keepdims=True)
            old_top = top_ref[target]
            new_top = jnp.maximum(old_top, local_top)
            local_mass = jnp.sum(jnp.exp(values - new_top), axis=0, keepdims=True)
            mass_ref[target] = mass_ref[target] * jnp.exp(old_top - new_top) + local_mass
            top_ref[target] = new_top


def local_pass(along_rows, slots, images, prototypes, other_column):
    blocks = RB_DEV if along_rows else PB_DEV
    shape = jax.ShapeDtypeStruct((blocks, 1, TILE), jnp.float32)
    return pl.pallas_call(
        functools.partial(pass_kernel, along_rows),
        out_shape=(shape, shape),
        in_specs=slot_specs() + whole_specs(3),
        out_specs=tuple(whole_specs(2)),
    )(*slots, images, prototypes, other_column)


def final_kernel(rows_ref, protos_ref, valid_ref, images_ref, prototypes_ref,
                 col_ref, row_ref, out_ref):
    out_ref[...] = jnp.zeros(out_ref.shape, jnp.float32)
    score_scale = float(E) ** (-0.5)
    for position in range(MAXT):

        @pl.when(valid_ref[position] == 1)
        def _():
            row_block = rows_ref[position]
            proto_block = protos_ref[position]
            rows_here = images_ref[pl.ds(pl.multiple_of(row_block * TILE, TILE), TILE), :]
            protos_here = prototypes_ref[pl.ds(pl.multiple_of(proto_block * TILE, TILE), TILE), :]
            products = lax.dot_general(
                protos_here, rows_here, (((1,), (1,)), ((), ())), preferred_element_type=jnp.float32
            )
            weights = jnp.exp(
                products * score_scale + col_ref[proto_block] + row_ref[row_block]
            ).astype(jnp.bfloat16)
            out_ref[proto_block] += jnp.dot(weights, rows_here, preferred_element_type=jnp.float32)


def final_pass(slots, images, prototypes, col_column, row_pot):
    return pl.pallas_call(
        final_kernel,
        out_shape=jax.ShapeDtypeStruct((PB_DEV, TILE, E), jnp.float32),
        in_specs=slot_specs() + whole_specs(4),
        out_specs=pl.BlockSpec(memory_space=pltpu.VMEM),
    )(*slots, images, prototypes, col_column, row_pot.reshape(RB_DEV, 1, TILE))


def shards(images, prototypes, tile_row, tile_proto, tile_valid):
    img_count = lax.axis_size("img")
    proto_count = lax.axis_size("proto")
    slots = (tile_row.reshape(MAXT), tile_proto.reshape(MAXT), tile_valid.reshape(MAXT))
    log_ratio = math.log(PB_DEV * proto_count / (RB_DEV * img_count))

    col_pot = jnp.zeros((PB_DEV, TILE), jnp.float32)
    row_pot = jnp.zeros((RB_DEV, TILE), jnp.float32)
    for iteration in range(ITERS):
        row_local_top, row_local_mass = local_pass(
            True, slots, images, prototypes, col_pot.reshape(PB_DEV, TILE, 1)
        )
        row_highest, row_summed = merge_tops(
            row_local_top.reshape(RB_DEV, TILE), row_local_mass.reshape(RB_DEV, TILE), "proto"
        )
        row_pot = log_ratio - (row_highest + jnp.log(row_summed))
        local_top, local_mass = local_pass(
            False, slots, images, prototypes, row_pot.reshape(RB_DEV, TILE, 1)
        )
        highest, summed = merge_tops(
            local_top.reshape(PB_DEV, TILE), local_mass.reshape(PB_DEV, TILE), "img"
        )
        col_pot = -(highest + jnp.log(summed))

    partial_value = final_pass(
        slots, images, prototypes, col_pot.reshape(PB_DEV, TILE, 1), row_pot
    )
    proto_share = lax.psum_scatter(
        partial_value.reshape(PB_DEV * TILE, E).astype(jnp.bfloat16),
        "img",
        scatter_dimension=0,
        tiled=True,
    ).astype(jnp.float32)
    return (proto_share, col_pot.reshape(PB_DEV * TILE))


def solution(mesh):
    return jax.shard_map(
        shards,
        mesh=mesh,
        in_specs=(
            P("img", None),
            P("proto", None),
            P("img", "proto", None),
            P("img", "proto", None),
            P("img", "proto", None),
        ),
        out_specs=(P(("proto", "img"), None), P("proto")),
        check_vma=False,
    )
```

```python
import functools
import math

import jax
import jax.numpy as jnp
from jax import lax
from jax.experimental import pallas as pl
from jax.experimental.pallas import tpu as pltpu
from jax.sharding import PartitionSpec as P

E = 256
TILE = 512
RB_DEV = 4
PB_DEV = 8
MAXT = 6
ITERS = 3


far_below = -1e30


def running_top(values_of, live_slots, reduced, slot_blocks, block_count):

    def advance(position, tops):
        local_top = jnp.max(values_of(position), axis=reduced)
        target = slot_blocks[position]
        old_top = lax.dynamic_index_in_dim(tops, target, 0, keepdims=False)
        return lax.dynamic_update_index_in_dim(tops, jnp.maximum(old_top, local_top), target, 0)

    return lax.fori_loop(
        0, live_slots, advance, jnp.full((block_count, TILE), far_below, jnp.float32)
    )


def running_mass(values_of, live_slots, reduced, slot_blocks, tops):

    def advance(position, masses):
        target = slot_blocks[position]
        top_here = lax.dynamic_index_in_dim(tops, target, 0, keepdims=False)
        local_mass = jnp.sum(
            jnp.exp(values_of(position) - jnp.expand_dims(top_here, reduced)), axis=reduced
        )
        old_mass = lax.dynamic_index_in_dim(masses, target, 0, keepdims=False)
        return lax.dynamic_update_index_in_dim(masses, old_mass + local_mass, target, 0)

    return lax.fori_loop(0, live_slots, advance, jnp.zeros_like(tops))


def gather_kernel(axis, x_ref, out_ref, landed, send_sems, recv_sems):
    count = lax.axis_size(axis)
    me = lax.axis_index(axis)

    def peer_copy(peer, slot):
        return pltpu.make_async_remote_copy(
            src_ref=x_ref,
            dst_ref=landed.at[slot],
            send_sem=send_sems.at[slot],
            recv_sem=recv_sems.at[slot],
            device_id={axis: peer},
            device_id_type=pl.DeviceIdType.MESH,
        )

    landed[me] = x_ref[...]

    def send(step, carry):
        peer = lax.rem(me + step, count)
        peer_copy(peer, me).start()
        return carry

    lax.fori_loop(1, count, send, 0)

    def receive(step, carry):
        peer = lax.rem(me + count - step, count)
        peer_copy(peer, peer).wait_recv()
        return carry

    lax.fori_loop(1, count, receive, 0)

    def drain(step, carry):
        peer = lax.rem(me + step, count)
        peer_copy(peer, me).wait_send()
        return carry

    lax.fori_loop(1, count, drain, 0)
    out_ref[...] = landed[...]


def gather_peers(block, axis):
    count = lax.axis_size(axis)
    shape = (count,) + block.shape
    return pl.pallas_call(
        functools.partial(gather_kernel, axis),
        out_shape=jax.ShapeDtypeStruct(shape, block.dtype),
        in_specs=[pl.BlockSpec(memory_space=pltpu.VMEM)],
        out_specs=pl.BlockSpec(memory_space=pltpu.VMEM),
        scratch_shapes=[
            pltpu.VMEM(shape, block.dtype),
            pltpu.SemaphoreType.DMA((count,)),
            pltpu.SemaphoreType.DMA((count,)),
        ],
        compiler_params=pltpu.CompilerParams(has_side_effects=True),
    )(block)


def merge_tops(local_top, local_mass, axis):
    gathered = gather_peers(jnp.stack([local_top, local_mass]), axis)
    tops, masses = gathered[:, 0], gathered[:, 1]
    highest = jnp.max(tops, axis=0)
    summed = jnp.sum(masses * jnp.exp(tops - highest[None]), axis=0)
    return highest, summed


def slot_specs():
    return [pl.BlockSpec(memory_space=pltpu.SMEM)] * 3


def whole_specs(count):
    return [pl.BlockSpec(memory_space=pltpu.VMEM)] * count


def pass_kernel(along_rows, rows_ref, protos_ref, valid_ref, images_ref, prototypes_ref,
                other_ref, top_ref, mass_ref):
    top_ref[...] = jnp.full(top_ref.shape, far_below, jnp.float32)
    mass_ref[...] = jnp.zeros(mass_ref.shape, jnp.float32)
    score_scale = float(E) ** (-0.5)
    for position in range(MAXT):

        @pl.when(valid_ref[position] == 1)
        def _():
            row_block = rows_ref[position]
            proto_block = protos_ref[position]
            rows_here = images_ref[pl.ds(pl.multiple_of(row_block * TILE, TILE), TILE), :]
            protos_here = prototypes_ref[pl.ds(pl.multiple_of(proto_block * TILE, TILE), TILE), :]
            if along_rows:
                first, second, other_block, target = protos_here, rows_here, proto_block, row_block
            else:
                first, second, other_block, target = rows_here, protos_here, row_block, proto_block
            products = lax.dot_general(
                first, second, (((1,), (1,)), ((), ())), preferred_element_type=jnp.float32
            )
            values = products * score_scale + other_ref[other_block]
            local_top = jnp.max(values, axis=0, keepdims=True)
            old_top = top_ref[target]
            new_top = jnp.maximum(old_top, local_top)
            local_mass = jnp.sum(jnp.exp(values - new_top), axis=0, keepdims=True)
            mass_ref[target] = mass_ref[target] * jnp.exp(old_top - new_top) + local_mass
            top_ref[target] = new_top


def local_pass(along_rows, slots, images, prototypes, other_column):
    blocks = RB_DEV if along_rows else PB_DEV
    shape = jax.ShapeDtypeStruct((blocks, 1, TILE), jnp.float32)
    return pl.pallas_call(
        functools.partial(pass_kernel, along_rows),
        out_shape=(shape, shape),
        in_specs=slot_specs() + whole_specs(3),
        out_specs=tuple(whole_specs(2)),
    )(*slots, images, prototypes, other_column)


def final_kernel(rows_ref, protos_ref, valid_ref, images_ref, prototypes_ref,
                 col_ref, row_ref, out_ref):
    out_ref[...] = jnp.zeros(out_ref.shape, jnp.float32)
    score_scale = float(E) ** (-0.5)
    for position in range(MAXT):

        @pl.when(valid_ref[position] == 1)
        def _():
            row_block = rows_ref[position]
            proto_block = protos_ref[position]
            rows_here = images_ref[pl.ds(pl.multiple_of(row_block * TILE, TILE), TILE), :]
            protos_here = prototypes_ref[pl.ds(pl.multiple_of(proto_block * TILE, TILE), TILE), :]
            products = lax.dot_general(
                protos_here, rows_here, (((1,), (1,)), ((), ())), preferred_element_type=jnp.float32
            )
            weights = jnp.exp(
                products * score_scale + col_ref[proto_block] + row_ref[row_block]
            ).astype(jnp.bfloat16)
            out_ref[proto_block] += jnp.dot(weights, rows_here, preferred_element_type=jnp.float32)


def final_pass(slots, images, prototypes, col_column, row_pot):
    return pl.pallas_call(
        final_kernel,
        out_shape=jax.ShapeDtypeStruct((PB_DEV, TILE, E), jnp.float32),
        in_specs=slot_specs() + whole_specs(4),
        out_specs=pl.BlockSpec(memory_space=pltpu.VMEM),
    )(*slots, images, prototypes, col_column, row_pot.reshape(RB_DEV, 1, TILE))


def to_column(lanes):
    padded = jnp.concatenate(
        [lanes, jnp.zeros((8 - lanes.shape[0], TILE), jnp.float32)], axis=0
    ) if lanes.shape[0] < 8 else lanes
    return jnp.transpose(padded)


def exchange(axis, count, stage, local, packed, landed, send_sems, recv_sems):
    me = lax.axis_index(axis)
    packed[...] = local
    landed[stage, me] = local

    def peer_copy(peer, slot):
        return pltpu.make_async_remote_copy(
            src_ref=packed,
            dst_ref=landed.at[stage, slot],
            send_sem=send_sems.at[stage, peer],
            recv_sem=recv_sems.at[stage, slot],
            device_id={axis: peer},
            device_id_type=pl.DeviceIdType.MESH,
        )

    def send(step, carry):
        peer = lax.rem(me + step, count)
        peer_copy(peer, me).start()
        return carry

    lax.fori_loop(1, count, send, 0)

    def receive(step, carry):
        peer = lax.rem(me + count - step, count)
        peer_copy(peer, peer).wait_recv()
        return carry

    lax.fori_loop(1, count, receive, 0)

    def drain(step, carry):
        peer = lax.rem(me + step, count)
        peer_copy(peer, me).wait_send()
        return carry

    lax.fori_loop(1, count, drain, 0)
    gathered = landed[stage]
    tops, masses = gathered[:, 0], gathered[:, 1]
    highest = jnp.max(tops, axis=0)
    summed = jnp.sum(masses * jnp.exp(tops - highest[None]), axis=0)
    return highest, summed


def pick_column(columns, chosen_block, blocks):
    picked = columns[:, 0:1]
    for block in range(1, blocks):
        picked = jnp.where(chosen_block == block, columns[:, block:block + 1], picked)
    return picked


def local_merge(along_rows, rows_ref, protos_ref, valid_ref, slot_images_ref, slot_protos_ref,
                other_columns):
    blocks = RB_DEV if along_rows else PB_DEV
    other_blocks = PB_DEV if along_rows else RB_DEV
    tops = [jnp.full((1, TILE), far_below, jnp.float32) for _ in range(blocks)]
    masses = [jnp.zeros((1, TILE), jnp.float32) for _ in range(blocks)]
    score_scale = float(E) ** (-0.5)
    for position in range(MAXT):
        row_block = rows_ref[position]
        proto_block = protos_ref[position]
        live = valid_ref[position] == 1
        rows_here = slot_images_ref[position]
        protos_here = slot_protos_ref[position]
        if along_rows:
            first, second, other_block, target = protos_here, rows_here, proto_block, row_block
        else:
            first, second, other_block, target = rows_here, protos_here, row_block, proto_block
        products = lax.dot_general(
            first, second, (((1,), (1,)), ((), ())), preferred_element_type=jnp.float32
        )
        values = products * score_scale + pick_column(other_columns, other_block, other_blocks)
        local_top = jnp.max(values, axis=0, keepdims=True)
        local_mass = jnp.sum(jnp.exp(values - local_top), axis=0, keepdims=True)
        for block in range(blocks):
            chosen = jnp.logical_and(live, target == block)
            new_top = jnp.maximum(tops[block], local_top)
            new_mass = masses[block] * jnp.exp(tops[block] - new_top) + local_mass * jnp.exp(
                local_top - new_top
            )
            tops[block] = jnp.where(chosen, new_top, tops[block])
            masses[block] = jnp.where(chosen, new_mass, masses[block])
    return jnp.stack([jnp.concatenate(tops, axis=0), jnp.concatenate(masses, axis=0)])


def sinkhorn_kernel(log_ratio, rows_ref, protos_ref, valid_ref, images_ref, prototypes_ref,
                    row_out, col_out, col_columns_out,
                    row_packed, col_packed, row_landed, col_landed,
                    row_send, row_recv, col_send, col_recv):
    proto_count = lax.axis_size("proto")
    img_count = lax.axis_size("img")
    proto_me = lax.axis_index("proto")
    img_me = lax.axis_index("img")
    barrier = pltpu.get_barrier_semaphore()

    def greet_proto(step, carry):
        peer = lax.rem(proto_me + step, proto_count)
        pl.semaphore_signal(barrier, inc=1, device_id={"proto": peer},
                            device_id_type=pl.DeviceIdType.MESH)
        return carry

    def greet_img(step, carry):
        peer = lax.rem(img_me + step, img_count)
        pl.semaphore_signal(barrier, inc=1, device_id={"img": peer},
                            device_id_type=pl.DeviceIdType.MESH)
        return carry

    lax.fori_loop(1, proto_count, greet_proto, 0)
    lax.fori_loop(1, img_count, greet_img, 0)
    pl.semaphore_wait(barrier, proto_count + img_count - 2)

    col_t = jnp.zeros((TILE, PB_DEV), jnp.float32)
    for iteration in range(ITERS):
        local = local_merge(True, rows_ref, protos_ref, valid_ref, images_ref, prototypes_ref,
                            col_t)
        highest, summed = exchange("proto", proto_count, iteration, local, row_packed,
                                   row_landed, row_send, row_recv)
        row_pot = log_ratio - (highest + jnp.log(summed))
        row_t = to_column(row_pot)
        local = local_merge(False, rows_ref, protos_ref, valid_ref, images_ref, prototypes_ref,
                            row_t)
        highest, summed = exchange("img", img_count, iteration, local, col_packed,
                                   col_landed, col_send, col_recv)
        col_pot = -(highest + jnp.log(summed))
        col_t = to_column(col_pot)
    row_out[...] = row_pot
    col_out[...] = col_pot
    for block in range(PB_DEV):
        col_columns_out[block] = col_t[:, block:block + 1]


def sinkhorn(slots, slot_images, slot_protos, log_ratio):
    proto_count = lax.axis_size("proto")
    img_count = lax.axis_size("img")
    vmem = pltpu.VMEM
    return pl.pallas_call(
        functools.partial(sinkhorn_kernel, log_ratio),
        out_shape=(
            jax.ShapeDtypeStruct((RB_DEV, TILE), jnp.float32),
            jax.ShapeDtypeStruct((PB_DEV, TILE), jnp.float32),
            jax.ShapeDtypeStruct((PB_DEV, TILE, 1), jnp.float32),
        ),
        in_specs=slot_specs() + whole_specs(2),
        out_specs=tuple(whole_specs(3)),
        scratch_shapes=[
            vmem((2, RB_DEV, TILE), jnp.float32),
            vmem((2, PB_DEV, TILE), jnp.float32),
            vmem((ITERS, proto_count, 2, RB_DEV, TILE), jnp.float32),
            vmem((ITERS, img_count, 2, PB_DEV, TILE), jnp.float32),
            pltpu.SemaphoreType.DMA((ITERS, proto_count)),
            pltpu.SemaphoreType.DMA((ITERS, proto_count)),
            pltpu.SemaphoreType.DMA((ITERS, img_count)),
            pltpu.SemaphoreType.DMA((ITERS, img_count)),
        ],
        compiler_params=pltpu.CompilerParams(collective_id=0, has_side_effects=True),
    )(*slots, slot_images, slot_protos)


def shards(images, prototypes, tile_row, tile_proto, tile_valid):
    img_count = lax.axis_size("img")
    proto_count = lax.axis_size("proto")
    slots = (tile_row.reshape(MAXT), tile_proto.reshape(MAXT), tile_valid.reshape(MAXT))
    log_ratio = math.log(PB_DEV * proto_count / (RB_DEV * img_count))
    slot_images = images.reshape(RB_DEV, TILE, E)[slots[0]]
    slot_protos = prototypes.reshape(PB_DEV, TILE, E)[slots[1]]
    row_pot, col_pot, col_columns = sinkhorn(slots, slot_images, slot_protos, log_ratio)
    partial_value = final_pass(slots, images, prototypes, col_columns, row_pot)
    proto_share = lax.psum_scatter(
        partial_value.reshape(PB_DEV * TILE, E).astype(jnp.bfloat16),
        "img",
        scatter_dimension=0,
        tiled=True,
    ).astype(jnp.float32)
    return (proto_share, col_pot.reshape(PB_DEV * TILE))


def solution(mesh):
    return jax.shard_map(
        shards,
        mesh=mesh,
        in_specs=(
            P("img", None),
            P("proto", None),
            P("img", "proto", None),
            P("img", "proto", None),
            P("img", "proto", None),
        ),
        out_specs=(P(("proto", "img"), None), P("proto")),
        check_vma=False,
    )
```

```python
import functools
import math

import jax
import jax.numpy as jnp
from jax import lax
from jax.experimental import pallas as pl
from jax.experimental.pallas import tpu as pltpu
from jax.sharding import PartitionSpec as P

E = 256
TILE = 512
RB_DEV = 4
PB_DEV = 8
MAXT = 6
ITERS = 3


far_below = -1e30


def running_top(values_of, live_slots, reduced, slot_blocks, block_count):

    def advance(position, tops):
        local_top = jnp.max(values_of(position), axis=reduced)
        target = slot_blocks[position]
        old_top = lax.dynamic_index_in_dim(tops, target, 0, keepdims=False)
        return lax.dynamic_update_index_in_dim(tops, jnp.maximum(old_top, local_top), target, 0)

    return lax.fori_loop(
        0, live_slots, advance, jnp.full((block_count, TILE), far_below, jnp.float32)
    )


def running_mass(values_of, live_slots, reduced, slot_blocks, tops):

    def advance(position, masses):
        target = slot_blocks[position]
        top_here = lax.dynamic_index_in_dim(tops, target, 0, keepdims=False)
        local_mass = jnp.sum(
            jnp.exp(values_of(position) - jnp.expand_dims(top_here, reduced)), axis=reduced
        )
        old_mass = lax.dynamic_index_in_dim(masses, target, 0, keepdims=False)
        return lax.dynamic_update_index_in_dim(masses, old_mass + local_mass, target, 0)

    return lax.fori_loop(0, live_slots, advance, jnp.zeros_like(tops))


def gather_kernel(axis, x_ref, out_ref, landed, send_sems, recv_sems):
    count = lax.axis_size(axis)
    me = lax.axis_index(axis)

    def peer_copy(peer, slot):
        return pltpu.make_async_remote_copy(
            src_ref=x_ref,
            dst_ref=landed.at[slot],
            send_sem=send_sems.at[slot],
            recv_sem=recv_sems.at[slot],
            device_id={axis: peer},
            device_id_type=pl.DeviceIdType.MESH,
        )

    landed[me] = x_ref[...]

    def send(step, carry):
        peer = lax.rem(me + step, count)
        peer_copy(peer, me).start()
        return carry

    lax.fori_loop(1, count, send, 0)

    def receive(step, carry):
        peer = lax.rem(me + count - step, count)
        peer_copy(peer, peer).wait_recv()
        return carry

    lax.fori_loop(1, count, receive, 0)

    def drain(step, carry):
        peer = lax.rem(me + step, count)
        peer_copy(peer, me).wait_send()
        return carry

    lax.fori_loop(1, count, drain, 0)
    out_ref[...] = landed[...]


def gather_peers(block, axis):
    count = lax.axis_size(axis)
    shape = (count,) + block.shape
    return pl.pallas_call(
        functools.partial(gather_kernel, axis),
        out_shape=jax.ShapeDtypeStruct(shape, block.dtype),
        in_specs=[pl.BlockSpec(memory_space=pltpu.VMEM)],
        out_specs=pl.BlockSpec(memory_space=pltpu.VMEM),
        scratch_shapes=[
            pltpu.VMEM(shape, block.dtype),
            pltpu.SemaphoreType.DMA((count,)),
            pltpu.SemaphoreType.DMA((count,)),
        ],
        compiler_params=pltpu.CompilerParams(has_side_effects=True),
    )(block)


def merge_tops(local_top, local_mass, axis):
    gathered = gather_peers(jnp.stack([local_top, local_mass]), axis)
    tops, masses = gathered[:, 0], gathered[:, 1]
    highest = jnp.max(tops, axis=0)
    summed = jnp.sum(masses * jnp.exp(tops - highest[None]), axis=0)
    return highest, summed


def slot_specs():
    return [pl.BlockSpec(memory_space=pltpu.SMEM)] * 3


def whole_specs(count):
    return [pl.BlockSpec(memory_space=pltpu.VMEM)] * count


def pass_kernel(along_rows, rows_ref, protos_ref, valid_ref, images_ref, prototypes_ref,
                other_ref, top_ref, mass_ref):
    top_ref[...] = jnp.full(top_ref.shape, far_below, jnp.float32)
    mass_ref[...] = jnp.zeros(mass_ref.shape, jnp.float32)
    score_scale = float(E) ** (-0.5)
    for position in range(MAXT):

        @pl.when(valid_ref[position] == 1)
        def _():
            row_block = rows_ref[position]
            proto_block = protos_ref[position]
            rows_here = images_ref[pl.ds(pl.multiple_of(row_block * TILE, TILE), TILE), :]
            protos_here = prototypes_ref[pl.ds(pl.multiple_of(proto_block * TILE, TILE), TILE), :]
            if along_rows:
                first, second, other_block, target = protos_here, rows_here, proto_block, row_block
            else:
                first, second, other_block, target = rows_here, protos_here, row_block, proto_block
            products = lax.dot_general(
                first, second, (((1,), (1,)), ((), ())), preferred_element_type=jnp.float32
            )
            values = products * score_scale + other_ref[other_block]
            local_top = jnp.max(values, axis=0, keepdims=True)
            old_top = top_ref[target]
            new_top = jnp.maximum(old_top, local_top)
            local_mass = jnp.sum(jnp.exp(values - new_top), axis=0, keepdims=True)
            mass_ref[target] = mass_ref[target] * jnp.exp(old_top - new_top) + local_mass
            top_ref[target] = new_top


def local_pass(along_rows, slots, images, prototypes, other_column):
    blocks = RB_DEV if along_rows else PB_DEV
    shape = jax.ShapeDtypeStruct((blocks, 1, TILE), jnp.float32)
    return pl.pallas_call(
        functools.partial(pass_kernel, along_rows),
        out_shape=(shape, shape),
        in_specs=slot_specs() + whole_specs(3),
        out_specs=tuple(whole_specs(2)),
    )(*slots, images, prototypes, other_column)


def final_kernel(rows_ref, protos_ref, valid_ref, images_ref, prototypes_ref,
                 col_ref, row_ref, out_ref):
    out_ref[...] = jnp.zeros(out_ref.shape, jnp.float32)
    score_scale = float(E) ** (-0.5)
    for position in range(MAXT):

        @pl.when(valid_ref[position] == 1)
        def _():
            row_block = rows_ref[position]
            proto_block = protos_ref[position]
            rows_here = images_ref[pl.ds(pl.multiple_of(row_block * TILE, TILE), TILE), :]
            protos_here = prototypes_ref[pl.ds(pl.multiple_of(proto_block * TILE, TILE), TILE), :]
            products = lax.dot_general(
                protos_here, rows_here, (((1,), (1,)), ((), ())), preferred_element_type=jnp.float32
            )
            weights = jnp.exp(
                products * score_scale + col_ref[proto_block] + row_ref[row_block]
            ).astype(jnp.bfloat16)
            out_ref[proto_block] += jnp.dot(weights, rows_here, preferred_element_type=jnp.float32)


def final_pass(slots, images, prototypes, col_column, row_pot):
    return pl.pallas_call(
        final_kernel,
        out_shape=jax.ShapeDtypeStruct((PB_DEV, TILE, E), jnp.float32),
        in_specs=slot_specs() + whole_specs(4),
        out_specs=pl.BlockSpec(memory_space=pltpu.VMEM),
    )(*slots, images, prototypes, col_column, row_pot.reshape(RB_DEV, 1, TILE))


def to_column(lanes):
    padded = jnp.concatenate(
        [lanes, jnp.zeros((8 - lanes.shape[0], TILE), jnp.float32)], axis=0
    ) if lanes.shape[0] < 8 else lanes
    return jnp.transpose(padded)


def exchange(axis, count, stage, local, packed, landed, send_sems, recv_sems):
    me = lax.axis_index(axis)
    packed[...] = local
    landed[stage, me] = local

    def peer_copy(peer, slot):
        return pltpu.make_async_remote_copy(
            src_ref=packed,
            dst_ref=landed.at[stage, slot],
            send_sem=send_sems.at[stage, peer],
            recv_sem=recv_sems.at[stage, slot],
            device_id={axis: peer},
            device_id_type=pl.DeviceIdType.MESH,
        )

    def send(step, carry):
        peer = lax.rem(me + step, count)
        peer_copy(peer, me).start()
        return carry

    lax.fori_loop(1, count, send, 0)

    def receive(step, carry):
        peer = lax.rem(me + count - step, count)
        peer_copy(peer, peer).wait_recv()
        return carry

    lax.fori_loop(1, count, receive, 0)

    def drain(step, carry):
        peer = lax.rem(me + step, count)
        peer_copy(peer, me).wait_send()
        return carry

    lax.fori_loop(1, count, drain, 0)
    gathered = landed[stage]
    highest = jnp.max(gathered, axis=0)
    summed = jnp.sum(jnp.exp(gathered - highest[None]), axis=0)
    return highest, summed


def pick_column(columns, chosen_block, blocks):
    picked = columns[:, 0:1]
    for block in range(1, blocks):
        picked = jnp.where(chosen_block == block, columns[:, block:block + 1], picked)
    return picked


def local_merge(along_rows, rows_ref, protos_ref, valid_ref, slot_images_ref, slot_protos_ref,
                other_columns):
    blocks = RB_DEV if along_rows else PB_DEV
    other_blocks = PB_DEV if along_rows else RB_DEV
    tops = [jnp.full((1, TILE), far_below, jnp.float32) for _ in range(blocks)]
    masses = [jnp.zeros((1, TILE), jnp.float32) for _ in range(blocks)]
    score_scale = float(E) ** (-0.5)
    for position in range(MAXT):
        row_block = rows_ref[position]
        proto_block = protos_ref[position]
        live = valid_ref[position] == 1
        rows_here = slot_images_ref[position]
        protos_here = slot_protos_ref[position]
        if along_rows:
            first, second, other_block, target = protos_here, rows_here, proto_block, row_block
        else:
            first, second, other_block, target = rows_here, protos_here, row_block, proto_block
        products = lax.dot_general(
            first, second, (((1,), (1,)), ((), ())), preferred_element_type=jnp.float32
        )
        values = products * score_scale + pick_column(other_columns, other_block, other_blocks)
        local_top = jnp.max(values, axis=0, keepdims=True)
        local_mass = jnp.sum(jnp.exp(values - local_top), axis=0, keepdims=True)
        for block in range(blocks):
            chosen = jnp.logical_and(live, target == block)
            new_top = jnp.maximum(tops[block], local_top)
            new_mass = masses[block] * jnp.exp(tops[block] - new_top) + local_mass * jnp.exp(
                local_top - new_top
            )
            tops[block] = jnp.where(chosen, new_top, tops[block])
            masses[block] = jnp.where(chosen, new_mass, masses[block])
    return jnp.concatenate(tops, axis=0) + jnp.log(jnp.concatenate(masses, axis=0))


def sinkhorn_kernel(log_ratio, rows_ref, protos_ref, valid_ref, images_ref, prototypes_ref,
                    row_out, col_out, col_columns_out,
                    row_packed, col_packed, row_landed, col_landed,
                    row_send, row_recv, col_send, col_recv):
    proto_count = lax.axis_size("proto")
    img_count = lax.axis_size("img")
    proto_me = lax.axis_index("proto")
    img_me = lax.axis_index("img")
    barrier = pltpu.get_barrier_semaphore()

    def greet_proto(step, carry):
        peer = lax.rem(proto_me + step, proto_count)
        pl.semaphore_signal(barrier, inc=1, device_id={"proto": peer},
                            device_id_type=pl.DeviceIdType.MESH)
        return carry

    def greet_img(step, carry):
        peer = lax.rem(img_me + step, img_count)
        pl.semaphore_signal(barrier, inc=1, device_id={"img": peer},
                            device_id_type=pl.DeviceIdType.MESH)
        return carry

    lax.fori_loop(1, proto_count, greet_proto, 0)
    lax.fori_loop(1, img_count, greet_img, 0)
    pl.semaphore_wait(barrier, proto_count + img_count - 2)

    col_t = jnp.zeros((TILE, PB_DEV), jnp.float32)
    for iteration in range(ITERS):
        local = local_merge(True, rows_ref, protos_ref, valid_ref, images_ref, prototypes_ref,
                            col_t)
        highest, summed = exchange("proto", proto_count, iteration, local, row_packed,
                                   row_landed, row_send, row_recv)
        row_pot = log_ratio - (highest + jnp.log(summed))
        row_t = to_column(row_pot)
        local = local_merge(False, rows_ref, protos_ref, valid_ref, images_ref, prototypes_ref,
                            row_t)
        highest, summed = exchange("img", img_count, iteration, local, col_packed,
                                   col_landed, col_send, col_recv)
        col_pot = -(highest + jnp.log(summed))
        col_t = to_column(col_pot)
    row_out[...] = row_pot
    col_out[...] = col_pot
    for block in range(PB_DEV):
        col_columns_out[block] = col_t[:, block:block + 1]


def sinkhorn(slots, slot_images, slot_protos, log_ratio):
    proto_count = lax.axis_size("proto")
    img_count = lax.axis_size("img")
    vmem = pltpu.VMEM
    return pl.pallas_call(
        functools.partial(sinkhorn_kernel, log_ratio),
        out_shape=(
            jax.ShapeDtypeStruct((RB_DEV, TILE), jnp.float32),
            jax.ShapeDtypeStruct((PB_DEV, TILE), jnp.float32),
            jax.ShapeDtypeStruct((PB_DEV, TILE, 1), jnp.float32),
        ),
        in_specs=slot_specs() + whole_specs(2),
        out_specs=tuple(whole_specs(3)),
        scratch_shapes=[
            vmem((RB_DEV, TILE), jnp.float32),
            vmem((PB_DEV, TILE), jnp.float32),
            vmem((ITERS, proto_count, RB_DEV, TILE), jnp.float32),
            vmem((ITERS, img_count, PB_DEV, TILE), jnp.float32),
            pltpu.SemaphoreType.DMA((ITERS, proto_count)),
            pltpu.SemaphoreType.DMA((ITERS, proto_count)),
            pltpu.SemaphoreType.DMA((ITERS, img_count)),
            pltpu.SemaphoreType.DMA((ITERS, img_count)),
        ],
        compiler_params=pltpu.CompilerParams(collective_id=0, has_side_effects=True),
    )(*slots, slot_images, slot_protos)


def shards(images, prototypes, tile_row, tile_proto, tile_valid):
    img_count = lax.axis_size("img")
    proto_count = lax.axis_size("proto")
    slots = (tile_row.reshape(MAXT), tile_proto.reshape(MAXT), tile_valid.reshape(MAXT))
    log_ratio = math.log(PB_DEV * proto_count / (RB_DEV * img_count))
    slot_images = images.reshape(RB_DEV, TILE, E)[slots[0]]
    slot_protos = prototypes.reshape(PB_DEV, TILE, E)[slots[1]]
    row_pot, col_pot, col_columns = sinkhorn(slots, slot_images, slot_protos, log_ratio)
    partial_value = final_pass(slots, images, prototypes, col_columns, row_pot)
    proto_share = lax.psum_scatter(
        partial_value.reshape(PB_DEV * TILE, E).astype(jnp.bfloat16),
        "img",
        scatter_dimension=0,
        tiled=True,
    ).astype(jnp.float32)
    return (proto_share, col_pot.reshape(PB_DEV * TILE))


def solution(mesh):
    return jax.shard_map(
        shards,
        mesh=mesh,
        in_specs=(
            P("img", None),
            P("proto", None),
            P("img", "proto", None),
            P("img", "proto", None),
            P("img", "proto", None),
        ),
        out_specs=(P(("proto", "img"), None), P("proto")),
        check_vma=False,
    )
```

```python
import functools
import math

import jax
import jax.numpy as jnp
from jax import lax
from jax.experimental import pallas as pl
from jax.experimental.pallas import tpu as pltpu
from jax.sharding import PartitionSpec as P

E = 256
TILE = 512
RB_DEV = 4
PB_DEV = 8
MAXT = 6
ITERS = 3


far_below = -1e30


def running_top(values_of, live_slots, reduced, slot_blocks, block_count):

    def advance(position, tops):
        local_top = jnp.max(values_of(position), axis=reduced)
        target = slot_blocks[position]
        old_top = lax.dynamic_index_in_dim(tops, target, 0, keepdims=False)
        return lax.dynamic_update_index_in_dim(tops, jnp.maximum(old_top, local_top), target, 0)

    return lax.fori_loop(
        0, live_slots, advance, jnp.full((block_count, TILE), far_below, jnp.float32)
    )


def running_mass(values_of, live_slots, reduced, slot_blocks, tops):

    def advance(position, masses):
        target = slot_blocks[position]
        top_here = lax.dynamic_index_in_dim(tops, target, 0, keepdims=False)
        local_mass = jnp.sum(
            jnp.exp(values_of(position) - jnp.expand_dims(top_here, reduced)), axis=reduced
        )
        old_mass = lax.dynamic_index_in_dim(masses, target, 0, keepdims=False)
        return lax.dynamic_update_index_in_dim(masses, old_mass + local_mass, target, 0)

    return lax.fori_loop(0, live_slots, advance, jnp.zeros_like(tops))


def gather_kernel(axis, x_ref, out_ref, landed, send_sems, recv_sems):
    count = lax.axis_size(axis)
    me = lax.axis_index(axis)

    def peer_copy(peer, slot):
        return pltpu.make_async_remote_copy(
            src_ref=x_ref,
            dst_ref=landed.at[slot],
            send_sem=send_sems.at[slot],
            recv_sem=recv_sems.at[slot],
            device_id={axis: peer},
            device_id_type=pl.DeviceIdType.MESH,
        )

    landed[me] = x_ref[...]

    def send(step, carry):
        peer = lax.rem(me + step, count)
        peer_copy(peer, me).start()
        return carry

    lax.fori_loop(1, count, send, 0)

    def receive(step, carry):
        peer = lax.rem(me + count - step, count)
        peer_copy(peer, peer).wait_recv()
        return carry

    lax.fori_loop(1, count, receive, 0)

    def drain(step, carry):
        peer = lax.rem(me + step, count)
        peer_copy(peer, me).wait_send()
        return carry

    lax.fori_loop(1, count, drain, 0)
    out_ref[...] = landed[...]


def gather_peers(block, axis):
    count = lax.axis_size(axis)
    shape = (count,) + block.shape
    return pl.pallas_call(
        functools.partial(gather_kernel, axis),
        out_shape=jax.ShapeDtypeStruct(shape, block.dtype),
        in_specs=[pl.BlockSpec(memory_space=pltpu.VMEM)],
        out_specs=pl.BlockSpec(memory_space=pltpu.VMEM),
        scratch_shapes=[
            pltpu.VMEM(shape, block.dtype),
            pltpu.SemaphoreType.DMA((count,)),
            pltpu.SemaphoreType.DMA((count,)),
        ],
        compiler_params=pltpu.CompilerParams(has_side_effects=True),
    )(block)


def merge_tops(local_top, local_mass, axis):
    gathered = gather_peers(jnp.stack([local_top, local_mass]), axis)
    tops, masses = gathered[:, 0], gathered[:, 1]
    highest = jnp.max(tops, axis=0)
    summed = jnp.sum(masses * jnp.exp(tops - highest[None]), axis=0)
    return highest, summed


def slot_specs():
    return [pl.BlockSpec(memory_space=pltpu.SMEM)] * 3


def whole_specs(count):
    return [pl.BlockSpec(memory_space=pltpu.VMEM)] * count


def pass_kernel(along_rows, rows_ref, protos_ref, valid_ref, images_ref, prototypes_ref,
                other_ref, top_ref, mass_ref):
    top_ref[...] = jnp.full(top_ref.shape, far_below, jnp.float32)
    mass_ref[...] = jnp.zeros(mass_ref.shape, jnp.float32)
    score_scale = float(E) ** (-0.5)
    for position in range(MAXT):

        @pl.when(valid_ref[position] == 1)
        def _():
            row_block = rows_ref[position]
            proto_block = protos_ref[position]
            rows_here = images_ref[pl.ds(pl.multiple_of(row_block * TILE, TILE), TILE), :]
            protos_here = prototypes_ref[pl.ds(pl.multiple_of(proto_block * TILE, TILE), TILE), :]
            if along_rows:
                first, second, other_block, target = protos_here, rows_here, proto_block, row_block
            else:
                first, second, other_block, target = rows_here, protos_here, row_block, proto_block
            products = lax.dot_general(
                first, second, (((1,), (1,)), ((), ())), preferred_element_type=jnp.float32
            )
            values = products * score_scale + other_ref[other_block]
            local_top = jnp.max(values, axis=0, keepdims=True)
            old_top = top_ref[target]
            new_top = jnp.maximum(old_top, local_top)
            local_mass = jnp.sum(jnp.exp(values - new_top), axis=0, keepdims=True)
            mass_ref[target] = mass_ref[target] * jnp.exp(old_top - new_top) + local_mass
            top_ref[target] = new_top


def local_pass(along_rows, slots, images, prototypes, other_column):
    blocks = RB_DEV if along_rows else PB_DEV
    shape = jax.ShapeDtypeStruct((blocks, 1, TILE), jnp.float32)
    return pl.pallas_call(
        functools.partial(pass_kernel, along_rows),
        out_shape=(shape, shape),
        in_specs=slot_specs() + whole_specs(3),
        out_specs=tuple(whole_specs(2)),
    )(*slots, images, prototypes, other_column)


def final_kernel(rows_ref, protos_ref, valid_ref, images_ref, prototypes_ref,
                 col_ref, row_ref, out_ref):
    out_ref[...] = jnp.zeros(out_ref.shape, jnp.float32)
    score_scale = float(E) ** (-0.5)
    for position in range(MAXT):

        @pl.when(valid_ref[position] == 1)
        def _():
            row_block = rows_ref[position]
            proto_block = protos_ref[position]
            rows_here = images_ref[pl.ds(pl.multiple_of(row_block * TILE, TILE), TILE), :]
            protos_here = prototypes_ref[pl.ds(pl.multiple_of(proto_block * TILE, TILE), TILE), :]
            products = lax.dot_general(
                protos_here, rows_here, (((1,), (1,)), ((), ())), preferred_element_type=jnp.float32
            )
            weights = jnp.exp(
                products * score_scale + col_ref[proto_block] + row_ref[row_block]
            ).astype(jnp.bfloat16)
            out_ref[proto_block] += jnp.dot(weights, rows_here, preferred_element_type=jnp.float32)


def final_pass(slots, images, prototypes, col_column, row_pot):
    return pl.pallas_call(
        final_kernel,
        out_shape=jax.ShapeDtypeStruct((PB_DEV, TILE, E), jnp.float32),
        in_specs=slot_specs() + whole_specs(4),
        out_specs=pl.BlockSpec(memory_space=pltpu.VMEM),
    )(*slots, images, prototypes, col_column, row_pot.reshape(RB_DEV, 1, TILE))


def to_column(lanes):
    padded = jnp.concatenate(
        [lanes, jnp.zeros((8 - lanes.shape[0], TILE), jnp.float32)], axis=0
    ) if lanes.shape[0] < 8 else lanes
    return jnp.transpose(padded)


def exchange(axis, count, stage, local, packed, landed, send_sems, recv_sems):
    me = lax.axis_index(axis)
    packed[...] = local
    landed[stage, me] = local

    def peer_copy(peer, slot):
        return pltpu.make_async_remote_copy(
            src_ref=packed,
            dst_ref=landed.at[stage, slot],
            send_sem=send_sems.at[stage, peer],
            recv_sem=recv_sems.at[stage, slot],
            device_id={axis: peer},
            device_id_type=pl.DeviceIdType.MESH,
        )

    def send(step, carry):
        peer = lax.rem(me + step, count)
        peer_copy(peer, me).start()
        return carry

    lax.fori_loop(1, count, send, 0)

    def receive(step, carry):
        peer = lax.rem(me + count - step, count)
        peer_copy(peer, peer).wait_recv()
        return carry

    lax.fori_loop(1, count, receive, 0)

    def drain(step, carry):
        peer = lax.rem(me + step, count)
        peer_copy(peer, me).wait_send()
        return carry

    lax.fori_loop(1, count, drain, 0)
    gathered = landed[stage]
    highest = jnp.max(gathered, axis=0)
    summed = jnp.sum(jnp.exp(gathered - highest[None]), axis=0)
    return highest, summed


def pick_column(columns, chosen_block, blocks):
    picked = columns[:, 0:1]
    for block in range(1, blocks):
        picked = jnp.where(chosen_block == block, columns[:, block:block + 1], picked)
    return picked


def local_merge(along_rows, rows_ref, protos_ref, valid_ref, slot_images_ref, slot_protos_ref,
                other_columns):
    blocks = RB_DEV if along_rows else PB_DEV
    other_blocks = PB_DEV if along_rows else RB_DEV
    tops = [jnp.full((1, TILE), far_below, jnp.float32) for _ in range(blocks)]
    masses = [jnp.zeros((1, TILE), jnp.float32) for _ in range(blocks)]
    score_scale = float(E) ** (-0.5)
    for position in range(MAXT):
        row_block = rows_ref[position]
        proto_block = protos_ref[position]
        live = valid_ref[position] == 1
        rows_here = slot_images_ref[position]
        protos_here = slot_protos_ref[position]
        if along_rows:
            first, second, other_block, target = protos_here, rows_here, proto_block, row_block
        else:
            first, second, other_block, target = rows_here, protos_here, row_block, proto_block
        products = lax.dot_general(
            first, second, (((1,), (1,)), ((), ())), preferred_element_type=jnp.float32
        )
        values = products * score_scale + pick_column(other_columns, other_block, other_blocks)
        local_top = jnp.max(values, axis=0, keepdims=True)
        local_mass = jnp.sum(jnp.exp(values - local_top), axis=0, keepdims=True)
        for block in range(blocks):
            chosen = jnp.logical_and(live, target == block)
            new_top = jnp.maximum(tops[block], local_top)
            new_mass = masses[block] * jnp.exp(tops[block] - new_top) + local_mass * jnp.exp(
                local_top - new_top
            )
            tops[block] = jnp.where(chosen, new_top, tops[block])
            masses[block] = jnp.where(chosen, new_mass, masses[block])
    return jnp.concatenate(tops, axis=0) + jnp.log(jnp.concatenate(masses, axis=0))


def sinkhorn_kernel(log_ratio, rows_ref, protos_ref, valid_ref, images_ref, prototypes_ref,
                    row_out, col_out, col_columns_out,
                    row_packed, col_packed, row_landed, col_landed,
                    row_send, row_recv, col_send, col_recv):
    proto_count = lax.axis_size("proto")
    img_count = lax.axis_size("img")
    proto_me = lax.axis_index("proto")
    img_me = lax.axis_index("img")
    barrier = pltpu.get_barrier_semaphore()

    def greet_proto(step, carry):
        peer = lax.rem(proto_me + step, proto_count)
        pl.semaphore_signal(barrier, inc=1, device_id={"proto": peer},
                            device_id_type=pl.DeviceIdType.MESH)
        return carry

    def greet_img(step, carry):
        peer = lax.rem(img_me + step, img_count)
        pl.semaphore_signal(barrier, inc=1, device_id={"img": peer},
                            device_id_type=pl.DeviceIdType.MESH)
        return carry

    lax.fori_loop(1, proto_count, greet_proto, 0)
    lax.fori_loop(1, img_count, greet_img, 0)
    pl.semaphore_wait(barrier, proto_count + img_count - 2)

    col_t = jnp.zeros((TILE, PB_DEV), jnp.float32)
    for iteration in range(ITERS):
        local = local_merge(True, rows_ref, protos_ref, valid_ref, images_ref, prototypes_ref,
                            col_t)
        highest, summed = exchange("proto", proto_count, iteration, local, row_packed,
                                   row_landed, row_send, row_recv)
        row_pot = log_ratio - (highest + jnp.log(summed))
        row_t = to_column(row_pot)
        local = local_merge(False, rows_ref, protos_ref, valid_ref, images_ref, prototypes_ref,
                            row_t)
        highest, summed = exchange("img", img_count, iteration, local, col_packed,
                                   col_landed, col_send, col_recv)
        col_pot = -(highest + jnp.log(summed))
        col_t = to_column(col_pot)
    row_out[...] = row_pot
    col_out[...] = col_pot
    for block in range(PB_DEV):
        col_columns_out[block] = col_t[:, block:block + 1]


def sinkhorn(slots, slot_images, slot_protos, log_ratio):
    proto_count = lax.axis_size("proto")
    img_count = lax.axis_size("img")
    vmem = pltpu.VMEM
    return pl.pallas_call(
        functools.partial(sinkhorn_kernel, log_ratio),
        out_shape=(
            jax.ShapeDtypeStruct((RB_DEV, TILE), jnp.float32),
            jax.ShapeDtypeStruct((PB_DEV, TILE), jnp.float32),
            jax.ShapeDtypeStruct((PB_DEV, TILE, 1), jnp.float32),
        ),
        in_specs=slot_specs() + whole_specs(2),
        out_specs=tuple(whole_specs(3)),
        scratch_shapes=[
            vmem((RB_DEV, TILE), jnp.float32),
            vmem((PB_DEV, TILE), jnp.float32),
            vmem((ITERS, proto_count, RB_DEV, TILE), jnp.float32),
            vmem((ITERS, img_count, PB_DEV, TILE), jnp.float32),
            pltpu.SemaphoreType.DMA((ITERS, proto_count)),
            pltpu.SemaphoreType.DMA((ITERS, proto_count)),
            pltpu.SemaphoreType.DMA((ITERS, img_count)),
            pltpu.SemaphoreType.DMA((ITERS, img_count)),
        ],
        compiler_params=pltpu.CompilerParams(collective_id=0, has_side_effects=True),
    )(*slots, slot_images, slot_protos)


def shards(images, prototypes, tile_row, tile_proto, tile_valid):
    img_count = lax.axis_size("img")
    proto_count = lax.axis_size("proto")
    slots = (tile_row.reshape(MAXT), tile_proto.reshape(MAXT), tile_valid.reshape(MAXT))
    log_ratio = math.log(PB_DEV * proto_count / (RB_DEV * img_count))
    slot_images = images.reshape(RB_DEV, TILE, E)[slots[0]]
    slot_protos = prototypes.reshape(PB_DEV, TILE, E)[slots[1]]
    row_pot, col_pot, col_columns = sinkhorn(slots, slot_images, slot_protos, log_ratio)
    partial_value = final_pass(slots, images, prototypes, col_columns, row_pot)
    img_count = lax.axis_size("img")
    shares = lax.all_to_all(
        partial_value.reshape(img_count, PB_DEV * TILE // img_count, E).astype(jnp.bfloat16),
        "img",
        0,
        0,
    )
    proto_share = jnp.sum(shares.astype(jnp.float32), axis=0)
    return (proto_share, col_pot.reshape(PB_DEV * TILE))


def solution(mesh):
    return jax.shard_map(
        shards,
        mesh=mesh,
        in_specs=(
            P("img", None),
            P("proto", None),
            P("img", "proto", None),
            P("img", "proto", None),
            P("img", "proto", None),
        ),
        out_specs=(P(("proto", "img"), None), P("proto")),
        check_vma=False,
    )
```

```python
import functools
import math

import jax
import jax.numpy as jnp
from jax import lax
from jax.experimental import pallas as pl
from jax.experimental.pallas import tpu as pltpu
from jax.sharding import PartitionSpec as P

E = 256
TILE = 512
RB_DEV = 4
PB_DEV = 8
MAXT = 6
ITERS = 3


far_below = -1e30


def running_top(values_of, live_slots, reduced, slot_blocks, block_count):

    def advance(position, tops):
        local_top = jnp.max(values_of(position), axis=reduced)
        target = slot_blocks[position]
        old_top = lax.dynamic_index_in_dim(tops, target, 0, keepdims=False)
        return lax.dynamic_update_index_in_dim(tops, jnp.maximum(old_top, local_top), target, 0)

    return lax.fori_loop(
        0, live_slots, advance, jnp.full((block_count, TILE), far_below, jnp.float32)
    )


def running_mass(values_of, live_slots, reduced, slot_blocks, tops):

    def advance(position, masses):
        target = slot_blocks[position]
        top_here = lax.dynamic_index_in_dim(tops, target, 0, keepdims=False)
        local_mass = jnp.sum(
            jnp.exp(values_of(position) - jnp.expand_dims(top_here, reduced)), axis=reduced
        )
        old_mass = lax.dynamic_index_in_dim(masses, target, 0, keepdims=False)
        return lax.dynamic_update_index_in_dim(masses, old_mass + local_mass, target, 0)

    return lax.fori_loop(0, live_slots, advance, jnp.zeros_like(tops))


def gather_kernel(axis, x_ref, out_ref, landed, send_sems, recv_sems):
    count = lax.axis_size(axis)
    me = lax.axis_index(axis)

    def peer_copy(peer, slot):
        return pltpu.make_async_remote_copy(
            src_ref=x_ref,
            dst_ref=landed.at[slot],
            send_sem=send_sems.at[slot],
            recv_sem=recv_sems.at[slot],
            device_id={axis: peer},
            device_id_type=pl.DeviceIdType.MESH,
        )

    landed[me] = x_ref[...]

    def send(step, carry):
        peer = lax.rem(me + step, count)
        peer_copy(peer, me).start()
        return carry

    lax.fori_loop(1, count, send, 0)

    def receive(step, carry):
        peer = lax.rem(me + count - step, count)
        peer_copy(peer, peer).wait_recv()
        return carry

    lax.fori_loop(1, count, receive, 0)

    def drain(step, carry):
        peer = lax.rem(me + step, count)
        peer_copy(peer, me).wait_send()
        return carry

    lax.fori_loop(1, count, drain, 0)
    out_ref[...] = landed[...]


def gather_peers(block, axis):
    count = lax.axis_size(axis)
    shape = (count,) + block.shape
    return pl.pallas_call(
        functools.partial(gather_kernel, axis),
        out_shape=jax.ShapeDtypeStruct(shape, block.dtype),
        in_specs=[pl.BlockSpec(memory_space=pltpu.VMEM)],
        out_specs=pl.BlockSpec(memory_space=pltpu.VMEM),
        scratch_shapes=[
            pltpu.VMEM(shape, block.dtype),
            pltpu.SemaphoreType.DMA((count,)),
            pltpu.SemaphoreType.DMA((count,)),
        ],
        compiler_params=pltpu.CompilerParams(has_side_effects=True),
    )(block)


def merge_tops(local_top, local_mass, axis):
    gathered = gather_peers(jnp.stack([local_top, local_mass]), axis)
    tops, masses = gathered[:, 0], gathered[:, 1]
    highest = jnp.max(tops, axis=0)
    summed = jnp.sum(masses * jnp.exp(tops - highest[None]), axis=0)
    return highest, summed


def slot_specs():
    return [pl.BlockSpec(memory_space=pltpu.SMEM)] * 3


def whole_specs(count):
    return [pl.BlockSpec(memory_space=pltpu.VMEM)] * count


def pass_kernel(along_rows, rows_ref, protos_ref, valid_ref, images_ref, prototypes_ref,
                other_ref, top_ref, mass_ref):
    top_ref[...] = jnp.full(top_ref.shape, far_below, jnp.float32)
    mass_ref[...] = jnp.zeros(mass_ref.shape, jnp.float32)
    score_scale = float(E) ** (-0.5)
    for position in range(MAXT):

        @pl.when(valid_ref[position] == 1)
        def _():
            row_block = rows_ref[position]
            proto_block = protos_ref[position]
            rows_here = images_ref[pl.ds(pl.multiple_of(row_block * TILE, TILE), TILE), :]
            protos_here = prototypes_ref[pl.ds(pl.multiple_of(proto_block * TILE, TILE), TILE), :]
            if along_rows:
                first, second, other_block, target = protos_here, rows_here, proto_block, row_block
            else:
                first, second, other_block, target = rows_here, protos_here, row_block, proto_block
            products = lax.dot_general(
                first, second, (((1,), (1,)), ((), ())), preferred_element_type=jnp.float32
            )
            values = products * score_scale + other_ref[other_block]
            local_top = jnp.max(values, axis=0, keepdims=True)
            old_top = top_ref[target]
            new_top = jnp.maximum(old_top, local_top)
            local_mass = jnp.sum(jnp.exp(values - new_top), axis=0, keepdims=True)
            mass_ref[target] = mass_ref[target] * jnp.exp(old_top - new_top) + local_mass
            top_ref[target] = new_top


def local_pass(along_rows, slots, images, prototypes, other_column):
    blocks = RB_DEV if along_rows else PB_DEV
    shape = jax.ShapeDtypeStruct((blocks, 1, TILE), jnp.float32)
    return pl.pallas_call(
        functools.partial(pass_kernel, along_rows),
        out_shape=(shape, shape),
        in_specs=slot_specs() + whole_specs(3),
        out_specs=tuple(whole_specs(2)),
    )(*slots, images, prototypes, other_column)


def final_kernel(rows_ref, protos_ref, valid_ref, images_ref, prototypes_ref,
                 col_ref, row_ref, out_ref):
    out_ref[...] = jnp.zeros(out_ref.shape, jnp.float32)
    score_scale = float(E) ** (-0.5)
    for position in range(MAXT):

        @pl.when(valid_ref[position] == 1)
        def _():
            row_block = rows_ref[position]
            proto_block = protos_ref[position]
            rows_here = images_ref[pl.ds(pl.multiple_of(row_block * TILE, TILE), TILE), :]
            protos_here = prototypes_ref[pl.ds(pl.multiple_of(proto_block * TILE, TILE), TILE), :]
            products = lax.dot_general(
                protos_here, rows_here, (((1,), (1,)), ((), ())), preferred_element_type=jnp.float32
            )
            weights = jnp.exp(
                products * score_scale + col_ref[proto_block] + row_ref[row_block]
            ).astype(jnp.bfloat16)
            out_ref[proto_block] += jnp.dot(weights, rows_here, preferred_element_type=jnp.float32)


def final_pass(slots, images, prototypes, col_column, row_pot):
    return pl.pallas_call(
        final_kernel,
        out_shape=jax.ShapeDtypeStruct((PB_DEV, TILE, E), jnp.float32),
        in_specs=slot_specs() + whole_specs(4),
        out_specs=pl.BlockSpec(memory_space=pltpu.VMEM),
    )(*slots, images, prototypes, col_column, row_pot.reshape(RB_DEV, 1, TILE))


def to_column(lanes):
    padded = jnp.concatenate(
        [lanes, jnp.zeros((8 - lanes.shape[0], TILE), jnp.float32)], axis=0
    ) if lanes.shape[0] < 8 else lanes
    return jnp.transpose(padded)


def stage_peer(axis, size, stride, step):
    me = lax.axis_index(axis)
    place = lax.rem(me // stride, size)
    return me + (lax.rem(place + step, size) - place) * stride, place


def exchange_stage(axis, size, stride, stage, local, packed, landed, send_sems, recv_sems):
    place = stage_peer(axis, size, stride, 0)[1]
    packed[...] = local
    landed[stage, place] = local

    def peer_copy(step, slot):
        return pltpu.make_async_remote_copy(
            src_ref=packed,
            dst_ref=landed.at[stage, slot],
            send_sem=send_sems.at[stage, lax.rem(place + step, size)],
            recv_sem=recv_sems.at[stage, slot],
            device_id={axis: stage_peer(axis, size, stride, step)[0]},
            device_id_type=pl.DeviceIdType.MESH,
        )

    def send(step, carry):
        peer_copy(step, place).start()
        return carry

    lax.fori_loop(1, size, send, 0)

    def receive(step, carry):
        peer_copy(size - step, lax.rem(place + size - step, size)).wait_recv()
        return carry

    lax.fori_loop(1, size, receive, 0)

    def drain(step, carry):
        peer_copy(step, place).wait_send()
        return carry

    lax.fori_loop(1, size, drain, 0)
    gathered = landed[stage]
    highest = jnp.max(gathered, axis=0)
    return highest + jnp.log(jnp.sum(jnp.exp(gathered - highest[None]), axis=0))


def exchange(axis, groups, stage, local, packed, landed_refs, send_refs, recv_refs):
    for (size, stride), landed, send_sems, recv_sems in zip(groups, landed_refs, send_refs,
                                                           recv_refs):
        local = exchange_stage(axis, size, stride, stage, local, packed, landed, send_sems,
                               recv_sems)
    return local


def pick_column(columns, chosen_block, blocks):
    picked = columns[:, 0:1]
    for block in range(1, blocks):
        picked = jnp.where(chosen_block == block, columns[:, block:block + 1], picked)
    return picked


def local_merge(along_rows, rows_ref, protos_ref, valid_ref, slot_images_ref, slot_protos_ref,
                other_columns):
    blocks = RB_DEV if along_rows else PB_DEV
    other_blocks = PB_DEV if along_rows else RB_DEV
    tops = [jnp.full((1, TILE), far_below, jnp.float32) for _ in range(blocks)]
    masses = [jnp.zeros((1, TILE), jnp.float32) for _ in range(blocks)]
    score_scale = float(E) ** (-0.5)
    for position in range(MAXT):
        row_block = rows_ref[position]
        proto_block = protos_ref[position]
        live = valid_ref[position] == 1
        rows_here = slot_images_ref[position]
        protos_here = slot_protos_ref[position]
        if along_rows:
            first, second, other_block, target = protos_here, rows_here, proto_block, row_block
        else:
            first, second, other_block, target = rows_here, protos_here, row_block, proto_block
        products = lax.dot_general(
            first, second, (((1,), (1,)), ((), ())), preferred_element_type=jnp.float32
        )
        values = products * score_scale + pick_column(other_columns, other_block, other_blocks)
        local_top = jnp.max(values, axis=0, keepdims=True)
        local_mass = jnp.sum(jnp.exp(values - local_top), axis=0, keepdims=True)
        for block in range(blocks):
            chosen = jnp.logical_and(live, target == block)
            new_top = jnp.maximum(tops[block], local_top)
            new_mass = masses[block] * jnp.exp(tops[block] - new_top) + local_mass * jnp.exp(
                local_top - new_top
            )
            tops[block] = jnp.where(chosen, new_top, tops[block])
            masses[block] = jnp.where(chosen, new_mass, masses[block])
    return jnp.maximum(
        jnp.concatenate(tops, axis=0) + jnp.log(jnp.concatenate(masses, axis=0)), far_below
    )


def axis_groups():
    proto_count = lax.axis_size("proto")
    img_count = lax.axis_size("img")
    return {
        "proto": ((PB_DEV, 1), (proto_count // PB_DEV, PB_DEV)),
        "img": ((2, 1), (img_count // 2, 2)),
    }


def sinkhorn_kernel(log_ratio, rows_ref, protos_ref, valid_ref, images_ref, prototypes_ref,
                    row_out, col_out, col_columns_out, row_packed, col_packed, *stage_refs):
    groups = axis_groups()
    row_refs = stage_refs[0:6]
    col_refs = stage_refs[6:12]
    barrier = pltpu.get_barrier_semaphore()
    greeted = 0
    for axis in ("proto", "img"):
        for size, stride in groups[axis]:

            def greet(step, carry):
                peer = stage_peer(axis, size, stride, step)[0]
                pl.semaphore_signal(barrier, inc=1, device_id={axis: peer},
                                    device_id_type=pl.DeviceIdType.MESH)
                return carry

            lax.fori_loop(1, size, greet, 0)
            greeted += size - 1
    pl.semaphore_wait(barrier, greeted)

    col_t = jnp.zeros((TILE, PB_DEV), jnp.float32)
    for iteration in range(ITERS):
        local = local_merge(True, rows_ref, protos_ref, valid_ref, images_ref, prototypes_ref,
                            col_t)
        merged = exchange("proto", groups["proto"], iteration, local, row_packed,
                          row_refs[0:2], row_refs[2:4], row_refs[4:6])
        row_pot = log_ratio - merged
        row_t = to_column(row_pot)
        local = local_merge(False, rows_ref, protos_ref, valid_ref, images_ref, prototypes_ref,
                            row_t)
        merged = exchange("img", groups["img"], iteration, local, col_packed,
                          col_refs[0:2], col_refs[2:4], col_refs[4:6])
        col_pot = -merged
        col_t = to_column(col_pot)
    row_out[...] = row_pot
    col_out[...] = col_pot
    for block in range(PB_DEV):
        col_columns_out[block] = col_t[:, block:block + 1]


def sinkhorn(slots, slot_images, slot_protos, log_ratio):
    groups = axis_groups()
    vmem = pltpu.VMEM
    stage_scratch = []
    for axis, blocks in (("proto", RB_DEV), ("img", PB_DEV)):
        sizes = [size for size, _ in groups[axis]]
        stage_scratch += [vmem((ITERS, size, blocks, TILE), jnp.float32) for size in sizes]
        stage_scratch += [pltpu.SemaphoreType.DMA((ITERS, size)) for size in sizes]
        stage_scratch += [pltpu.SemaphoreType.DMA((ITERS, size)) for size in sizes]
    return pl.pallas_call(
        functools.partial(sinkhorn_kernel, log_ratio),
        out_shape=(
            jax.ShapeDtypeStruct((RB_DEV, TILE), jnp.float32),
            jax.ShapeDtypeStruct((PB_DEV, TILE), jnp.float32),
            jax.ShapeDtypeStruct((PB_DEV, TILE, 1), jnp.float32),
        ),
        in_specs=slot_specs() + whole_specs(2),
        out_specs=tuple(whole_specs(3)),
        scratch_shapes=[
            vmem((RB_DEV, TILE), jnp.float32),
            vmem((PB_DEV, TILE), jnp.float32),
        ] + stage_scratch,
        compiler_params=pltpu.CompilerParams(collective_id=0, has_side_effects=True),
    )(*slots, slot_images, slot_protos)


def shards(images, prototypes, tile_row, tile_proto, tile_valid):
    img_count = lax.axis_size("img")
    proto_count = lax.axis_size("proto")
    slots = (tile_row.reshape(MAXT), tile_proto.reshape(MAXT), tile_valid.reshape(MAXT))
    log_ratio = math.log(PB_DEV * proto_count / (RB_DEV * img_count))
    slot_images = images.reshape(RB_DEV, TILE, E)[slots[0]]
    slot_protos = prototypes.reshape(PB_DEV, TILE, E)[slots[1]]
    row_pot, col_pot, col_columns = sinkhorn(slots, slot_images, slot_protos, log_ratio)
    partial_value = final_pass(slots, images, prototypes, col_columns, row_pot)
    img_count = lax.axis_size("img")
    shares = lax.all_to_all(
        partial_value.reshape(img_count, PB_DEV * TILE // img_count, E).astype(jnp.bfloat16),
        "img",
        0,
        0,
    )
    proto_share = jnp.sum(shares.astype(jnp.float32), axis=0)
    return (proto_share, col_pot.reshape(PB_DEV * TILE))


def solution(mesh):
    return jax.shard_map(
        shards,
        mesh=mesh,
        in_specs=(
            P("img", None),
            P("proto", None),
            P("img", "proto", None),
            P("img", "proto", None),
            P("img", "proto", None),
        ),
        out_specs=(P(("proto", "img"), None), P("proto")),
        check_vma=False,
    )
```

```python
import functools
import math

import jax
import jax.numpy as jnp
from jax import lax
from jax.experimental import pallas as pl
from jax.experimental.pallas import tpu as pltpu
from jax.sharding import PartitionSpec as P

E = 256
TILE = 512
RB_DEV = 4
PB_DEV = 8
MAXT = 6
ITERS = 3


far_below = -1e30


def running_top(values_of, live_slots, reduced, slot_blocks, block_count):

    def advance(position, tops):
        local_top = jnp.max(values_of(position), axis=reduced)
        target = slot_blocks[position]
        old_top = lax.dynamic_index_in_dim(tops, target, 0, keepdims=False)
        return lax.dynamic_update_index_in_dim(tops, jnp.maximum(old_top, local_top), target, 0)

    return lax.fori_loop(
        0, live_slots, advance, jnp.full((block_count, TILE), far_below, jnp.float32)
    )


def running_mass(values_of, live_slots, reduced, slot_blocks, tops):

    def advance(position, masses):
        target = slot_blocks[position]
        top_here = lax.dynamic_index_in_dim(tops, target, 0, keepdims=False)
        local_mass = jnp.sum(
            jnp.exp(values_of(position) - jnp.expand_dims(top_here, reduced)), axis=reduced
        )
        old_mass = lax.dynamic_index_in_dim(masses, target, 0, keepdims=False)
        return lax.dynamic_update_index_in_dim(masses, old_mass + local_mass, target, 0)

    return lax.fori_loop(0, live_slots, advance, jnp.zeros_like(tops))


def gather_kernel(axis, x_ref, out_ref, landed, send_sems, recv_sems):
    count = lax.axis_size(axis)
    me = lax.axis_index(axis)

    def peer_copy(peer, slot):
        return pltpu.make_async_remote_copy(
            src_ref=x_ref,
            dst_ref=landed.at[slot],
            send_sem=send_sems.at[slot],
            recv_sem=recv_sems.at[slot],
            device_id={axis: peer},
            device_id_type=pl.DeviceIdType.MESH,
        )

    landed[me] = x_ref[...]

    def send(step, carry):
        peer = lax.rem(me + step, count)
        peer_copy(peer, me).start()
        return carry

    lax.fori_loop(1, count, send, 0)

    def receive(step, carry):
        peer = lax.rem(me + count - step, count)
        peer_copy(peer, peer).wait_recv()
        return carry

    lax.fori_loop(1, count, receive, 0)

    def drain(step, carry):
        peer = lax.rem(me + step, count)
        peer_copy(peer, me).wait_send()
        return carry

    lax.fori_loop(1, count, drain, 0)
    out_ref[...] = landed[...]


def gather_peers(block, axis):
    count = lax.axis_size(axis)
    shape = (count,) + block.shape
    return pl.pallas_call(
        functools.partial(gather_kernel, axis),
        out_shape=jax.ShapeDtypeStruct(shape, block.dtype),
        in_specs=[pl.BlockSpec(memory_space=pltpu.VMEM)],
        out_specs=pl.BlockSpec(memory_space=pltpu.VMEM),
        scratch_shapes=[
            pltpu.VMEM(shape, block.dtype),
            pltpu.SemaphoreType.DMA((count,)),
            pltpu.SemaphoreType.DMA((count,)),
        ],
        compiler_params=pltpu.CompilerParams(has_side_effects=True),
    )(block)


def merge_tops(local_top, local_mass, axis):
    gathered = gather_peers(jnp.stack([local_top, local_mass]), axis)
    tops, masses = gathered[:, 0], gathered[:, 1]
    highest = jnp.max(tops, axis=0)
    summed = jnp.sum(masses * jnp.exp(tops - highest[None]), axis=0)
    return highest, summed


def slot_specs():
    return [pl.BlockSpec(memory_space=pltpu.SMEM)] * 3


def whole_specs(count):
    return [pl.BlockSpec(memory_space=pltpu.VMEM)] * count


def pass_kernel(along_rows, rows_ref, protos_ref, valid_ref, images_ref, prototypes_ref,
                other_ref, top_ref, mass_ref):
    top_ref[...] = jnp.full(top_ref.shape, far_below, jnp.float32)
    mass_ref[...] = jnp.zeros(mass_ref.shape, jnp.float32)
    score_scale = float(E) ** (-0.5)
    for position in range(MAXT):

        @pl.when(valid_ref[position] == 1)
        def _():
            row_block = rows_ref[position]
            proto_block = protos_ref[position]
            rows_here = images_ref[pl.ds(pl.multiple_of(row_block * TILE, TILE), TILE), :]
            protos_here = prototypes_ref[pl.ds(pl.multiple_of(proto_block * TILE, TILE), TILE), :]
            if along_rows:
                first, second, other_block, target = protos_here, rows_here, proto_block, row_block
            else:
                first, second, other_block, target = rows_here, protos_here, row_block, proto_block
            products = lax.dot_general(
                first, second, (((1,), (1,)), ((), ())), preferred_element_type=jnp.float32
            )
            values = products * score_scale + other_ref[other_block]
            local_top = jnp.max(values, axis=0, keepdims=True)
            old_top = top_ref[target]
            new_top = jnp.maximum(old_top, local_top)
            local_mass = jnp.sum(jnp.exp(values - new_top), axis=0, keepdims=True)
            mass_ref[target] = mass_ref[target] * jnp.exp(old_top - new_top) + local_mass
            top_ref[target] = new_top


def local_pass(along_rows, slots, images, prototypes, other_column):
    blocks = RB_DEV if along_rows else PB_DEV
    shape = jax.ShapeDtypeStruct((blocks, 1, TILE), jnp.float32)
    return pl.pallas_call(
        functools.partial(pass_kernel, along_rows),
        out_shape=(shape, shape),
        in_specs=slot_specs() + whole_specs(3),
        out_specs=tuple(whole_specs(2)),
    )(*slots, images, prototypes, other_column)


def final_kernel(rows_ref, protos_ref, valid_ref, images_ref, prototypes_ref,
                 col_ref, row_ref, out_ref):
    out_ref[...] = jnp.zeros(out_ref.shape, jnp.float32)
    score_scale = float(E) ** (-0.5)
    for position in range(MAXT):

        @pl.when(valid_ref[position] == 1)
        def _():
            row_block = rows_ref[position]
            proto_block = protos_ref[position]
            rows_here = images_ref[pl.ds(pl.multiple_of(row_block * TILE, TILE), TILE), :]
            protos_here = prototypes_ref[pl.ds(pl.multiple_of(proto_block * TILE, TILE), TILE), :]
            products = lax.dot_general(
                protos_here, rows_here, (((1,), (1,)), ((), ())), preferred_element_type=jnp.float32
            )
            weights = jnp.exp(
                products * score_scale + col_ref[proto_block] + row_ref[row_block]
            ).astype(jnp.bfloat16)
            out_ref[proto_block] += jnp.dot(weights, rows_here, preferred_element_type=jnp.float32)


def final_pass(slots, images, prototypes, col_column, row_pot):
    return pl.pallas_call(
        final_kernel,
        out_shape=jax.ShapeDtypeStruct((PB_DEV, TILE, E), jnp.float32),
        in_specs=slot_specs() + whole_specs(4),
        out_specs=pl.BlockSpec(memory_space=pltpu.VMEM),
    )(*slots, images, prototypes, col_column, row_pot.reshape(RB_DEV, 1, TILE))


def to_column(lanes):
    padded = jnp.concatenate(
        [lanes, jnp.zeros((8 - lanes.shape[0], TILE), jnp.float32)], axis=0
    ) if lanes.shape[0] < 8 else lanes
    return jnp.transpose(padded)


def stage_peer(axis, size, stride, step):
    me = lax.axis_index(axis)
    place = lax.rem(me // stride, size)
    return me + (lax.rem(place + step, size) - place) * stride, place


def exchange_stage(axis, size, stride, stage, local, packed, landed, send_sems, recv_sems):
    place = stage_peer(axis, size, stride, 0)[1]
    packed[...] = local
    landed[stage, place] = local

    def peer_copy(step, slot):
        return pltpu.make_async_remote_copy(
            src_ref=packed,
            dst_ref=landed.at[stage, slot],
            send_sem=send_sems.at[stage, lax.rem(place + step, size)],
            recv_sem=recv_sems.at[stage, slot],
            device_id={axis: stage_peer(axis, size, stride, step)[0]},
            device_id_type=pl.DeviceIdType.MESH,
        )

    def send(step, carry):
        peer_copy(step, place).start()
        return carry

    lax.fori_loop(1, size, send, 0)

    def receive(step, carry):
        peer_copy(size - step, lax.rem(place + size - step, size)).wait_recv()
        return carry

    lax.fori_loop(1, size, receive, 0)

    def drain(step, carry):
        peer_copy(step, place).wait_send()
        return carry

    lax.fori_loop(1, size, drain, 0)
    gathered = landed[stage]
    highest = jnp.max(gathered, axis=0)
    return highest + jnp.log(jnp.sum(jnp.exp(gathered - highest[None]), axis=0))


def exchange(axis, groups, stage, local, packed, landed_refs, send_refs, recv_refs):
    for (size, stride), landed, send_sems, recv_sems in zip(groups, landed_refs, send_refs,
                                                           recv_refs):
        local = exchange_stage(axis, size, stride, stage, local, packed, landed, send_sems,
                               recv_sems)
    return local


def pick_column(columns, chosen_block, blocks):
    picked = columns[:, 0:1]
    for block in range(1, blocks):
        picked = jnp.where(chosen_block == block, columns[:, block:block + 1], picked)
    return picked


def local_merge(along_rows, rows_ref, protos_ref, valid_ref, slot_images_ref, slot_protos_ref,
                other_columns):
    blocks = RB_DEV if along_rows else PB_DEV
    other_blocks = PB_DEV if along_rows else RB_DEV
    tops = [jnp.full((1, TILE), far_below, jnp.float32) for _ in range(blocks)]
    masses = [jnp.zeros((1, TILE), jnp.float32) for _ in range(blocks)]
    score_scale = float(E) ** (-0.5)
    for position in range(MAXT):
        row_block = rows_ref[position]
        proto_block = protos_ref[position]
        live = valid_ref[position] == 1
        rows_here = slot_images_ref[position]
        protos_here = slot_protos_ref[position]
        if along_rows:
            first, second, other_block, target = protos_here, rows_here, proto_block, row_block
        else:
            first, second, other_block, target = rows_here, protos_here, row_block, proto_block
        products = lax.dot_general(
            first, second, (((1,), (1,)), ((), ())), preferred_element_type=jnp.float32
        )
        values = products * score_scale + pick_column(other_columns, other_block, other_blocks)
        local_top = jnp.max(values, axis=0, keepdims=True)
        local_mass = jnp.sum(jnp.exp(values - local_top), axis=0, keepdims=True)
        for block in range(blocks):
            chosen = jnp.logical_and(live, target == block)
            new_top = jnp.maximum(tops[block], local_top)
            new_mass = masses[block] * jnp.exp(tops[block] - new_top) + local_mass * jnp.exp(
                local_top - new_top
            )
            tops[block] = jnp.where(chosen, new_top, tops[block])
            masses[block] = jnp.where(chosen, new_mass, masses[block])
    return jnp.maximum(
        jnp.concatenate(tops, axis=0) + jnp.log(jnp.concatenate(masses, axis=0)), far_below
    )


def axis_groups():
    proto_count = lax.axis_size("proto")
    img_count = lax.axis_size("img")
    return {
        "proto": ((PB_DEV, 1), (proto_count // PB_DEV, PB_DEV)),
        "img": ((2, 1), (img_count // 2, 2)),
    }


def sinkhorn_kernel(log_ratio, rows_ref, protos_ref, valid_ref, images_ref, prototypes_ref,
                    row_out, col_out, col_columns_out, row_packed, col_packed, *stage_refs):
    groups = axis_groups()
    row_refs = stage_refs[0:6]
    col_refs = stage_refs[6:12]
    barrier = pltpu.get_barrier_semaphore()
    greeted = 0
    for axis in ("proto", "img"):
        for size, stride in groups[axis]:

            def greet(step, carry):
                peer = stage_peer(axis, size, stride, step)[0]
                pl.semaphore_signal(barrier, inc=1, device_id={axis: peer},
                                    device_id_type=pl.DeviceIdType.MESH)
                return carry

            lax.fori_loop(1, size, greet, 0)
            greeted += size - 1
    pl.semaphore_wait(barrier, greeted)

    col_t = jnp.zeros((TILE, PB_DEV), jnp.float32)
    for iteration in range(ITERS):
        local = local_merge(True, rows_ref, protos_ref, valid_ref, images_ref, prototypes_ref,
                            col_t)
        merged = exchange("proto", groups["proto"], iteration, local, row_packed,
                          row_refs[0:2], row_refs[2:4], row_refs[4:6])
        row_pot = log_ratio - merged
        row_t = to_column(row_pot)
        local = local_merge(False, rows_ref, protos_ref, valid_ref, images_ref, prototypes_ref,
                            row_t)
        merged = exchange("img", groups["img"], iteration, local, col_packed,
                          col_refs[0:2], col_refs[2:4], col_refs[4:6])
        col_pot = -merged
        col_t = to_column(col_pot)
    row_out[...] = row_pot
    col_out[...] = col_pot
    for block in range(PB_DEV):
        col_columns_out[block] = col_t[:, block:block + 1]


def sinkhorn(slots, slot_images, slot_protos, log_ratio):
    groups = axis_groups()
    vmem = pltpu.VMEM
    stage_scratch = []
    for axis, blocks in (("proto", RB_DEV), ("img", PB_DEV)):
        sizes = [size for size, _ in groups[axis]]
        stage_scratch += [vmem((ITERS, size, blocks, TILE), jnp.float32) for size in sizes]
        stage_scratch += [pltpu.SemaphoreType.DMA((ITERS, size)) for size in sizes]
        stage_scratch += [pltpu.SemaphoreType.DMA((ITERS, size)) for size in sizes]
    return pl.pallas_call(
        functools.partial(sinkhorn_kernel, log_ratio),
        out_shape=(
            jax.ShapeDtypeStruct((RB_DEV, TILE), jnp.float32),
            jax.ShapeDtypeStruct((PB_DEV, TILE), jnp.float32),
            jax.ShapeDtypeStruct((PB_DEV, TILE, 1), jnp.float32),
        ),
        in_specs=slot_specs() + whole_specs(2),
        out_specs=tuple(whole_specs(3)),
        scratch_shapes=[
            vmem((RB_DEV, TILE), jnp.float32),
            vmem((PB_DEV, TILE), jnp.float32),
        ] + stage_scratch,
        compiler_params=pltpu.CompilerParams(collective_id=0, has_side_effects=True),
    )(*slots, slot_images, slot_protos)


def scatter_kernel(shares_ref, out_ref, landed, send_sems, recv_sems):
    count = lax.axis_size("img")
    me = lax.axis_index("img")
    barrier = pltpu.get_barrier_semaphore()

    def greet(step, carry):
        pl.semaphore_signal(barrier, inc=1, device_id={"img": lax.rem(me + step, count)},
                            device_id_type=pl.DeviceIdType.MESH)
        return carry

    lax.fori_loop(1, count, greet, 0)
    pl.semaphore_wait(barrier, count - 1)

    def peer_copy(peer, slot, source):
        return pltpu.make_async_remote_copy(
            src_ref=shares_ref.at[source],
            dst_ref=landed.at[slot],
            send_sem=send_sems.at[peer],
            recv_sem=recv_sems.at[slot],
            device_id={"img": peer},
            device_id_type=pl.DeviceIdType.MESH,
        )

    def send(step, carry):
        peer = lax.rem(me + step, count)
        peer_copy(peer, me, peer).start()
        return carry

    lax.fori_loop(1, count, send, 0)
    out_ref[...] = shares_ref[me].astype(jnp.float32)

    def receive(step, carry):
        peer = lax.rem(me + count - step, count)
        peer_copy(peer, peer, me).wait_recv()
        out_ref[...] += landed[peer].astype(jnp.float32)
        return carry

    lax.fori_loop(1, count, receive, 0)

    def drain(step, carry):
        peer = lax.rem(me + step, count)
        peer_copy(peer, me, peer).wait_send()
        return carry

    lax.fori_loop(1, count, drain, 0)


def scatter_sum(shares):
    count, rows, width = shares.shape
    return pl.pallas_call(
        scatter_kernel,
        out_shape=jax.ShapeDtypeStruct((rows, width), jnp.float32),
        in_specs=whole_specs(1),
        out_specs=pl.BlockSpec(memory_space=pltpu.VMEM),
        scratch_shapes=[
            pltpu.VMEM(shares.shape, shares.dtype),
            pltpu.SemaphoreType.DMA((count,)),
            pltpu.SemaphoreType.DMA((count,)),
        ],
        compiler_params=pltpu.CompilerParams(collective_id=1, has_side_effects=True),
    )(shares)


def shards(images, prototypes, tile_row, tile_proto, tile_valid):
    img_count = lax.axis_size("img")
    proto_count = lax.axis_size("proto")
    slots = (tile_row.reshape(MAXT), tile_proto.reshape(MAXT), tile_valid.reshape(MAXT))
    log_ratio = math.log(PB_DEV * proto_count / (RB_DEV * img_count))
    slot_images = images.reshape(RB_DEV, TILE, E)[slots[0]]
    slot_protos = prototypes.reshape(PB_DEV, TILE, E)[slots[1]]
    row_pot, col_pot, col_columns = sinkhorn(slots, slot_images, slot_protos, log_ratio)
    partial_value = final_pass(slots, images, prototypes, col_columns, row_pot)
    img_count = lax.axis_size("img")
    proto_share = scatter_sum(
        partial_value.reshape(img_count, PB_DEV * TILE // img_count, E).astype(jnp.bfloat16)
    )
    return (proto_share, col_pot.reshape(PB_DEV * TILE))


def solution(mesh):
    return jax.shard_map(
        shards,
        mesh=mesh,
        in_specs=(
            P("img", None),
            P("proto", None),
            P("img", "proto", None),
            P("img", "proto", None),
            P("img", "proto", None),
        ),
        out_specs=(P(("proto", "img"), None), P("proto")),
        check_vma=False,
    )
```

```python
import functools
import math

import jax
import jax.numpy as jnp
from jax import lax
from jax.experimental import pallas as pl
from jax.experimental.pallas import tpu as pltpu
from jax.sharding import PartitionSpec as P

E = 256
TILE = 512
RB_DEV = 4
PB_DEV = 8
MAXT = 6
ITERS = 3


far_below = -1e30


def running_top(values_of, live_slots, reduced, slot_blocks, block_count):

    def advance(position, tops):
        local_top = jnp.max(values_of(position), axis=reduced)
        target = slot_blocks[position]
        old_top = lax.dynamic_index_in_dim(tops, target, 0, keepdims=False)
        return lax.dynamic_update_index_in_dim(tops, jnp.maximum(old_top, local_top), target, 0)

    return lax.fori_loop(
        0, live_slots, advance, jnp.full((block_count, TILE), far_below, jnp.float32)
    )


def running_mass(values_of, live_slots, reduced, slot_blocks, tops):

    def advance(position, masses):
        target = slot_blocks[position]
        top_here = lax.dynamic_index_in_dim(tops, target, 0, keepdims=False)
        local_mass = jnp.sum(
            jnp.exp(values_of(position) - jnp.expand_dims(top_here, reduced)), axis=reduced
        )
        old_mass = lax.dynamic_index_in_dim(masses, target, 0, keepdims=False)
        return lax.dynamic_update_index_in_dim(masses, old_mass + local_mass, target, 0)

    return lax.fori_loop(0, live_slots, advance, jnp.zeros_like(tops))


def gather_kernel(axis, x_ref, out_ref, landed, send_sems, recv_sems):
    count = lax.axis_size(axis)
    me = lax.axis_index(axis)

    def peer_copy(peer, slot):
        return pltpu.make_async_remote_copy(
            src_ref=x_ref,
            dst_ref=landed.at[slot],
            send_sem=send_sems.at[slot],
            recv_sem=recv_sems.at[slot],
            device_id={axis: peer},
            device_id_type=pl.DeviceIdType.MESH,
        )

    landed[me] = x_ref[...]

    def send(step, carry):
        peer = lax.rem(me + step, count)
        peer_copy(peer, me).start()
        return carry

    lax.fori_loop(1, count, send, 0)

    def receive(step, carry):
        peer = lax.rem(me + count - step, count)
        peer_copy(peer, peer).wait_recv()
        return carry

    lax.fori_loop(1, count, receive, 0)

    def drain(step, carry):
        peer = lax.rem(me + step, count)
        peer_copy(peer, me).wait_send()
        return carry

    lax.fori_loop(1, count, drain, 0)
    out_ref[...] = landed[...]


def gather_peers(block, axis):
    count = lax.axis_size(axis)
    shape = (count,) + block.shape
    return pl.pallas_call(
        functools.partial(gather_kernel, axis),
        out_shape=jax.ShapeDtypeStruct(shape, block.dtype),
        in_specs=[pl.BlockSpec(memory_space=pltpu.VMEM)],
        out_specs=pl.BlockSpec(memory_space=pltpu.VMEM),
        scratch_shapes=[
            pltpu.VMEM(shape, block.dtype),
            pltpu.SemaphoreType.DMA((count,)),
            pltpu.SemaphoreType.DMA((count,)),
        ],
        compiler_params=pltpu.CompilerParams(has_side_effects=True),
    )(block)


def merge_tops(local_top, local_mass, axis):
    gathered = gather_peers(jnp.stack([local_top, local_mass]), axis)
    tops, masses = gathered[:, 0], gathered[:, 1]
    highest = jnp.max(tops, axis=0)
    summed = jnp.sum(masses * jnp.exp(tops - highest[None]), axis=0)
    return highest, summed


def slot_specs():
    return [pl.BlockSpec(memory_space=pltpu.SMEM)] * 3


def whole_specs(count):
    return [pl.BlockSpec(memory_space=pltpu.VMEM)] * count


def pass_kernel(along_rows, rows_ref, protos_ref, valid_ref, images_ref, prototypes_ref,
                other_ref, top_ref, mass_ref):
    top_ref[...] = jnp.full(top_ref.shape, far_below, jnp.float32)
    mass_ref[...] = jnp.zeros(mass_ref.shape, jnp.float32)
    score_scale = float(E) ** (-0.5)
    for position in range(MAXT):

        @pl.when(valid_ref[position] == 1)
        def _():
            row_block = rows_ref[position]
            proto_block = protos_ref[position]
            rows_here = images_ref[pl.ds(pl.multiple_of(row_block * TILE, TILE), TILE), :]
            protos_here = prototypes_ref[pl.ds(pl.multiple_of(proto_block * TILE, TILE), TILE), :]
            if along_rows:
                first, second, other_block, target = protos_here, rows_here, proto_block, row_block
            else:
                first, second, other_block, target = rows_here, protos_here, row_block, proto_block
            products = lax.dot_general(
                first, second, (((1,), (1,)), ((), ())), preferred_element_type=jnp.float32
            )
            values = products * score_scale + other_ref[other_block]
            local_top = jnp.max(values, axis=0, keepdims=True)
            old_top = top_ref[target]
            new_top = jnp.maximum(old_top, local_top)
            local_mass = jnp.sum(jnp.exp(values - new_top), axis=0, keepdims=True)
            mass_ref[target] = mass_ref[target] * jnp.exp(old_top - new_top) + local_mass
            top_ref[target] = new_top


def local_pass(along_rows, slots, images, prototypes, other_column):
    blocks = RB_DEV if along_rows else PB_DEV
    shape = jax.ShapeDtypeStruct((blocks, 1, TILE), jnp.float32)
    return pl.pallas_call(
        functools.partial(pass_kernel, along_rows),
        out_shape=(shape, shape),
        in_specs=slot_specs() + whole_specs(3),
        out_specs=tuple(whole_specs(2)),
    )(*slots, images, prototypes, other_column)


def final_kernel(rows_ref, protos_ref, valid_ref, images_ref, prototypes_ref,
                 col_ref, row_ref, out_ref):
    out_ref[...] = jnp.zeros(out_ref.shape, jnp.float32)
    score_scale = float(E) ** (-0.5)
    for position in range(MAXT):

        @pl.when(valid_ref[position] == 1)
        def _():
            row_block = rows_ref[position]
            proto_block = protos_ref[position]
            rows_here = images_ref[pl.ds(pl.multiple_of(row_block * TILE, TILE), TILE), :]
            protos_here = prototypes_ref[pl.ds(pl.multiple_of(proto_block * TILE, TILE), TILE), :]
            products = lax.dot_general(
                protos_here, rows_here, (((1,), (1,)), ((), ())), preferred_element_type=jnp.float32
            )
            weights = jnp.exp(
                products * score_scale + col_ref[proto_block] + row_ref[row_block]
            ).astype(jnp.bfloat16)
            out_ref[proto_block] += jnp.dot(weights, rows_here, preferred_element_type=jnp.float32)


def final_pass(slots, images, prototypes, col_column, row_pot):
    return pl.pallas_call(
        final_kernel,
        out_shape=jax.ShapeDtypeStruct((PB_DEV, TILE, E), jnp.float32),
        in_specs=slot_specs() + whole_specs(4),
        out_specs=pl.BlockSpec(memory_space=pltpu.VMEM),
    )(*slots, images, prototypes, col_column, row_pot.reshape(RB_DEV, 1, TILE))


def to_column(lanes):
    padded = jnp.concatenate(
        [lanes, jnp.zeros((8 - lanes.shape[0], TILE), jnp.float32)], axis=0
    ) if lanes.shape[0] < 8 else lanes
    return jnp.transpose(padded)


def stage_peer(axis, size, stride, step):
    me = lax.axis_index(axis)
    place = lax.rem(me // stride, size)
    return me + (lax.rem(place + step, size) - place) * stride, place


def exchange_stage(axis, size, stride, stage, local, packed, landed, send_sems, recv_sems):
    place = stage_peer(axis, size, stride, 0)[1]
    packed[...] = local
    landed[stage, place] = local

    def peer_copy(step, slot):
        return pltpu.make_async_remote_copy(
            src_ref=packed,
            dst_ref=landed.at[stage, slot],
            send_sem=send_sems.at[stage, lax.rem(place + step, size)],
            recv_sem=recv_sems.at[stage, slot],
            device_id={axis: stage_peer(axis, size, stride, step)[0]},
            device_id_type=pl.DeviceIdType.MESH,
        )

    def send(step, carry):
        peer_copy(step, place).start()
        return carry

    lax.fori_loop(1, size, send, 0)

    def receive(step, carry):
        peer_copy(size - step, lax.rem(place + size - step, size)).wait_recv()
        return carry

    lax.fori_loop(1, size, receive, 0)

    def drain(step, carry):
        peer_copy(step, place).wait_send()
        return carry

    lax.fori_loop(1, size, drain, 0)
    gathered = landed[stage]
    highest = jnp.max(gathered, axis=0)
    return highest + jnp.log(jnp.sum(jnp.exp(gathered - highest[None]), axis=0))


def exchange(axis, groups, stage, local, packed, landed_refs, send_refs, recv_refs):
    for (size, stride), landed, send_sems, recv_sems in zip(groups, landed_refs, send_refs,
                                                           recv_refs):
        local = exchange_stage(axis, size, stride, stage, local, packed, landed, send_sems,
                               recv_sems)
    return local


def pick_column(columns, chosen_block, blocks):
    picked = columns[:, 0:1]
    for block in range(1, blocks):
        picked = jnp.where(chosen_block == block, columns[:, block:block + 1], picked)
    return picked


def local_merge(along_rows, rows_ref, protos_ref, valid_ref, slot_images_ref, slot_protos_ref,
                other_columns):
    blocks = RB_DEV if along_rows else PB_DEV
    other_blocks = PB_DEV if along_rows else RB_DEV
    tops = [jnp.full((1, TILE), far_below, jnp.float32) for _ in range(blocks)]
    masses = [jnp.zeros((1, TILE), jnp.float32) for _ in range(blocks)]
    score_scale = float(E) ** (-0.5)
    for position in range(MAXT):
        row_block = rows_ref[position]
        proto_block = protos_ref[position]
        live = valid_ref[position] == 1
        rows_here = slot_images_ref[position]
        protos_here = slot_protos_ref[position]
        if along_rows:
            first, second, other_block, target = protos_here, rows_here, proto_block, row_block
        else:
            first, second, other_block, target = rows_here, protos_here, row_block, proto_block
        products = lax.dot_general(
            first, second, (((1,), (1,)), ((), ())), preferred_element_type=jnp.float32
        )
        values = products * score_scale + pick_column(other_columns, other_block, other_blocks)
        local_top = jnp.max(values, axis=0, keepdims=True)
        local_mass = jnp.sum(jnp.exp(values - local_top), axis=0, keepdims=True)
        for block in range(blocks):
            chosen = jnp.logical_and(live, target == block)
            new_top = jnp.maximum(tops[block], local_top)
            new_mass = masses[block] * jnp.exp(tops[block] - new_top) + local_mass * jnp.exp(
                local_top - new_top
            )
            tops[block] = jnp.where(chosen, new_top, tops[block])
            masses[block] = jnp.where(chosen, new_mass, masses[block])
    return jnp.maximum(
        jnp.concatenate(tops, axis=0) + jnp.log(jnp.concatenate(masses, axis=0)), far_below
    )


def axis_groups():
    proto_count = lax.axis_size("proto")
    img_count = lax.axis_size("img")
    return {
        "proto": ((PB_DEV, 1), (proto_count // PB_DEV, PB_DEV)),
        "img": ((2, 1), (img_count // 2, 2)),
    }


def sinkhorn_kernel(log_ratio, rows_ref, protos_ref, valid_ref, images_ref, prototypes_ref,
                    row_out, col_out, col_columns_out, row_packed, col_packed, *stage_refs):
    groups = axis_groups()
    row_refs = stage_refs[0:6]
    col_refs = stage_refs[6:12]
    barrier = pltpu.get_barrier_semaphore()
    greeted = 0
    for axis in ("proto", "img"):
        for size, stride in groups[axis]:

            def greet(step, carry):
                peer = stage_peer(axis, size, stride, step)[0]
                pl.semaphore_signal(barrier, inc=1, device_id={axis: peer},
                                    device_id_type=pl.DeviceIdType.MESH)
                return carry

            lax.fori_loop(1, size, greet, 0)
            greeted += size - 1
    pl.semaphore_wait(barrier, greeted)

    col_t = jnp.zeros((TILE, PB_DEV), jnp.float32)
    for iteration in range(ITERS):
        local = local_merge(True, rows_ref, protos_ref, valid_ref, images_ref, prototypes_ref,
                            col_t)
        merged = exchange("proto", groups["proto"], iteration, local, row_packed,
                          row_refs[0:2], row_refs[2:4], row_refs[4:6])
        row_pot = log_ratio - merged
        row_t = to_column(row_pot)
        local = local_merge(False, rows_ref, protos_ref, valid_ref, images_ref, prototypes_ref,
                            row_t)
        merged = exchange("img", groups["img"], iteration, local, col_packed,
                          col_refs[0:2], col_refs[2:4], col_refs[4:6])
        col_pot = -merged
        col_t = to_column(col_pot)
    row_out[...] = row_pot
    col_out[...] = col_pot
    for block in range(PB_DEV):
        col_columns_out[block] = col_t[:, block:block + 1]


def sinkhorn(slots, slot_images, slot_protos, log_ratio):
    groups = axis_groups()
    vmem = pltpu.VMEM
    stage_scratch = []
    for axis, blocks in (("proto", RB_DEV), ("img", PB_DEV)):
        sizes = [size for size, _ in groups[axis]]
        stage_scratch += [vmem((ITERS, size, blocks, TILE), jnp.float32) for size in sizes]
        stage_scratch += [pltpu.SemaphoreType.DMA((ITERS, size)) for size in sizes]
        stage_scratch += [pltpu.SemaphoreType.DMA((ITERS, size)) for size in sizes]
    return pl.pallas_call(
        functools.partial(sinkhorn_kernel, log_ratio),
        out_shape=(
            jax.ShapeDtypeStruct((RB_DEV, TILE), jnp.float32),
            jax.ShapeDtypeStruct((PB_DEV, TILE), jnp.float32),
            jax.ShapeDtypeStruct((PB_DEV, TILE, 1), jnp.float32),
        ),
        in_specs=slot_specs() + whole_specs(2),
        out_specs=tuple(whole_specs(3)),
        scratch_shapes=[
            vmem((RB_DEV, TILE), jnp.float32),
            vmem((PB_DEV, TILE), jnp.float32),
        ] + stage_scratch,
        compiler_params=pltpu.CompilerParams(collective_id=0, has_side_effects=True),
    )(*slots, slot_images, slot_protos)


def scatter_kernel(shares_ref, out_ref, paired, pair_sums, landed, pair_sems, send_sems,
                   recv_sems):
    count = lax.axis_size("img")
    chips = count // 2
    me = lax.axis_index("img")
    core = lax.rem(me, 2)
    chip = me // 2
    partner = me + 1 - 2 * core
    barrier = pltpu.get_barrier_semaphore()
    pl.semaphore_signal(barrier, inc=1, device_id={"img": partner},
                        device_id_type=pl.DeviceIdType.MESH)

    def greet(step, carry):
        peer = lax.rem(chip + step, chips) * 2 + core
        pl.semaphore_signal(barrier, inc=1, device_id={"img": peer},
                            device_id_type=pl.DeviceIdType.MESH)
        return carry

    lax.fori_loop(1, chips, greet, 0)
    pl.semaphore_wait(barrier, chips)

    pair_copy = pltpu.make_async_remote_copy(
        src_ref=shares_ref.at[1 - core],
        dst_ref=paired,
        send_sem=pair_sems.at[0],
        recv_sem=pair_sems.at[1],
        device_id={"img": partner},
        device_id_type=pl.DeviceIdType.MESH,
    )
    pair_copy.start()
    pair_copy.wait_recv()
    pair_sums[...] = (
        shares_ref[core].astype(jnp.float32) + paired[...].astype(jnp.float32)
    ).astype(jnp.bfloat16)
    pair_copy.wait_send()

    def peer_copy(peer_chip, slot):
        return pltpu.make_async_remote_copy(
            src_ref=pair_sums.at[peer_chip],
            dst_ref=landed.at[slot],
            send_sem=send_sems.at[peer_chip],
            recv_sem=recv_sems.at[slot],
            device_id={"img": peer_chip * 2 + core},
            device_id_type=pl.DeviceIdType.MESH,
        )

    def send(step, carry):
        peer_copy(lax.rem(chip + step, chips), chip).start()
        return carry

    lax.fori_loop(1, chips, send, 0)
    out_ref[...] = pair_sums[chip].astype(jnp.float32)

    def receive(step, carry):
        source = lax.rem(chip + chips - step, chips)
        peer_copy(source, source).wait_recv()
        out_ref[...] += landed[source].astype(jnp.float32)
        return carry

    lax.fori_loop(1, chips, receive, 0)

    def drain(step, carry):
        peer_copy(lax.rem(chip + step, chips), chip).wait_send()
        return carry

    lax.fori_loop(1, chips, drain, 0)


def scatter_sum(shares):
    cores, chips, rows, width = shares.shape
    half = (chips, rows, width)
    return pl.pallas_call(
        scatter_kernel,
        out_shape=jax.ShapeDtypeStruct((rows, width), jnp.float32),
        in_specs=whole_specs(1),
        out_specs=pl.BlockSpec(memory_space=pltpu.VMEM),
        scratch_shapes=[
            pltpu.VMEM(half, shares.dtype),
            pltpu.VMEM(half, shares.dtype),
            pltpu.VMEM(half, shares.dtype),
            pltpu.SemaphoreType.DMA((2,)),
            pltpu.SemaphoreType.DMA((chips,)),
            pltpu.SemaphoreType.DMA((chips,)),
        ],
        compiler_params=pltpu.CompilerParams(collective_id=1, has_side_effects=True),
    )(shares)


def shards(images, prototypes, tile_row, tile_proto, tile_valid):
    img_count = lax.axis_size("img")
    proto_count = lax.axis_size("proto")
    slots = (tile_row.reshape(MAXT), tile_proto.reshape(MAXT), tile_valid.reshape(MAXT))
    log_ratio = math.log(PB_DEV * proto_count / (RB_DEV * img_count))
    slot_images = images.reshape(RB_DEV, TILE, E)[slots[0]]
    slot_protos = prototypes.reshape(PB_DEV, TILE, E)[slots[1]]
    row_pot, col_pot, col_columns = sinkhorn(slots, slot_images, slot_protos, log_ratio)
    partial_value = final_pass(slots, images, prototypes, col_columns, row_pot)
    img_count = lax.axis_size("img")
    by_core = partial_value.reshape(img_count // 2, 2, PB_DEV * TILE // img_count, E)
    proto_share = scatter_sum(jnp.swapaxes(by_core, 0, 1).astype(jnp.bfloat16))
    return (proto_share, col_pot.reshape(PB_DEV * TILE))


def solution(mesh):
    return jax.shard_map(
        shards,
        mesh=mesh,
        in_specs=(
            P("img", None),
            P("proto", None),
            P("img", "proto", None),
            P("img", "proto", None),
            P("img", "proto", None),
        ),
        out_specs=(P(("proto", "img"), None), P("proto")),
        check_vma=False,
    )
```

```python
import functools
import math

import jax
import jax.numpy as jnp
from jax import lax
from jax.experimental import pallas as pl
from jax.experimental.pallas import tpu as pltpu
from jax.sharding import PartitionSpec as P

E = 256
TILE = 512
RB_DEV = 4
PB_DEV = 8
MAXT = 6
ITERS = 3


far_below = -1e30


def running_top(values_of, live_slots, reduced, slot_blocks, block_count):

    def advance(position, tops):
        local_top = jnp.max(values_of(position), axis=reduced)
        target = slot_blocks[position]
        old_top = lax.dynamic_index_in_dim(tops, target, 0, keepdims=False)
        return lax.dynamic_update_index_in_dim(tops, jnp.maximum(old_top, local_top), target, 0)

    return lax.fori_loop(
        0, live_slots, advance, jnp.full((block_count, TILE), far_below, jnp.float32)
    )


def running_mass(values_of, live_slots, reduced, slot_blocks, tops):

    def advance(position, masses):
        target = slot_blocks[position]
        top_here = lax.dynamic_index_in_dim(tops, target, 0, keepdims=False)
        local_mass = jnp.sum(
            jnp.exp(values_of(position) - jnp.expand_dims(top_here, reduced)), axis=reduced
        )
        old_mass = lax.dynamic_index_in_dim(masses, target, 0, keepdims=False)
        return lax.dynamic_update_index_in_dim(masses, old_mass + local_mass, target, 0)

    return lax.fori_loop(0, live_slots, advance, jnp.zeros_like(tops))


def gather_kernel(axis, x_ref, out_ref, landed, send_sems, recv_sems):
    count = lax.axis_size(axis)
    me = lax.axis_index(axis)

    def peer_copy(peer, slot):
        return pltpu.make_async_remote_copy(
            src_ref=x_ref,
            dst_ref=landed.at[slot],
            send_sem=send_sems.at[slot],
            recv_sem=recv_sems.at[slot],
            device_id={axis: peer},
            device_id_type=pl.DeviceIdType.MESH,
        )

    landed[me] = x_ref[...]

    def send(step, carry):
        peer = lax.rem(me + step, count)
        peer_copy(peer, me).start()
        return carry

    lax.fori_loop(1, count, send, 0)

    def receive(step, carry):
        peer = lax.rem(me + count - step, count)
        peer_copy(peer, peer).wait_recv()
        return carry

    lax.fori_loop(1, count, receive, 0)

    def drain(step, carry):
        peer = lax.rem(me + step, count)
        peer_copy(peer, me).wait_send()
        return carry

    lax.fori_loop(1, count, drain, 0)
    out_ref[...] = landed[...]


def gather_peers(block, axis):
    count = lax.axis_size(axis)
    shape = (count,) + block.shape
    return pl.pallas_call(
        functools.partial(gather_kernel, axis),
        out_shape=jax.ShapeDtypeStruct(shape, block.dtype),
        in_specs=[pl.BlockSpec(memory_space=pltpu.VMEM)],
        out_specs=pl.BlockSpec(memory_space=pltpu.VMEM),
        scratch_shapes=[
            pltpu.VMEM(shape, block.dtype),
            pltpu.SemaphoreType.DMA((count,)),
            pltpu.SemaphoreType.DMA((count,)),
        ],
        compiler_params=pltpu.CompilerParams(has_side_effects=True),
    )(block)


def merge_tops(local_top, local_mass, axis):
    gathered = gather_peers(jnp.stack([local_top, local_mass]), axis)
    tops, masses = gathered[:, 0], gathered[:, 1]
    highest = jnp.max(tops, axis=0)
    summed = jnp.sum(masses * jnp.exp(tops - highest[None]), axis=0)
    return highest, summed


def slot_specs():
    return [pl.BlockSpec(memory_space=pltpu.SMEM)] * 3


def whole_specs(count):
    return [pl.BlockSpec(memory_space=pltpu.VMEM)] * count


def pass_kernel(along_rows, rows_ref, protos_ref, valid_ref, images_ref, prototypes_ref,
                other_ref, top_ref, mass_ref):
    top_ref[...] = jnp.full(top_ref.shape, far_below, jnp.float32)
    mass_ref[...] = jnp.zeros(mass_ref.shape, jnp.float32)
    score_scale = float(E) ** (-0.5)
    for position in range(MAXT):

        @pl.when(valid_ref[position] == 1)
        def _():
            row_block = rows_ref[position]
            proto_block = protos_ref[position]
            rows_here = images_ref[pl.ds(pl.multiple_of(row_block * TILE, TILE), TILE), :]
            protos_here = prototypes_ref[pl.ds(pl.multiple_of(proto_block * TILE, TILE), TILE), :]
            if along_rows:
                first, second, other_block, target = protos_here, rows_here, proto_block, row_block
            else:
                first, second, other_block, target = rows_here, protos_here, row_block, proto_block
            products = lax.dot_general(
                first, second, (((1,), (1,)), ((), ())), preferred_element_type=jnp.float32
            )
            values = products * score_scale + other_ref[other_block]
            local_top = jnp.max(values, axis=0, keepdims=True)
            old_top = top_ref[target]
            new_top = jnp.maximum(old_top, local_top)
            local_mass = jnp.sum(jnp.exp(values - new_top), axis=0, keepdims=True)
            mass_ref[target] = mass_ref[target] * jnp.exp(old_top - new_top) + local_mass
            top_ref[target] = new_top


def local_pass(along_rows, slots, images, prototypes, other_column):
    blocks = RB_DEV if along_rows else PB_DEV
    shape = jax.ShapeDtypeStruct((blocks, 1, TILE), jnp.float32)
    return pl.pallas_call(
        functools.partial(pass_kernel, along_rows),
        out_shape=(shape, shape),
        in_specs=slot_specs() + whole_specs(3),
        out_specs=tuple(whole_specs(2)),
    )(*slots, images, prototypes, other_column)


def final_kernel(rows_ref, protos_ref, valid_ref, images_ref, prototypes_ref,
                 col_ref, row_ref, shares_ref, acc_ref):
    acc_ref[...] = jnp.zeros(acc_ref.shape, jnp.float32)
    score_scale = float(E) ** (-0.5)
    for position in range(MAXT):

        @pl.when(valid_ref[position] == 1)
        def _():
            row_block = rows_ref[position]
            proto_block = protos_ref[position]
            rows_here = images_ref[pl.ds(pl.multiple_of(row_block * TILE, TILE), TILE), :]
            protos_here = prototypes_ref[pl.ds(pl.multiple_of(proto_block * TILE, TILE), TILE), :]
            products = lax.dot_general(
                protos_here, rows_here, (((1,), (1,)), ((), ())), preferred_element_type=jnp.float32
            )
            weights = jnp.exp(
                products * score_scale + col_ref[proto_block] + row_ref[row_block]
            ).astype(jnp.bfloat16)
            acc_ref[proto_block] += jnp.dot(weights, rows_here, preferred_element_type=jnp.float32)

    half = TILE // 2
    for block in range(PB_DEV):
        for core in range(2):
            shares_ref[core, block] = acc_ref[block, core * half:(core + 1) * half, :].astype(
                jnp.bfloat16
            )


def final_pass(slots, images, prototypes, col_column, row_pot):
    return pl.pallas_call(
        final_kernel,
        out_shape=jax.ShapeDtypeStruct((2, PB_DEV, TILE // 2, E), jnp.bfloat16),
        in_specs=slot_specs() + whole_specs(4),
        out_specs=pl.BlockSpec(memory_space=pltpu.VMEM),
        scratch_shapes=[pltpu.VMEM((PB_DEV, TILE, E), jnp.float32)],
    )(*slots, images, prototypes, col_column, row_pot)


def to_column(lanes):
    padded = jnp.concatenate(
        [lanes, jnp.zeros((8 - lanes.shape[0], TILE), jnp.float32)], axis=0
    ) if lanes.shape[0] < 8 else lanes
    return jnp.transpose(padded)


def stage_peer(axis, size, stride, step):
    me = lax.axis_index(axis)
    place = lax.rem(me // stride, size)
    return me + (lax.rem(place + step, size) - place) * stride, place


def exchange_stage(axis, size, stride, stage, local, packed, landed, send_sems, recv_sems):
    place = stage_peer(axis, size, stride, 0)[1]
    packed[...] = local
    landed[stage, place] = local

    def peer_copy(step, slot):
        return pltpu.make_async_remote_copy(
            src_ref=packed,
            dst_ref=landed.at[stage, slot],
            send_sem=send_sems.at[stage, lax.rem(place + step, size)],
            recv_sem=recv_sems.at[stage, slot],
            device_id={axis: stage_peer(axis, size, stride, step)[0]},
            device_id_type=pl.DeviceIdType.MESH,
        )

    def send(step, carry):
        peer_copy(step, place).start()
        return carry

    lax.fori_loop(1, size, send, 0)

    def receive(step, carry):
        peer_copy(size - step, lax.rem(place + size - step, size)).wait_recv()
        return carry

    lax.fori_loop(1, size, receive, 0)

    def drain(step, carry):
        peer_copy(step, place).wait_send()
        return carry

    lax.fori_loop(1, size, drain, 0)
    gathered = landed[stage]
    highest = jnp.max(gathered, axis=0)
    return highest + jnp.log(jnp.sum(jnp.exp(gathered - highest[None]), axis=0))


def exchange(axis, groups, stage, local, packed, landed_refs, send_refs, recv_refs):
    for (size, stride), landed, send_sems, recv_sems in zip(groups, landed_refs, send_refs,
                                                           recv_refs):
        local = exchange_stage(axis, size, stride, stage, local, packed, landed, send_sems,
                               recv_sems)
    return local


def pick_column(columns, chosen_block, blocks):
    picked = columns[:, 0:1]
    for block in range(1, blocks):
        picked = jnp.where(chosen_block == block, columns[:, block:block + 1], picked)
    return picked


def local_merge(along_rows, rows_ref, protos_ref, valid_ref, slot_images_ref, slot_protos_ref,
                other_columns):
    blocks = RB_DEV if along_rows else PB_DEV
    other_blocks = PB_DEV if along_rows else RB_DEV
    tops = [jnp.full((1, TILE), far_below, jnp.float32) for _ in range(blocks)]
    masses = [jnp.zeros((1, TILE), jnp.float32) for _ in range(blocks)]
    score_scale = float(E) ** (-0.5)
    for position in range(MAXT):
        row_block = rows_ref[position]
        proto_block = protos_ref[position]
        live = valid_ref[position] == 1
        rows_here = slot_images_ref[position]
        protos_here = slot_protos_ref[position]
        if along_rows:
            first, second, other_block, target = protos_here, rows_here, proto_block, row_block
        else:
            first, second, other_block, target = rows_here, protos_here, row_block, proto_block
        products = lax.dot_general(
            first, second, (((1,), (1,)), ((), ())), preferred_element_type=jnp.float32
        )
        values = products * score_scale + pick_column(other_columns, other_block, other_blocks)
        local_top = jnp.max(values, axis=0, keepdims=True)
        local_mass = jnp.sum(jnp.exp(values - local_top), axis=0, keepdims=True)
        for block in range(blocks):
            chosen = jnp.logical_and(live, target == block)
            new_top = jnp.maximum(tops[block], local_top)
            new_mass = masses[block] * jnp.exp(tops[block] - new_top) + local_mass * jnp.exp(
                local_top - new_top
            )
            tops[block] = jnp.where(chosen, new_top, tops[block])
            masses[block] = jnp.where(chosen, new_mass, masses[block])
    return jnp.maximum(
        jnp.concatenate(tops, axis=0) + jnp.log(jnp.concatenate(masses, axis=0)), far_below
    )


def axis_groups():
    proto_count = lax.axis_size("proto")
    img_count = lax.axis_size("img")
    return {
        "proto": ((PB_DEV, 1), (proto_count // PB_DEV, PB_DEV)),
        "img": ((2, 1), (img_count // 2, 2)),
    }


def sinkhorn_kernel(log_ratio, rows_ref, protos_ref, valid_ref, images_ref, prototypes_ref,
                    row_out, col_out, col_columns_out, row_packed, col_packed, *stage_refs):
    groups = axis_groups()
    row_refs = stage_refs[0:6]
    col_refs = stage_refs[6:12]
    barrier = pltpu.get_barrier_semaphore()
    greeted = 0
    for axis in ("proto", "img"):
        for size, stride in groups[axis]:

            def greet(step, carry):
                peer = stage_peer(axis, size, stride, step)[0]
                pl.semaphore_signal(barrier, inc=1, device_id={axis: peer},
                                    device_id_type=pl.DeviceIdType.MESH)
                return carry

            lax.fori_loop(1, size, greet, 0)
            greeted += size - 1
    pl.semaphore_wait(barrier, greeted)

    col_t = jnp.zeros((TILE, PB_DEV), jnp.float32)
    for iteration in range(ITERS):
        local = local_merge(True, rows_ref, protos_ref, valid_ref, images_ref, prototypes_ref,
                            col_t)
        merged = exchange("proto", groups["proto"], iteration, local, row_packed,
                          row_refs[0:2], row_refs[2:4], row_refs[4:6])
        row_pot = log_ratio - merged
        row_t = to_column(row_pot)
        local = local_merge(False, rows_ref, protos_ref, valid_ref, images_ref, prototypes_ref,
                            row_t)
        merged = exchange("img", groups["img"], iteration, local, col_packed,
                          col_refs[0:2], col_refs[2:4], col_refs[4:6])
        col_pot = -merged
        col_t = to_column(col_pot)
    for block in range(RB_DEV):
        row_out[block] = row_pot[block:block + 1]
    col_out[...] = col_pot
    for block in range(PB_DEV):
        col_columns_out[block] = col_t[:, block:block + 1]


def sinkhorn(slots, slot_images, slot_protos, log_ratio):
    groups = axis_groups()
    vmem = pltpu.VMEM
    stage_scratch = []
    for axis, blocks in (("proto", RB_DEV), ("img", PB_DEV)):
        sizes = [size for size, _ in groups[axis]]
        stage_scratch += [vmem((ITERS, size, blocks, TILE), jnp.float32) for size in sizes]
        stage_scratch += [pltpu.SemaphoreType.DMA((ITERS, size)) for size in sizes]
        stage_scratch += [pltpu.SemaphoreType.DMA((ITERS, size)) for size in sizes]
    return pl.pallas_call(
        functools.partial(sinkhorn_kernel, log_ratio),
        out_shape=(
            jax.ShapeDtypeStruct((RB_DEV, 1, TILE), jnp.float32),
            jax.ShapeDtypeStruct((PB_DEV, TILE), jnp.float32),
            jax.ShapeDtypeStruct((PB_DEV, TILE, 1), jnp.float32),
        ),
        in_specs=slot_specs() + whole_specs(2),
        out_specs=tuple(whole_specs(3)),
        scratch_shapes=[
            vmem((RB_DEV, TILE), jnp.float32),
            vmem((PB_DEV, TILE), jnp.float32),
        ] + stage_scratch,
        compiler_params=pltpu.CompilerParams(collective_id=0, has_side_effects=True),
    )(*slots, slot_images, slot_protos)


def scatter_kernel(shares_ref, out_ref, paired, pair_sums, landed, pair_sems, send_sems,
                   recv_sems):
    count = lax.axis_size("img")
    chips = count // 2
    me = lax.axis_index("img")
    core = lax.rem(me, 2)
    chip = me // 2
    partner = me + 1 - 2 * core
    barrier = pltpu.get_barrier_semaphore()
    pl.semaphore_signal(barrier, inc=1, device_id={"img": partner},
                        device_id_type=pl.DeviceIdType.MESH)

    def greet(step, carry):
        peer = lax.rem(chip + step, chips) * 2 + core
        pl.semaphore_signal(barrier, inc=1, device_id={"img": peer},
                            device_id_type=pl.DeviceIdType.MESH)
        return carry

    lax.fori_loop(1, chips, greet, 0)
    pl.semaphore_wait(barrier, chips)

    pair_copy = pltpu.make_async_remote_copy(
        src_ref=shares_ref.at[1 - core],
        dst_ref=paired,
        send_sem=pair_sems.at[0],
        recv_sem=pair_sems.at[1],
        device_id={"img": partner},
        device_id_type=pl.DeviceIdType.MESH,
    )
    pair_copy.start()
    pair_copy.wait_recv()
    pair_sums[...] = (
        shares_ref[core].astype(jnp.float32) + paired[...].astype(jnp.float32)
    ).astype(jnp.bfloat16)
    pair_copy.wait_send()

    def peer_copy(peer_chip, slot):
        return pltpu.make_async_remote_copy(
            src_ref=pair_sums.at[peer_chip],
            dst_ref=landed.at[slot],
            send_sem=send_sems.at[peer_chip],
            recv_sem=recv_sems.at[slot],
            device_id={"img": peer_chip * 2 + core},
            device_id_type=pl.DeviceIdType.MESH,
        )

    def send(step, carry):
        peer_copy(lax.rem(chip + step, chips), chip).start()
        return carry

    lax.fori_loop(1, chips, send, 0)
    out_ref[...] = pair_sums[chip].astype(jnp.float32)

    def receive(step, carry):
        source = lax.rem(chip + chips - step, chips)
        peer_copy(source, source).wait_recv()
        out_ref[...] += landed[source].astype(jnp.float32)
        return carry

    lax.fori_loop(1, chips, receive, 0)

    def drain(step, carry):
        peer_copy(lax.rem(chip + step, chips), chip).wait_send()
        return carry

    lax.fori_loop(1, chips, drain, 0)


def scatter_sum(shares):
    cores, chips, rows, width = shares.shape
    half = (chips, rows, width)
    return pl.pallas_call(
        scatter_kernel,
        out_shape=jax.ShapeDtypeStruct((rows, width), jnp.float32),
        in_specs=whole_specs(1),
        out_specs=pl.BlockSpec(memory_space=pltpu.VMEM),
        scratch_shapes=[
            pltpu.VMEM(half, shares.dtype),
            pltpu.VMEM(half, shares.dtype),
            pltpu.VMEM(half, shares.dtype),
            pltpu.SemaphoreType.DMA((2,)),
            pltpu.SemaphoreType.DMA((chips,)),
            pltpu.SemaphoreType.DMA((chips,)),
        ],
        compiler_params=pltpu.CompilerParams(collective_id=1, has_side_effects=True),
    )(shares)


def shards(images, prototypes, tile_row, tile_proto, tile_valid):
    img_count = lax.axis_size("img")
    proto_count = lax.axis_size("proto")
    slots = (tile_row.reshape(MAXT), tile_proto.reshape(MAXT), tile_valid.reshape(MAXT))
    log_ratio = math.log(PB_DEV * proto_count / (RB_DEV * img_count))
    slot_images = images.reshape(RB_DEV, TILE, E)[slots[0]]
    slot_protos = prototypes.reshape(PB_DEV, TILE, E)[slots[1]]
    row_pot, col_pot, col_columns = sinkhorn(slots, slot_images, slot_protos, log_ratio)
    partial_value = final_pass(slots, images, prototypes, col_columns, row_pot)
    proto_share = scatter_sum(partial_value)
    return (proto_share, col_pot.reshape(PB_DEV * TILE))


def solution(mesh):
    return jax.shard_map(
        shards,
        mesh=mesh,
        in_specs=(
            P("img", None),
            P("proto", None),
            P("img", "proto", None),
            P("img", "proto", None),
            P("img", "proto", None),
        ),
        out_specs=(P(("proto", "img"), None), P("proto")),
        check_vma=False,
    )
```

```python
import functools
import math

import jax
import jax.numpy as jnp
from jax import lax
from jax.experimental import pallas as pl
from jax.experimental.pallas import tpu as pltpu
from jax.sharding import PartitionSpec as P

E = 256
TILE = 512
RB_DEV = 4
PB_DEV = 8
MAXT = 6
ITERS = 3


far_below = -1e30


def running_top(values_of, live_slots, reduced, slot_blocks, block_count):

    def advance(position, tops):
        local_top = jnp.max(values_of(position), axis=reduced)
        target = slot_blocks[position]
        old_top = lax.dynamic_index_in_dim(tops, target, 0, keepdims=False)
        return lax.dynamic_update_index_in_dim(tops, jnp.maximum(old_top, local_top), target, 0)

    return lax.fori_loop(
        0, live_slots, advance, jnp.full((block_count, TILE), far_below, jnp.float32)
    )


def running_mass(values_of, live_slots, reduced, slot_blocks, tops):

    def advance(position, masses):
        target = slot_blocks[position]
        top_here = lax.dynamic_index_in_dim(tops, target, 0, keepdims=False)
        local_mass = jnp.sum(
            jnp.exp(values_of(position) - jnp.expand_dims(top_here, reduced)), axis=reduced
        )
        old_mass = lax.dynamic_index_in_dim(masses, target, 0, keepdims=False)
        return lax.dynamic_update_index_in_dim(masses, old_mass + local_mass, target, 0)

    return lax.fori_loop(0, live_slots, advance, jnp.zeros_like(tops))


def gather_kernel(axis, x_ref, out_ref, landed, send_sems, recv_sems):
    count = lax.axis_size(axis)
    me = lax.axis_index(axis)

    def peer_copy(peer, slot):
        return pltpu.make_async_remote_copy(
            src_ref=x_ref,
            dst_ref=landed.at[slot],
            send_sem=send_sems.at[slot],
            recv_sem=recv_sems.at[slot],
            device_id={axis: peer},
            device_id_type=pl.DeviceIdType.MESH,
        )

    landed[me] = x_ref[...]

    def send(step, carry):
        peer = lax.rem(me + step, count)
        peer_copy(peer, me).start()
        return carry

    lax.fori_loop(1, count, send, 0)

    def receive(step, carry):
        peer = lax.rem(me + count - step, count)
        peer_copy(peer, peer).wait_recv()
        return carry

    lax.fori_loop(1, count, receive, 0)

    def drain(step, carry):
        peer = lax.rem(me + step, count)
        peer_copy(peer, me).wait_send()
        return carry

    lax.fori_loop(1, count, drain, 0)
    out_ref[...] = landed[...]


def gather_peers(block, axis):
    count = lax.axis_size(axis)
    shape = (count,) + block.shape
    return pl.pallas_call(
        functools.partial(gather_kernel, axis),
        out_shape=jax.ShapeDtypeStruct(shape, block.dtype),
        in_specs=[pl.BlockSpec(memory_space=pltpu.VMEM)],
        out_specs=pl.BlockSpec(memory_space=pltpu.VMEM),
        scratch_shapes=[
            pltpu.VMEM(shape, block.dtype),
            pltpu.SemaphoreType.DMA((count,)),
            pltpu.SemaphoreType.DMA((count,)),
        ],
        compiler_params=pltpu.CompilerParams(has_side_effects=True),
    )(block)


def merge_tops(local_top, local_mass, axis):
    gathered = gather_peers(jnp.stack([local_top, local_mass]), axis)
    tops, masses = gathered[:, 0], gathered[:, 1]
    highest = jnp.max(tops, axis=0)
    summed = jnp.sum(masses * jnp.exp(tops - highest[None]), axis=0)
    return highest, summed


def slot_specs():
    return [pl.BlockSpec(memory_space=pltpu.SMEM)] * 3


def whole_specs(count):
    return [pl.BlockSpec(memory_space=pltpu.VMEM)] * count


def pass_kernel(along_rows, rows_ref, protos_ref, valid_ref, images_ref, prototypes_ref,
                other_ref, top_ref, mass_ref):
    top_ref[...] = jnp.full(top_ref.shape, far_below, jnp.float32)
    mass_ref[...] = jnp.zeros(mass_ref.shape, jnp.float32)
    score_scale = float(E) ** (-0.5)
    for position in range(MAXT):

        @pl.when(valid_ref[position] == 1)
        def _():
            row_block = rows_ref[position]
            proto_block = protos_ref[position]
            rows_here = images_ref[pl.ds(pl.multiple_of(row_block * TILE, TILE), TILE), :]
            protos_here = prototypes_ref[pl.ds(pl.multiple_of(proto_block * TILE, TILE), TILE), :]
            if along_rows:
                first, second, other_block, target = protos_here, rows_here, proto_block, row_block
            else:
                first, second, other_block, target = rows_here, protos_here, row_block, proto_block
            products = lax.dot_general(
                first, second, (((1,), (1,)), ((), ())), preferred_element_type=jnp.float32
            )
            values = products * score_scale + other_ref[other_block]
            local_top = jnp.max(values, axis=0, keepdims=True)
            old_top = top_ref[target]
            new_top = jnp.maximum(old_top, local_top)
            local_mass = jnp.sum(jnp.exp(values - new_top), axis=0, keepdims=True)
            mass_ref[target] = mass_ref[target] * jnp.exp(old_top - new_top) + local_mass
            top_ref[target] = new_top


def local_pass(along_rows, slots, images, prototypes, other_column):
    blocks = RB_DEV if along_rows else PB_DEV
    shape = jax.ShapeDtypeStruct((blocks, 1, TILE), jnp.float32)
    return pl.pallas_call(
        functools.partial(pass_kernel, along_rows),
        out_shape=(shape, shape),
        in_specs=slot_specs() + whole_specs(3),
        out_specs=tuple(whole_specs(2)),
    )(*slots, images, prototypes, other_column)


def final_kernel(rows_ref, protos_ref, valid_ref, images_ref, prototypes_ref,
                 col_ref, row_ref, shares_ref, acc_ref):
    acc_ref[...] = jnp.zeros(acc_ref.shape, jnp.float32)
    score_scale = float(E) ** (-0.5)
    for position in range(MAXT):

        @pl.when(valid_ref[position] == 1)
        def _():
            row_block = rows_ref[position]
            proto_block = protos_ref[position]
            rows_here = images_ref[pl.ds(pl.multiple_of(row_block * TILE, TILE), TILE), :]
            protos_here = prototypes_ref[pl.ds(pl.multiple_of(proto_block * TILE, TILE), TILE), :]
            products = lax.dot_general(
                protos_here, rows_here, (((1,), (1,)), ((), ())), preferred_element_type=jnp.float32
            )
            weights = jnp.exp(
                products * score_scale + col_ref[proto_block] + row_ref[row_block]
            ).astype(jnp.bfloat16)
            acc_ref[proto_block] += jnp.dot(weights, rows_here, preferred_element_type=jnp.float32)

    half = TILE // 2
    for block in range(PB_DEV):
        for core in range(2):
            shares_ref[core, block] = acc_ref[block, core * half:(core + 1) * half, :].astype(
                jnp.bfloat16
            )


def final_pass(slots, images, prototypes, col_column, row_pot):
    return pl.pallas_call(
        final_kernel,
        out_shape=jax.ShapeDtypeStruct((2, PB_DEV, TILE // 2, E), jnp.bfloat16),
        in_specs=slot_specs() + whole_specs(4),
        out_specs=pl.BlockSpec(memory_space=pltpu.VMEM),
        scratch_shapes=[pltpu.VMEM((PB_DEV, TILE, E), jnp.float32)],
    )(*slots, images, prototypes, col_column, row_pot)


def to_column(lanes):
    padded = jnp.concatenate(
        [lanes, jnp.zeros((8 - lanes.shape[0], TILE), jnp.float32)], axis=0
    ) if lanes.shape[0] < 8 else lanes
    return jnp.transpose(padded)


def stage_peer(axis, size, stride, step):
    me = lax.axis_index(axis)
    place = lax.rem(me // stride, size)
    return me + (lax.rem(place + step, size) - place) * stride, place


def exchange_stage(axis, size, stride, stage, local, packed, landed, send_sems, recv_sems):
    place = stage_peer(axis, size, stride, 0)[1]
    packed[...] = local
    landed[stage, place] = local

    def peer_copy(step, slot):
        return pltpu.make_async_remote_copy(
            src_ref=packed,
            dst_ref=landed.at[stage, slot],
            send_sem=send_sems.at[stage, lax.rem(place + step, size)],
            recv_sem=recv_sems.at[stage, slot],
            device_id={axis: stage_peer(axis, size, stride, step)[0]},
            device_id_type=pl.DeviceIdType.MESH,
        )

    def send(step, carry):
        peer_copy(step, place).start()
        return carry

    lax.fori_loop(1, size, send, 0)

    def receive(step, carry):
        peer_copy(size - step, lax.rem(place + size - step, size)).wait_recv()
        return carry

    lax.fori_loop(1, size, receive, 0)

    def drain(step, carry):
        peer_copy(step, place).wait_send()
        return carry

    lax.fori_loop(1, size, drain, 0)
    gathered = landed[stage]
    highest = jnp.max(gathered, axis=0)
    return highest + jnp.log(jnp.sum(jnp.exp(gathered - highest[None]), axis=0))


def exchange(axis, groups, stage, local, packed, landed_refs, send_refs, recv_refs):
    for (size, stride), landed, send_sems, recv_sems in zip(groups, landed_refs, send_refs,
                                                           recv_refs):
        local = exchange_stage(axis, size, stride, stage, local, packed, landed, send_sems,
                               recv_sems)
    return local


def pick_column(columns, chosen_block, blocks):
    picked = columns[:, 0:1]
    for block in range(1, blocks):
        picked = jnp.where(chosen_block == block, columns[:, block:block + 1], picked)
    return picked


def local_merge(along_rows, rows_ref, protos_ref, valid_ref, slot_images_ref, slot_protos_ref,
                other_columns):
    blocks = RB_DEV if along_rows else PB_DEV
    other_blocks = PB_DEV if along_rows else RB_DEV
    tops = [jnp.full((1, TILE), far_below, jnp.float32) for _ in range(blocks)]
    masses = [jnp.zeros((1, TILE), jnp.float32) for _ in range(blocks)]
    score_scale = float(E) ** (-0.5)
    for position in range(MAXT):
        row_block = rows_ref[position]
        proto_block = protos_ref[position]
        live = valid_ref[position] == 1
        rows_here = slot_images_ref[position]
        protos_here = slot_protos_ref[position]
        if along_rows:
            first, second, other_block, target = protos_here, rows_here, proto_block, row_block
        else:
            first, second, other_block, target = rows_here, protos_here, row_block, proto_block
        products = lax.dot_general(
            first, second, (((1,), (1,)), ((), ())), preferred_element_type=jnp.float32
        )
        values = products * score_scale + pick_column(other_columns, other_block, other_blocks)
        local_top = jnp.max(values, axis=0, keepdims=True)
        local_mass = jnp.sum(jnp.exp(values - local_top), axis=0, keepdims=True)
        for block in range(blocks):
            chosen = jnp.logical_and(live, target == block)
            new_top = jnp.maximum(tops[block], local_top)
            new_mass = masses[block] * jnp.exp(tops[block] - new_top) + local_mass * jnp.exp(
                local_top - new_top
            )
            tops[block] = jnp.where(chosen, new_top, tops[block])
            masses[block] = jnp.where(chosen, new_mass, masses[block])
    return jnp.maximum(
        jnp.concatenate(tops, axis=0) + jnp.log(jnp.concatenate(masses, axis=0)), far_below
    )


def axis_groups():
    proto_count = lax.axis_size("proto")
    img_count = lax.axis_size("img")
    return {
        "proto": ((PB_DEV, 1), (proto_count // PB_DEV, PB_DEV)),
        "img": ((2, 1), (img_count // 2, 2)),
    }


def sinkhorn_kernel(log_ratio, rows_ref, protos_ref, valid_ref, images_ref, prototypes_ref,
                    row_out, col_out, col_columns_out, row_packed, col_packed, *stage_refs):
    groups = axis_groups()
    row_refs = stage_refs[0:6]
    col_refs = stage_refs[6:12]
    barrier = pltpu.get_barrier_semaphore()
    greeted = 0
    for axis in ("proto", "img"):
        for size, stride in groups[axis]:

            def greet(step, carry):
                peer = stage_peer(axis, size, stride, step)[0]
                pl.semaphore_signal(barrier, inc=1, device_id={axis: peer},
                                    device_id_type=pl.DeviceIdType.MESH)
                return carry

            lax.fori_loop(1, size, greet, 0)
            greeted += size - 1
    pl.semaphore_wait(barrier, greeted)

    col_t = jnp.zeros((TILE, PB_DEV), jnp.float32)
    for iteration in range(ITERS):
        local = local_merge(True, rows_ref, protos_ref, valid_ref, images_ref, prototypes_ref,
                            col_t)
        merged = exchange("proto", groups["proto"], iteration, local, row_packed,
                          row_refs[0:2], row_refs[2:4], row_refs[4:6])
        row_pot = log_ratio - merged
        row_t = to_column(row_pot)
        local = local_merge(False, rows_ref, protos_ref, valid_ref, images_ref, prototypes_ref,
                            row_t)
        merged = exchange("img", groups["img"], iteration, local, col_packed,
                          col_refs[0:2], col_refs[2:4], col_refs[4:6])
        col_pot = -merged
        col_t = to_column(col_pot)
    for block in range(RB_DEV):
        row_out[block] = row_pot[block:block + 1]
    col_out[...] = col_pot
    for block in range(PB_DEV):
        col_columns_out[block] = col_t[:, block:block + 1]


def sinkhorn(slots, slot_images, slot_protos, log_ratio):
    groups = axis_groups()
    vmem = pltpu.VMEM
    stage_scratch = []
    for axis, blocks in (("proto", RB_DEV), ("img", PB_DEV)):
        sizes = [size for size, _ in groups[axis]]
        stage_scratch += [vmem((ITERS, size, blocks, TILE), jnp.float32) for size in sizes]
        stage_scratch += [pltpu.SemaphoreType.DMA((ITERS, size)) for size in sizes]
        stage_scratch += [pltpu.SemaphoreType.DMA((ITERS, size)) for size in sizes]
    return pl.pallas_call(
        functools.partial(sinkhorn_kernel, log_ratio),
        out_shape=(
            jax.ShapeDtypeStruct((RB_DEV, 1, TILE), jnp.float32),
            jax.ShapeDtypeStruct((PB_DEV, TILE), jnp.float32),
            jax.ShapeDtypeStruct((PB_DEV, TILE, 1), jnp.float32),
        ),
        in_specs=slot_specs() + whole_specs(2),
        out_specs=tuple(whole_specs(3)),
        scratch_shapes=[
            vmem((RB_DEV, TILE), jnp.float32),
            vmem((PB_DEV, TILE), jnp.float32),
        ] + stage_scratch,
        compiler_params=pltpu.CompilerParams(collective_id=0, has_side_effects=True),
    )(*slots, slot_images, slot_protos)


def scatter_kernel(shares_ref, out_ref, paired, pair_sums, landed, pair_sems, send_sems,
                   recv_sems):
    count = lax.axis_size("img")
    chips = count // 2
    me = lax.axis_index("img")
    core = lax.rem(me, 2)
    chip = me // 2
    partner = me + 1 - 2 * core
    barrier = pltpu.get_barrier_semaphore()
    pl.semaphore_signal(barrier, inc=1, device_id={"img": partner},
                        device_id_type=pl.DeviceIdType.MESH)

    def greet(step, carry):
        peer = lax.rem(chip + step, chips) * 2 + core
        pl.semaphore_signal(barrier, inc=1, device_id={"img": peer},
                            device_id_type=pl.DeviceIdType.MESH)
        return carry

    lax.fori_loop(1, chips, greet, 0)
    pl.semaphore_wait(barrier, chips)

    def pair_copy(piece):
        return pltpu.make_async_remote_copy(
            src_ref=shares_ref.at[1 - core, piece],
            dst_ref=paired.at[piece],
            send_sem=pair_sems.at[0, piece],
            recv_sem=pair_sems.at[1, piece],
            device_id={"img": partner},
            device_id_type=pl.DeviceIdType.MESH,
        )

    def peer_copy(peer_chip, slot):
        return pltpu.make_async_remote_copy(
            src_ref=pair_sums.at[peer_chip],
            dst_ref=landed.at[slot],
            send_sem=send_sems.at[peer_chip],
            recv_sem=recv_sems.at[slot],
            device_id={"img": peer_chip * 2 + core},
            device_id_type=pl.DeviceIdType.MESH,
        )

    def pair_send(step, carry):
        pair_copy(lax.rem(chip + step, chips)).start()
        return carry

    lax.fori_loop(1, chips + 1, pair_send, 0)

    def add_pair(piece):
        pair_copy(piece).wait_recv()
        pair_sums[piece] = (
            shares_ref[core, piece].astype(jnp.float32) + paired[piece].astype(jnp.float32)
        ).astype(jnp.bfloat16)

    def send(step, carry):
        piece = lax.rem(chip + step, chips)
        add_pair(piece)
        peer_copy(piece, chip).start()
        return carry

    lax.fori_loop(1, chips, send, 0)
    add_pair(chip)
    out_ref[...] = pair_sums[chip].astype(jnp.float32)

    def receive(step, carry):
        source = lax.rem(chip + chips - step, chips)
        peer_copy(source, source).wait_recv()
        out_ref[...] += landed[source].astype(jnp.float32)
        return carry

    lax.fori_loop(1, chips, receive, 0)

    def drain(step, carry):
        peer_copy(lax.rem(chip + step, chips), chip).wait_send()
        return carry

    lax.fori_loop(1, chips, drain, 0)

    def pair_drain(step, carry):
        pair_copy(lax.rem(chip + step, chips)).wait_send()
        return carry

    lax.fori_loop(1, chips + 1, pair_drain, 0)


def scatter_sum(shares):
    cores, chips, rows, width = shares.shape
    half = (chips, rows, width)
    return pl.pallas_call(
        scatter_kernel,
        out_shape=jax.ShapeDtypeStruct((rows, width), jnp.float32),
        in_specs=whole_specs(1),
        out_specs=pl.BlockSpec(memory_space=pltpu.VMEM),
        scratch_shapes=[
            pltpu.VMEM(half, shares.dtype),
            pltpu.VMEM(half, shares.dtype),
            pltpu.VMEM(half, shares.dtype),
            pltpu.SemaphoreType.DMA((2, chips)),
            pltpu.SemaphoreType.DMA((chips,)),
            pltpu.SemaphoreType.DMA((chips,)),
        ],
        compiler_params=pltpu.CompilerParams(collective_id=1, has_side_effects=True),
    )(shares)


def shards(images, prototypes, tile_row, tile_proto, tile_valid):
    img_count = lax.axis_size("img")
    proto_count = lax.axis_size("proto")
    slots = (tile_row.reshape(MAXT), tile_proto.reshape(MAXT), tile_valid.reshape(MAXT))
    log_ratio = math.log(PB_DEV * proto_count / (RB_DEV * img_count))
    slot_images = images.reshape(RB_DEV, TILE, E)[slots[0]]
    slot_protos = prototypes.reshape(PB_DEV, TILE, E)[slots[1]]
    row_pot, col_pot, col_columns = sinkhorn(slots, slot_images, slot_protos, log_ratio)
    partial_value = final_pass(slots, images, prototypes, col_columns, row_pot)
    proto_share = scatter_sum(partial_value)
    return (proto_share, col_pot.reshape(PB_DEV * TILE))


def solution(mesh):
    return jax.shard_map(
        shards,
        mesh=mesh,
        in_specs=(
            P("img", None),
            P("proto", None),
            P("img", "proto", None),
            P("img", "proto", None),
            P("img", "proto", None),
        ),
        out_specs=(P(("proto", "img"), None), P("proto")),
        check_vma=False,
    )
```

```python
import functools
import math

import jax
import jax.numpy as jnp
from jax import lax
from jax.experimental import pallas as pl
from jax.experimental.pallas import tpu as pltpu
from jax.sharding import PartitionSpec as P

E = 256
TILE = 512
RB_DEV = 4
PB_DEV = 8
MAXT = 6
ITERS = 3


far_below = -1e30


def running_top(values_of, live_slots, reduced, slot_blocks, block_count):

    def advance(position, tops):
        local_top = jnp.max(values_of(position), axis=reduced)
        target = slot_blocks[position]
        old_top = lax.dynamic_index_in_dim(tops, target, 0, keepdims=False)
        return lax.dynamic_update_index_in_dim(tops, jnp.maximum(old_top, local_top), target, 0)

    return lax.fori_loop(
        0, live_slots, advance, jnp.full((block_count, TILE), far_below, jnp.float32)
    )


def running_mass(values_of, live_slots, reduced, slot_blocks, tops):

    def advance(position, masses):
        target = slot_blocks[position]
        top_here = lax.dynamic_index_in_dim(tops, target, 0, keepdims=False)
        local_mass = jnp.sum(
            jnp.exp(values_of(position) - jnp.expand_dims(top_here, reduced)), axis=reduced
        )
        old_mass = lax.dynamic_index_in_dim(masses, target, 0, keepdims=False)
        return lax.dynamic_update_index_in_dim(masses, old_mass + local_mass, target, 0)

    return lax.fori_loop(0, live_slots, advance, jnp.zeros_like(tops))


def gather_kernel(axis, x_ref, out_ref, landed, send_sems, recv_sems):
    count = lax.axis_size(axis)
    me = lax.axis_index(axis)

    def peer_copy(peer, slot):
        return pltpu.make_async_remote_copy(
            src_ref=x_ref,
            dst_ref=landed.at[slot],
            send_sem=send_sems.at[slot],
            recv_sem=recv_sems.at[slot],
            device_id={axis: peer},
            device_id_type=pl.DeviceIdType.MESH,
        )

    landed[me] = x_ref[...]

    def send(step, carry):
        peer = lax.rem(me + step, count)
        peer_copy(peer, me).start()
        return carry

    lax.fori_loop(1, count, send, 0)

    def receive(step, carry):
        peer = lax.rem(me + count - step, count)
        peer_copy(peer, peer).wait_recv()
        return carry

    lax.fori_loop(1, count, receive, 0)

    def drain(step, carry):
        peer = lax.rem(me + step, count)
        peer_copy(peer, me).wait_send()
        return carry

    lax.fori_loop(1, count, drain, 0)
    out_ref[...] = landed[...]


def gather_peers(block, axis):
    count = lax.axis_size(axis)
    shape = (count,) + block.shape
    return pl.pallas_call(
        functools.partial(gather_kernel, axis),
        out_shape=jax.ShapeDtypeStruct(shape, block.dtype),
        in_specs=[pl.BlockSpec(memory_space=pltpu.VMEM)],
        out_specs=pl.BlockSpec(memory_space=pltpu.VMEM),
        scratch_shapes=[
            pltpu.VMEM(shape, block.dtype),
            pltpu.SemaphoreType.DMA((count,)),
            pltpu.SemaphoreType.DMA((count,)),
        ],
        compiler_params=pltpu.CompilerParams(has_side_effects=True),
    )(block)


def merge_tops(local_top, local_mass, axis):
    gathered = gather_peers(jnp.stack([local_top, local_mass]), axis)
    tops, masses = gathered[:, 0], gathered[:, 1]
    highest = jnp.max(tops, axis=0)
    summed = jnp.sum(masses * jnp.exp(tops - highest[None]), axis=0)
    return highest, summed


def slot_specs():
    return [pl.BlockSpec(memory_space=pltpu.SMEM)] * 3


def whole_specs(count):
    return [pl.BlockSpec(memory_space=pltpu.VMEM)] * count


def pass_kernel(along_rows, rows_ref, protos_ref, valid_ref, images_ref, prototypes_ref,
                other_ref, top_ref, mass_ref):
    top_ref[...] = jnp.full(top_ref.shape, far_below, jnp.float32)
    mass_ref[...] = jnp.zeros(mass_ref.shape, jnp.float32)
    score_scale = float(E) ** (-0.5)
    for position in range(MAXT):

        @pl.when(valid_ref[position] == 1)
        def _():
            row_block = rows_ref[position]
            proto_block = protos_ref[position]
            rows_here = images_ref[pl.ds(pl.multiple_of(row_block * TILE, TILE), TILE), :]
            protos_here = prototypes_ref[pl.ds(pl.multiple_of(proto_block * TILE, TILE), TILE), :]
            if along_rows:
                first, second, other_block, target = protos_here, rows_here, proto_block, row_block
            else:
                first, second, other_block, target = rows_here, protos_here, row_block, proto_block
            products = lax.dot_general(
                first, second, (((1,), (1,)), ((), ())), preferred_element_type=jnp.float32
            )
            values = products * score_scale + other_ref[other_block]
            local_top = jnp.max(values, axis=0, keepdims=True)
            old_top = top_ref[target]
            new_top = jnp.maximum(old_top, local_top)
            local_mass = jnp.sum(jnp.exp(values - new_top), axis=0, keepdims=True)
            mass_ref[target] = mass_ref[target] * jnp.exp(old_top - new_top) + local_mass
            top_ref[target] = new_top


def local_pass(along_rows, slots, images, prototypes, other_column):
    blocks = RB_DEV if along_rows else PB_DEV
    shape = jax.ShapeDtypeStruct((blocks, 1, TILE), jnp.float32)
    return pl.pallas_call(
        functools.partial(pass_kernel, along_rows),
        out_shape=(shape, shape),
        in_specs=slot_specs() + whole_specs(3),
        out_specs=tuple(whole_specs(2)),
    )(*slots, images, prototypes, other_column)


def final_kernel(rows_ref, protos_ref, valid_ref, images_ref, prototypes_ref,
                 col_ref, row_ref, shares_ref, acc_ref):
    acc_ref[...] = jnp.zeros(acc_ref.shape, jnp.float32)
    score_scale = float(E) ** (-0.5)
    for position in range(MAXT):

        @pl.when(valid_ref[position] == 1)
        def _():
            row_block = rows_ref[position]
            proto_block = protos_ref[position]
            rows_here = images_ref[pl.ds(pl.multiple_of(row_block * TILE, TILE), TILE), :]
            protos_here = prototypes_ref[pl.ds(pl.multiple_of(proto_block * TILE, TILE), TILE), :]
            products = lax.dot_general(
                protos_here, rows_here, (((1,), (1,)), ((), ())), preferred_element_type=jnp.float32
            )
            weights = jnp.exp(
                products * score_scale + col_ref[proto_block] + row_ref[row_block]
            ).astype(jnp.bfloat16)
            acc_ref[proto_block] += jnp.dot(weights, rows_here, preferred_element_type=jnp.float32)

    half = TILE // 2
    for block in range(PB_DEV):
        for core in range(2):
            shares_ref[core, block] = acc_ref[block, core * half:(core + 1) * half, :].astype(
                jnp.bfloat16
            )


def final_pass(slots, images, prototypes, col_column, row_pot):
    return pl.pallas_call(
        final_kernel,
        out_shape=jax.ShapeDtypeStruct((2, PB_DEV, TILE // 2, E), jnp.bfloat16),
        in_specs=slot_specs() + whole_specs(4),
        out_specs=pl.BlockSpec(memory_space=pltpu.VMEM),
        scratch_shapes=[pltpu.VMEM((PB_DEV, TILE, E), jnp.float32)],
    )(*slots, images, prototypes, col_column, row_pot)


def to_column(lanes):
    padded = jnp.concatenate(
        [lanes, jnp.zeros((8 - lanes.shape[0], TILE), jnp.float32)], axis=0
    ) if lanes.shape[0] < 8 else lanes
    return jnp.transpose(padded)


def stage_peer(axis, size, stride, step):
    me = lax.axis_index(axis)
    place = lax.rem(me // stride, size)
    return me + (lax.rem(place + step, size) - place) * stride, place


def exchange_stage(axis, size, stride, stage, local, packed, landed, send_sems, recv_sems):
    place = stage_peer(axis, size, stride, 0)[1]
    packed[...] = local
    landed[stage, place] = local

    def peer_copy(step, slot):
        return pltpu.make_async_remote_copy(
            src_ref=packed,
            dst_ref=landed.at[stage, slot],
            send_sem=send_sems.at[stage, lax.rem(place + step, size)],
            recv_sem=recv_sems.at[stage, slot],
            device_id={axis: stage_peer(axis, size, stride, step)[0]},
            device_id_type=pl.DeviceIdType.MESH,
        )

    def send(step, carry):
        peer_copy(step, place).start()
        return carry

    lax.fori_loop(1, size, send, 0)

    def receive(step, carry):
        peer_copy(size - step, lax.rem(place + size - step, size)).wait_recv()
        return carry

    lax.fori_loop(1, size, receive, 0)

    def drain(step, carry):
        peer_copy(step, place).wait_send()
        return carry

    lax.fori_loop(1, size, drain, 0)
    gathered = landed[stage]
    highest = jnp.max(gathered, axis=0)
    return highest + jnp.log(jnp.sum(jnp.exp(gathered - highest[None]), axis=0))


def exchange(axis, groups, stage, local, packed, landed_refs, send_refs, recv_refs):
    for (size, stride), landed, send_sems, recv_sems in zip(groups, landed_refs, send_refs,
                                                           recv_refs):
        local = exchange_stage(axis, size, stride, stage, local, packed, landed, send_sems,
                               recv_sems)
    return local


def pick_column(columns, chosen_block, blocks):
    picked = columns[:, 0:1]
    for block in range(1, blocks):
        picked = jnp.where(chosen_block == block, columns[:, block:block + 1], picked)
    return picked


def local_merge(along_rows, rows_ref, protos_ref, valid_ref, slot_images_ref, slot_protos_ref,
                other_columns, cache, fill):
    blocks = RB_DEV if along_rows else PB_DEV
    other_blocks = PB_DEV if along_rows else RB_DEV
    tops = [jnp.full((1, TILE), far_below, jnp.float32) for _ in range(blocks)]
    masses = [jnp.zeros((1, TILE), jnp.float32) for _ in range(blocks)]
    score_scale = float(E) ** (-0.5)
    for position in range(MAXT):
        row_block = rows_ref[position]
        proto_block = protos_ref[position]
        live = valid_ref[position] == 1
        rows_here = slot_images_ref[position]
        protos_here = slot_protos_ref[position]
        if along_rows:
            first, second, other_block, target = protos_here, rows_here, proto_block, row_block
        else:
            first, second, other_block, target = rows_here, protos_here, row_block, proto_block
        if fill:
            scores = lax.dot_general(
                first, second, (((1,), (1,)), ((), ())), preferred_element_type=jnp.float32
            ) * score_scale
            cache[position] = scores
        else:
            scores = cache[position]
        values = scores + pick_column(other_columns, other_block, other_blocks)
        local_top = jnp.max(values, axis=0, keepdims=True)
        local_mass = jnp.sum(jnp.exp(values - local_top), axis=0, keepdims=True)
        for block in range(blocks):
            chosen = jnp.logical_and(live, target == block)
            new_top = jnp.maximum(tops[block], local_top)
            new_mass = masses[block] * jnp.exp(tops[block] - new_top) + local_mass * jnp.exp(
                local_top - new_top
            )
            tops[block] = jnp.where(chosen, new_top, tops[block])
            masses[block] = jnp.where(chosen, new_mass, masses[block])
    return jnp.maximum(
        jnp.concatenate(tops, axis=0) + jnp.log(jnp.concatenate(masses, axis=0)), far_below
    )


def axis_groups():
    proto_count = lax.axis_size("proto")
    img_count = lax.axis_size("img")
    return {
        "proto": ((PB_DEV, 1), (proto_count // PB_DEV, PB_DEV)),
        "img": ((2, 1), (img_count // 2, 2)),
    }


def sinkhorn_kernel(log_ratio, rows_ref, protos_ref, valid_ref, images_ref, prototypes_ref,
                    row_out, col_out, col_columns_out, row_cache, col_cache, row_packed,
                    col_packed, *stage_refs):
    groups = axis_groups()
    row_refs = stage_refs[0:6]
    col_refs = stage_refs[6:12]
    barrier = pltpu.get_barrier_semaphore()
    greeted = 0
    for axis in ("proto", "img"):
        for size, stride in groups[axis]:

            def greet(step, carry):
                peer = stage_peer(axis, size, stride, step)[0]
                pl.semaphore_signal(barrier, inc=1, device_id={axis: peer},
                                    device_id_type=pl.DeviceIdType.MESH)
                return carry

            lax.fori_loop(1, size, greet, 0)
            greeted += size - 1
    pl.semaphore_wait(barrier, greeted)

    col_t = jnp.zeros((TILE, PB_DEV), jnp.float32)
    for iteration in range(ITERS):
        local = local_merge(True, rows_ref, protos_ref, valid_ref, images_ref, prototypes_ref,
                            col_t, row_cache, iteration == 0)
        merged = exchange("proto", groups["proto"], iteration, local, row_packed,
                          row_refs[0:2], row_refs[2:4], row_refs[4:6])
        row_pot = log_ratio - merged
        row_t = to_column(row_pot)
        local = local_merge(False, rows_ref, protos_ref, valid_ref, images_ref, prototypes_ref,
                            row_t, col_cache, iteration == 0)
        merged = exchange("img", groups["img"], iteration, local, col_packed,
                          col_refs[0:2], col_refs[2:4], col_refs[4:6])
        col_pot = -merged
        col_t = to_column(col_pot)
    for block in range(RB_DEV):
        row_out[block] = row_pot[block:block + 1]
    col_out[...] = col_pot
    for block in range(PB_DEV):
        col_columns_out[block] = col_t[:, block:block + 1]


def sinkhorn(slots, slot_images, slot_protos, log_ratio):
    groups = axis_groups()
    vmem = pltpu.VMEM
    stage_scratch = []
    for axis, blocks in (("proto", RB_DEV), ("img", PB_DEV)):
        sizes = [size for size, _ in groups[axis]]
        stage_scratch += [vmem((ITERS, size, blocks, TILE), jnp.float32) for size in sizes]
        stage_scratch += [pltpu.SemaphoreType.DMA((ITERS, size)) for size in sizes]
        stage_scratch += [pltpu.SemaphoreType.DMA((ITERS, size)) for size in sizes]
    return pl.pallas_call(
        functools.partial(sinkhorn_kernel, log_ratio),
        out_shape=(
            jax.ShapeDtypeStruct((RB_DEV, 1, TILE), jnp.float32),
            jax.ShapeDtypeStruct((PB_DEV, TILE), jnp.float32),
            jax.ShapeDtypeStruct((PB_DEV, TILE, 1), jnp.float32),
        ),
        in_specs=slot_specs() + whole_specs(2),
        out_specs=tuple(whole_specs(3)),
        scratch_shapes=[
            vmem((MAXT, TILE, TILE), jnp.float32),
            vmem((MAXT, TILE, TILE), jnp.float32),
            vmem((RB_DEV, TILE), jnp.float32),
            vmem((PB_DEV, TILE), jnp.float32),
        ] + stage_scratch,
        compiler_params=pltpu.CompilerParams(collective_id=0, has_side_effects=True),
    )(*slots, slot_images, slot_protos)


def scatter_kernel(shares_ref, out_ref, paired, pair_sums, landed, pair_sems, send_sems,
                   recv_sems):
    count = lax.axis_size("img")
    chips = count // 2
    me = lax.axis_index("img")
    core = lax.rem(me, 2)
    chip = me // 2
    partner = me + 1 - 2 * core
    barrier = pltpu.get_barrier_semaphore()
    pl.semaphore_signal(barrier, inc=1, device_id={"img": partner},
                        device_id_type=pl.DeviceIdType.MESH)

    def greet(step, carry):
        peer = lax.rem(chip + step, chips) * 2 + core
        pl.semaphore_signal(barrier, inc=1, device_id={"img": peer},
                            device_id_type=pl.DeviceIdType.MESH)
        return carry

    lax.fori_loop(1, chips, greet, 0)
    pl.semaphore_wait(barrier, chips)

    def pair_copy(piece):
        return pltpu.make_async_remote_copy(
            src_ref=shares_ref.at[1 - core, piece],
            dst_ref=paired.at[piece],
            send_sem=pair_sems.at[0, piece],
            recv_sem=pair_sems.at[1, piece],
            device_id={"img": partner},
            device_id_type=pl.DeviceIdType.MESH,
        )

    def peer_copy(peer_chip, slot):
        return pltpu.make_async_remote_copy(
            src_ref=pair_sums.at[peer_chip],
            dst_ref=landed.at[slot],
            send_sem=send_sems.at[peer_chip],
            recv_sem=recv_sems.at[slot],
            device_id={"img": peer_chip * 2 + core},
            device_id_type=pl.DeviceIdType.MESH,
        )

    def pair_send(step, carry):
        pair_copy(lax.rem(chip + step, chips)).start()
        return carry

    lax.fori_loop(1, chips + 1, pair_send, 0)

    def add_pair(piece):
        pair_copy(piece).wait_recv()
        pair_sums[piece] = (
            shares_ref[core, piece].astype(jnp.float32) + paired[piece].astype(jnp.float32)
        ).astype(jnp.bfloat16)

    def send(step, carry):
        piece = lax.rem(chip + step, chips)
        add_pair(piece)
        peer_copy(piece, chip).start()
        return carry

    lax.fori_loop(1, chips, send, 0)
    add_pair(chip)
    out_ref[...] = pair_sums[chip].astype(jnp.float32)

    def receive(step, carry):
        source = lax.rem(chip + chips - step, chips)
        peer_copy(source, source).wait_recv()
        out_ref[...] += landed[source].astype(jnp.float32)
        return carry

    lax.fori_loop(1, chips, receive, 0)

    def drain(step, carry):
        peer_copy(lax.rem(chip + step, chips), chip).wait_send()
        return carry

    lax.fori_loop(1, chips, drain, 0)

    def pair_drain(step, carry):
        pair_copy(lax.rem(chip + step, chips)).wait_send()
        return carry

    lax.fori_loop(1, chips + 1, pair_drain, 0)


def scatter_sum(shares):
    cores, chips, rows, width = shares.shape
    half = (chips, rows, width)
    return pl.pallas_call(
        scatter_kernel,
        out_shape=jax.ShapeDtypeStruct((rows, width), jnp.float32),
        in_specs=whole_specs(1),
        out_specs=pl.BlockSpec(memory_space=pltpu.VMEM),
        scratch_shapes=[
            pltpu.VMEM(half, shares.dtype),
            pltpu.VMEM(half, shares.dtype),
            pltpu.VMEM(half, shares.dtype),
            pltpu.SemaphoreType.DMA((2, chips)),
            pltpu.SemaphoreType.DMA((chips,)),
            pltpu.SemaphoreType.DMA((chips,)),
        ],
        compiler_params=pltpu.CompilerParams(collective_id=1, has_side_effects=True),
    )(shares)


def shards(images, prototypes, tile_row, tile_proto, tile_valid):
    img_count = lax.axis_size("img")
    proto_count = lax.axis_size("proto")
    slots = (tile_row.reshape(MAXT), tile_proto.reshape(MAXT), tile_valid.reshape(MAXT))
    log_ratio = math.log(PB_DEV * proto_count / (RB_DEV * img_count))
    slot_images = images.reshape(RB_DEV, TILE, E)[slots[0]]
    slot_protos = prototypes.reshape(PB_DEV, TILE, E)[slots[1]]
    row_pot, col_pot, col_columns = sinkhorn(slots, slot_images, slot_protos, log_ratio)
    partial_value = final_pass(slots, images, prototypes, col_columns, row_pot)
    proto_share = scatter_sum(partial_value)
    return (proto_share, col_pot.reshape(PB_DEV * TILE))


def solution(mesh):
    return jax.shard_map(
        shards,
        mesh=mesh,
        in_specs=(
            P("img", None),
            P("proto", None),
            P("img", "proto", None),
            P("img", "proto", None),
            P("img", "proto", None),
        ),
        out_specs=(P(("proto", "img"), None), P("proto")),
        check_vma=False,
    )
```

```python
import functools
import math

import jax
import jax.numpy as jnp
from jax import lax
from jax.experimental import pallas as pl
from jax.experimental.pallas import tpu as pltpu
from jax.sharding import PartitionSpec as P

E = 256
TILE = 512
RB_DEV = 4
PB_DEV = 8
MAXT = 6
ITERS = 3


far_below = -1e30


def running_top(values_of, live_slots, reduced, slot_blocks, block_count):

    def advance(position, tops):
        local_top = jnp.max(values_of(position), axis=reduced)
        target = slot_blocks[position]
        old_top = lax.dynamic_index_in_dim(tops, target, 0, keepdims=False)
        return lax.dynamic_update_index_in_dim(tops, jnp.maximum(old_top, local_top), target, 0)

    return lax.fori_loop(
        0, live_slots, advance, jnp.full((block_count, TILE), far_below, jnp.float32)
    )


def running_mass(values_of, live_slots, reduced, slot_blocks, tops):

    def advance(position, masses):
        target = slot_blocks[position]
        top_here = lax.dynamic_index_in_dim(tops, target, 0, keepdims=False)
        local_mass = jnp.sum(
            jnp.exp(values_of(position) - jnp.expand_dims(top_here, reduced)), axis=reduced
        )
        old_mass = lax.dynamic_index_in_dim(masses, target, 0, keepdims=False)
        return lax.dynamic_update_index_in_dim(masses, old_mass + local_mass, target, 0)

    return lax.fori_loop(0, live_slots, advance, jnp.zeros_like(tops))


def gather_kernel(axis, x_ref, out_ref, landed, send_sems, recv_sems):
    count = lax.axis_size(axis)
    me = lax.axis_index(axis)

    def peer_copy(peer, slot):
        return pltpu.make_async_remote_copy(
            src_ref=x_ref,
            dst_ref=landed.at[slot],
            send_sem=send_sems.at[slot],
            recv_sem=recv_sems.at[slot],
            device_id={axis: peer},
            device_id_type=pl.DeviceIdType.MESH,
        )

    landed[me] = x_ref[...]

    def send(step, carry):
        peer = lax.rem(me + step, count)
        peer_copy(peer, me).start()
        return carry

    lax.fori_loop(1, count, send, 0)

    def receive(step, carry):
        peer = lax.rem(me + count - step, count)
        peer_copy(peer, peer).wait_recv()
        return carry

    lax.fori_loop(1, count, receive, 0)

    def drain(step, carry):
        peer = lax.rem(me + step, count)
        peer_copy(peer, me).wait_send()
        return carry

    lax.fori_loop(1, count, drain, 0)
    out_ref[...] = landed[...]


def gather_peers(block, axis):
    count = lax.axis_size(axis)
    shape = (count,) + block.shape
    return pl.pallas_call(
        functools.partial(gather_kernel, axis),
        out_shape=jax.ShapeDtypeStruct(shape, block.dtype),
        in_specs=[pl.BlockSpec(memory_space=pltpu.VMEM)],
        out_specs=pl.BlockSpec(memory_space=pltpu.VMEM),
        scratch_shapes=[
            pltpu.VMEM(shape, block.dtype),
            pltpu.SemaphoreType.DMA((count,)),
            pltpu.SemaphoreType.DMA((count,)),
        ],
        compiler_params=pltpu.CompilerParams(has_side_effects=True),
    )(block)


def merge_tops(local_top, local_mass, axis):
    gathered = gather_peers(jnp.stack([local_top, local_mass]), axis)
    tops, masses = gathered[:, 0], gathered[:, 1]
    highest = jnp.max(tops, axis=0)
    summed = jnp.sum(masses * jnp.exp(tops - highest[None]), axis=0)
    return highest, summed


def slot_specs():
    return [pl.BlockSpec(memory_space=pltpu.SMEM)] * 3


def whole_specs(count):
    return [pl.BlockSpec(memory_space=pltpu.VMEM)] * count


def pass_kernel(along_rows, rows_ref, protos_ref, valid_ref, images_ref, prototypes_ref,
                other_ref, top_ref, mass_ref):
    top_ref[...] = jnp.full(top_ref.shape, far_below, jnp.float32)
    mass_ref[...] = jnp.zeros(mass_ref.shape, jnp.float32)
    score_scale = float(E) ** (-0.5)
    for position in range(MAXT):

        @pl.when(valid_ref[position] == 1)
        def _():
            row_block = rows_ref[position]
            proto_block = protos_ref[position]
            rows_here = images_ref[pl.ds(pl.multiple_of(row_block * TILE, TILE), TILE), :]
            protos_here = prototypes_ref[pl.ds(pl.multiple_of(proto_block * TILE, TILE), TILE), :]
            if along_rows:
                first, second, other_block, target = protos_here, rows_here, proto_block, row_block
            else:
                first, second, other_block, target = rows_here, protos_here, row_block, proto_block
            products = lax.dot_general(
                first, second, (((1,), (1,)), ((), ())), preferred_element_type=jnp.float32
            )
            values = products * score_scale + other_ref[other_block]
            local_top = jnp.max(values, axis=0, keepdims=True)
            old_top = top_ref[target]
            new_top = jnp.maximum(old_top, local_top)
            local_mass = jnp.sum(jnp.exp(values - new_top), axis=0, keepdims=True)
            mass_ref[target] = mass_ref[target] * jnp.exp(old_top - new_top) + local_mass
            top_ref[target] = new_top


def local_pass(along_rows, slots, images, prototypes, other_column):
    blocks = RB_DEV if along_rows else PB_DEV
    shape = jax.ShapeDtypeStruct((blocks, 1, TILE), jnp.float32)
    return pl.pallas_call(
        functools.partial(pass_kernel, along_rows),
        out_shape=(shape, shape),
        in_specs=slot_specs() + whole_specs(3),
        out_specs=tuple(whole_specs(2)),
    )(*slots, images, prototypes, other_column)


def final_kernel(rows_ref, protos_ref, valid_ref, images_ref, prototypes_ref,
                 col_ref, row_ref, shares_ref, acc_ref):
    acc_ref[...] = jnp.zeros(acc_ref.shape, jnp.float32)
    score_scale = float(E) ** (-0.5)
    for position in range(MAXT):

        @pl.when(valid_ref[position] == 1)
        def _():
            row_block = rows_ref[position]
            proto_block = protos_ref[position]
            rows_here = images_ref[pl.ds(pl.multiple_of(row_block * TILE, TILE), TILE), :]
            protos_here = prototypes_ref[pl.ds(pl.multiple_of(proto_block * TILE, TILE), TILE), :]
            products = lax.dot_general(
                protos_here, rows_here, (((1,), (1,)), ((), ())), preferred_element_type=jnp.float32
            )
            weights = jnp.exp(
                products * score_scale + col_ref[proto_block] + row_ref[row_block]
            ).astype(jnp.bfloat16)
            acc_ref[proto_block] += jnp.dot(weights, rows_here, preferred_element_type=jnp.float32)

    half = TILE // 2
    for block in range(PB_DEV):
        for core in range(2):
            shares_ref[core, block] = acc_ref[block, core * half:(core + 1) * half, :].astype(
                jnp.bfloat16
            )


def final_pass(slots, images, prototypes, col_column, row_pot):
    return pl.pallas_call(
        final_kernel,
        out_shape=jax.ShapeDtypeStruct((2, PB_DEV, TILE // 2, E), jnp.bfloat16),
        in_specs=slot_specs() + whole_specs(4),
        out_specs=pl.BlockSpec(memory_space=pltpu.VMEM),
        scratch_shapes=[pltpu.VMEM((PB_DEV, TILE, E), jnp.float32)],
    )(*slots, images, prototypes, col_column, row_pot)


def to_column(lanes):
    padded = jnp.concatenate(
        [lanes, jnp.zeros((8 - lanes.shape[0], TILE), jnp.float32)], axis=0
    ) if lanes.shape[0] < 8 else lanes
    return jnp.transpose(padded)


def stage_peer(axis, size, stride, step):
    me = lax.axis_index(axis)
    place = lax.rem(me // stride, size)
    return me + (lax.rem(place + step, size) - place) * stride, place


def exchange_stage(axis, size, stride, stage, local, packed, landed, send_sems, recv_sems):
    place = stage_peer(axis, size, stride, 0)[1]
    packed[...] = local
    landed[stage, place] = local

    def peer_copy(step, slot):
        return pltpu.make_async_remote_copy(
            src_ref=packed,
            dst_ref=landed.at[stage, slot],
            send_sem=send_sems.at[stage, lax.rem(place + step, size)],
            recv_sem=recv_sems.at[stage, slot],
            device_id={axis: stage_peer(axis, size, stride, step)[0]},
            device_id_type=pl.DeviceIdType.MESH,
        )

    def send(step, carry):
        peer_copy(step, place).start()
        return carry

    lax.fori_loop(1, size, send, 0)

    def receive(step, carry):
        peer_copy(size - step, lax.rem(place + size - step, size)).wait_recv()
        return carry

    lax.fori_loop(1, size, receive, 0)

    def drain(step, carry):
        peer_copy(step, place).wait_send()
        return carry

    lax.fori_loop(1, size, drain, 0)
    gathered = landed[stage]
    highest = jnp.max(gathered, axis=0)
    return highest + jnp.log(jnp.sum(jnp.exp(gathered - highest[None]), axis=0))


def exchange(axis, groups, stage, local, packed, landed_refs, send_refs, recv_refs):
    for (size, stride), landed, send_sems, recv_sems in zip(groups, landed_refs, send_refs,
                                                           recv_refs):
        local = exchange_stage(axis, size, stride, stage, local, packed, landed, send_sems,
                               recv_sems)
    return local


def pick_column(columns, chosen_block, blocks):
    picked = columns[:, 0:1]
    for block in range(1, blocks):
        picked = jnp.where(chosen_block == block, columns[:, block:block + 1], picked)
    return picked


def local_merge(along_rows, rows_ref, protos_ref, valid_ref, slot_images_ref, slot_protos_ref,
                other_columns):
    blocks = RB_DEV if along_rows else PB_DEV
    other_blocks = PB_DEV if along_rows else RB_DEV
    tops = [jnp.full((1, TILE), far_below, jnp.float32) for _ in range(blocks)]
    masses = [jnp.zeros((1, TILE), jnp.float32) for _ in range(blocks)]
    score_scale = float(E) ** (-0.5)
    for position in range(MAXT):
        row_block = rows_ref[position]
        proto_block = protos_ref[position]
        live = valid_ref[position] == 1
        rows_here = slot_images_ref[position]
        protos_here = slot_protos_ref[position]
        if along_rows:
            first, second, other_block, target = protos_here, rows_here, proto_block, row_block
        else:
            first, second, other_block, target = rows_here, protos_here, row_block, proto_block
        products = lax.dot_general(
            first, second, (((1,), (1,)), ((), ())), preferred_element_type=jnp.float32
        )
        values = products * score_scale + pick_column(other_columns, other_block, other_blocks)
        local_top = jnp.max(values, axis=0, keepdims=True)
        local_mass = jnp.sum(jnp.exp(values - local_top), axis=0, keepdims=True)
        for block in range(blocks):
            chosen = jnp.logical_and(live, target == block)
            new_top = jnp.maximum(tops[block], local_top)
            new_mass = masses[block] * jnp.exp(tops[block] - new_top) + local_mass * jnp.exp(
                local_top - new_top
            )
            tops[block] = jnp.where(chosen, new_top, tops[block])
            masses[block] = jnp.where(chosen, new_mass, masses[block])
    return jnp.maximum(
        jnp.concatenate(tops, axis=0) + jnp.log(jnp.concatenate(masses, axis=0)), far_below
    )


def axis_groups():
    proto_count = lax.axis_size("proto")
    img_count = lax.axis_size("img")
    return {
        "proto": ((PB_DEV, 1), (proto_count // PB_DEV, PB_DEV)),
        "img": ((2, 1), (img_count // 2, 2)),
    }


def sinkhorn_kernel(log_ratio, rows_ref, protos_ref, valid_ref, images_ref, prototypes_ref,
                    row_out, col_out, col_columns_out, row_packed, col_packed, *stage_refs):
    groups = axis_groups()
    row_refs = stage_refs[0:6]
    col_refs = stage_refs[6:12]
    barrier = pltpu.get_barrier_semaphore()
    greeted = 0
    for axis in ("proto", "img"):
        for size, stride in groups[axis]:

            def greet(step, carry):
                peer = stage_peer(axis, size, stride, step)[0]
                pl.semaphore_signal(barrier, inc=1, device_id={axis: peer},
                                    device_id_type=pl.DeviceIdType.MESH)
                return carry

            lax.fori_loop(1, size, greet, 0)
            greeted += size - 1
    pl.semaphore_wait(barrier, greeted)

    col_t = jnp.zeros((TILE, PB_DEV), jnp.float32)
    for iteration in range(ITERS):
        local = local_merge(True, rows_ref, protos_ref, valid_ref, images_ref, prototypes_ref,
                            col_t)
        merged = exchange("proto", groups["proto"], iteration, local, row_packed,
                          row_refs[0:2], row_refs[2:4], row_refs[4:6])
        row_pot = log_ratio - merged
        row_t = to_column(row_pot)
        local = local_merge(False, rows_ref, protos_ref, valid_ref, images_ref, prototypes_ref,
                            row_t)
        merged = exchange("img", groups["img"], iteration, local, col_packed,
                          col_refs[0:2], col_refs[2:4], col_refs[4:6])
        col_pot = -merged
        col_t = to_column(col_pot)
    for block in range(RB_DEV):
        row_out[block] = row_pot[block:block + 1]
    col_out[...] = col_pot
    for block in range(PB_DEV):
        col_columns_out[block] = col_t[:, block:block + 1]


def sinkhorn(slots, slot_images, slot_protos, log_ratio):
    groups = axis_groups()
    vmem = pltpu.VMEM
    stage_scratch = []
    for axis, blocks in (("proto", RB_DEV), ("img", PB_DEV)):
        sizes = [size for size, _ in groups[axis]]
        stage_scratch += [vmem((ITERS, size, blocks, TILE), jnp.float32) for size in sizes]
        stage_scratch += [pltpu.SemaphoreType.DMA((ITERS, size)) for size in sizes]
        stage_scratch += [pltpu.SemaphoreType.DMA((ITERS, size)) for size in sizes]
    return pl.pallas_call(
        functools.partial(sinkhorn_kernel, log_ratio),
        out_shape=(
            jax.ShapeDtypeStruct((RB_DEV, 1, TILE), jnp.float32),
            jax.ShapeDtypeStruct((PB_DEV, TILE), jnp.float32),
            jax.ShapeDtypeStruct((PB_DEV, TILE, 1), jnp.float32),
        ),
        in_specs=slot_specs() + whole_specs(2),
        out_specs=tuple(whole_specs(3)),
        scratch_shapes=[
            vmem((RB_DEV, TILE), jnp.float32),
            vmem((PB_DEV, TILE), jnp.float32),
        ] + stage_scratch,
        compiler_params=pltpu.CompilerParams(collective_id=0, has_side_effects=True),
    )(*slots, slot_images, slot_protos)


def scatter_kernel(shares_ref, out_ref, paired, pair_sums, landed, pair_sems, send_sems,
                   recv_sems):
    count = lax.axis_size("img")
    chips = count // 2
    me = lax.axis_index("img")
    core = lax.rem(me, 2)
    chip = me // 2
    partner = me + 1 - 2 * core
    barrier = pltpu.get_barrier_semaphore()
    pl.semaphore_signal(barrier, inc=1, device_id={"img": partner},
                        device_id_type=pl.DeviceIdType.MESH)

    def greet(step, carry):
        peer = lax.rem(chip + step, chips) * 2 + core
        pl.semaphore_signal(barrier, inc=1, device_id={"img": peer},
                            device_id_type=pl.DeviceIdType.MESH)
        return carry

    lax.fori_loop(1, chips, greet, 0)
    pl.semaphore_wait(barrier, chips)

    def pair_copy(piece):
        return pltpu.make_async_remote_copy(
            src_ref=shares_ref.at[1 - core, piece],
            dst_ref=paired.at[piece],
            send_sem=pair_sems.at[0, piece],
            recv_sem=pair_sems.at[1, piece],
            device_id={"img": partner},
            device_id_type=pl.DeviceIdType.MESH,
        )

    def peer_copy(peer_chip, slot):
        return pltpu.make_async_remote_copy(
            src_ref=pair_sums.at[peer_chip],
            dst_ref=landed.at[slot],
            send_sem=send_sems.at[peer_chip],
            recv_sem=recv_sems.at[slot],
            device_id={"img": peer_chip * 2 + core},
            device_id_type=pl.DeviceIdType.MESH,
        )

    def pair_send(step, carry):
        pair_copy(lax.rem(chip + step, chips)).start()
        return carry

    lax.fori_loop(1, chips + 1, pair_send, 0)

    def add_pair(piece):
        pair_copy(piece).wait_recv()
        pair_sums[piece] = (
            shares_ref[core, piece].astype(jnp.float32) + paired[piece].astype(jnp.float32)
        ).astype(jnp.bfloat16)

    def send(step, carry):
        piece = lax.rem(chip + step, chips)
        add_pair(piece)
        peer_copy(piece, chip).start()
        return carry

    lax.fori_loop(1, chips, send, 0)
    add_pair(chip)
    out_ref[...] = pair_sums[chip].astype(jnp.float32)

    def receive(step, carry):
        source = lax.rem(chip + chips - step, chips)
        peer_copy(source, source).wait_recv()
        out_ref[...] += landed[source].astype(jnp.float32)
        return carry

    lax.fori_loop(1, chips, receive, 0)

    def drain(step, carry):
        peer_copy(lax.rem(chip + step, chips), chip).wait_send()
        return carry

    lax.fori_loop(1, chips, drain, 0)

    def pair_drain(step, carry):
        pair_copy(lax.rem(chip + step, chips)).wait_send()
        return carry

    lax.fori_loop(1, chips + 1, pair_drain, 0)


def scatter_sum(shares):
    cores, chips, rows, width = shares.shape
    half = (chips, rows, width)
    return pl.pallas_call(
        scatter_kernel,
        out_shape=jax.ShapeDtypeStruct((rows, width), jnp.float32),
        in_specs=whole_specs(1),
        out_specs=pl.BlockSpec(memory_space=pltpu.VMEM),
        scratch_shapes=[
            pltpu.VMEM(half, shares.dtype),
            pltpu.VMEM(half, shares.dtype),
            pltpu.VMEM(half, shares.dtype),
            pltpu.SemaphoreType.DMA((2, chips)),
            pltpu.SemaphoreType.DMA((chips,)),
            pltpu.SemaphoreType.DMA((chips,)),
        ],
        compiler_params=pltpu.CompilerParams(collective_id=1, has_side_effects=True),
    )(shares)


def copy_kernel(rows_ref, protos_ref, image_block, proto_block, image_out, proto_out):
    image_out[...] = image_block[...]
    proto_out[...] = proto_block[...]


def gather_slots(slots, images, prototypes):
    block = (None, TILE, E)
    return pl.pallas_call(
        copy_kernel,
        out_shape=(
            jax.ShapeDtypeStruct((MAXT, TILE, E), images.dtype),
            jax.ShapeDtypeStruct((MAXT, TILE, E), prototypes.dtype),
        ),
        grid_spec=pltpu.PrefetchScalarGridSpec(
            num_scalar_prefetch=2,
            grid=(MAXT,),
            in_specs=[
                pl.BlockSpec(block, lambda s, rows, protos: (rows[s], 0, 0)),
                pl.BlockSpec(block, lambda s, rows, protos: (protos[s], 0, 0)),
            ],
            out_specs=[
                pl.BlockSpec(block, lambda s, rows, protos: (s, 0, 0)),
                pl.BlockSpec(block, lambda s, rows, protos: (s, 0, 0)),
            ],
        ),
    )(slots[0], slots[1], images.reshape(RB_DEV, TILE, E), prototypes.reshape(PB_DEV, TILE, E))


def shards(images, prototypes, tile_row, tile_proto, tile_valid):
    img_count = lax.axis_size("img")
    proto_count = lax.axis_size("proto")
    slots = (tile_row.reshape(MAXT), tile_proto.reshape(MAXT), tile_valid.reshape(MAXT))
    log_ratio = math.log(PB_DEV * proto_count / (RB_DEV * img_count))
    slot_images, slot_protos = gather_slots(slots, images, prototypes)
    row_pot, col_pot, col_columns = sinkhorn(slots, slot_images, slot_protos, log_ratio)
    partial_value = final_pass(slots, images, prototypes, col_columns, row_pot)
    proto_share = scatter_sum(partial_value)
    return (proto_share, col_pot.reshape(PB_DEV * TILE))


def solution(mesh):
    return jax.shard_map(
        shards,
        mesh=mesh,
        in_specs=(
            P("img", None),
            P("proto", None),
            P("img", "proto", None),
            P("img", "proto", None),
            P("img", "proto", None),
        ),
        out_specs=(P(("proto", "img"), None), P("proto")),
        check_vma=False,
    )
```

```python
import functools
import math

import jax
import jax.numpy as jnp
from jax import lax
from jax.experimental import pallas as pl
from jax.experimental.pallas import tpu as pltpu
from jax.sharding import PartitionSpec as P

E = 256
TILE = 512
RB_DEV = 4
PB_DEV = 8
MAXT = 6
ITERS = 3


far_below = -1e30


def running_top(values_of, live_slots, reduced, slot_blocks, block_count):

    def advance(position, tops):
        local_top = jnp.max(values_of(position), axis=reduced)
        target = slot_blocks[position]
        old_top = lax.dynamic_index_in_dim(tops, target, 0, keepdims=False)
        return lax.dynamic_update_index_in_dim(tops, jnp.maximum(old_top, local_top), target, 0)

    return lax.fori_loop(
        0, live_slots, advance, jnp.full((block_count, TILE), far_below, jnp.float32)
    )


def running_mass(values_of, live_slots, reduced, slot_blocks, tops):

    def advance(position, masses):
        target = slot_blocks[position]
        top_here = lax.dynamic_index_in_dim(tops, target, 0, keepdims=False)
        local_mass = jnp.sum(
            jnp.exp(values_of(position) - jnp.expand_dims(top_here, reduced)), axis=reduced
        )
        old_mass = lax.dynamic_index_in_dim(masses, target, 0, keepdims=False)
        return lax.dynamic_update_index_in_dim(masses, old_mass + local_mass, target, 0)

    return lax.fori_loop(0, live_slots, advance, jnp.zeros_like(tops))


def gather_kernel(axis, x_ref, out_ref, landed, send_sems, recv_sems):
    count = lax.axis_size(axis)
    me = lax.axis_index(axis)

    def peer_copy(peer, slot):
        return pltpu.make_async_remote_copy(
            src_ref=x_ref,
            dst_ref=landed.at[slot],
            send_sem=send_sems.at[slot],
            recv_sem=recv_sems.at[slot],
            device_id={axis: peer},
            device_id_type=pl.DeviceIdType.MESH,
        )

    landed[me] = x_ref[...]

    def send(step, carry):
        peer = lax.rem(me + step, count)
        peer_copy(peer, me).start()
        return carry

    lax.fori_loop(1, count, send, 0)

    def receive(step, carry):
        peer = lax.rem(me + count - step, count)
        peer_copy(peer, peer).wait_recv()
        return carry

    lax.fori_loop(1, count, receive, 0)

    def drain(step, carry):
        peer = lax.rem(me + step, count)
        peer_copy(peer, me).wait_send()
        return carry

    lax.fori_loop(1, count, drain, 0)
    out_ref[...] = landed[...]


def gather_peers(block, axis):
    count = lax.axis_size(axis)
    shape = (count,) + block.shape
    return pl.pallas_call(
        functools.partial(gather_kernel, axis),
        out_shape=jax.ShapeDtypeStruct(shape, block.dtype),
        in_specs=[pl.BlockSpec(memory_space=pltpu.VMEM)],
        out_specs=pl.BlockSpec(memory_space=pltpu.VMEM),
        scratch_shapes=[
            pltpu.VMEM(shape, block.dtype),
            pltpu.SemaphoreType.DMA((count,)),
            pltpu.SemaphoreType.DMA((count,)),
        ],
        compiler_params=pltpu.CompilerParams(has_side_effects=True),
    )(block)


def merge_tops(local_top, local_mass, axis):
    gathered = gather_peers(jnp.stack([local_top, local_mass]), axis)
    tops, masses = gathered[:, 0], gathered[:, 1]
    highest = jnp.max(tops, axis=0)
    summed = jnp.sum(masses * jnp.exp(tops - highest[None]), axis=0)
    return highest, summed


def slot_specs():
    return [pl.BlockSpec(memory_space=pltpu.SMEM)] * 3


def whole_specs(count):
    return [pl.BlockSpec(memory_space=pltpu.VMEM)] * count


def pass_kernel(along_rows, rows_ref, protos_ref, valid_ref, images_ref, prototypes_ref,
                other_ref, top_ref, mass_ref):
    top_ref[...] = jnp.full(top_ref.shape, far_below, jnp.float32)
    mass_ref[...] = jnp.zeros(mass_ref.shape, jnp.float32)
    score_scale = float(E) ** (-0.5)
    for position in range(MAXT):

        @pl.when(valid_ref[position] == 1)
        def _():
            row_block = rows_ref[position]
            proto_block = protos_ref[position]
            rows_here = images_ref[pl.ds(pl.multiple_of(row_block * TILE, TILE), TILE), :]
            protos_here = prototypes_ref[pl.ds(pl.multiple_of(proto_block * TILE, TILE), TILE), :]
            if along_rows:
                first, second, other_block, target = protos_here, rows_here, proto_block, row_block
            else:
                first, second, other_block, target = rows_here, protos_here, row_block, proto_block
            products = lax.dot_general(
                first, second, (((1,), (1,)), ((), ())), preferred_element_type=jnp.float32
            )
            values = products * score_scale + other_ref[other_block]
            local_top = jnp.max(values, axis=0, keepdims=True)
            old_top = top_ref[target]
            new_top = jnp.maximum(old_top, local_top)
            local_mass = jnp.sum(jnp.exp(values - new_top), axis=0, keepdims=True)
            mass_ref[target] = mass_ref[target] * jnp.exp(old_top - new_top) + local_mass
            top_ref[target] = new_top


def local_pass(along_rows, slots, images, prototypes, other_column):
    blocks = RB_DEV if along_rows else PB_DEV
    shape = jax.ShapeDtypeStruct((blocks, 1, TILE), jnp.float32)
    return pl.pallas_call(
        functools.partial(pass_kernel, along_rows),
        out_shape=(shape, shape),
        in_specs=slot_specs() + whole_specs(3),
        out_specs=tuple(whole_specs(2)),
    )(*slots, images, prototypes, other_column)


def final_kernel(rows_ref, protos_ref, valid_ref, images_ref, prototypes_ref,
                 col_ref, row_ref, col_lanes_ref, shares_ref, col_out, acc_ref):
    col_out[...] = col_lanes_ref[...]
    acc_ref[...] = jnp.zeros(acc_ref.shape, jnp.float32)
    score_scale = float(E) ** (-0.5)
    for position in range(MAXT):

        @pl.when(valid_ref[position] == 1)
        def _():
            row_block = rows_ref[position]
            proto_block = protos_ref[position]
            rows_here = images_ref[pl.ds(pl.multiple_of(row_block * TILE, TILE), TILE), :]
            protos_here = prototypes_ref[pl.ds(pl.multiple_of(proto_block * TILE, TILE), TILE), :]
            products = lax.dot_general(
                protos_here, rows_here, (((1,), (1,)), ((), ())), preferred_element_type=jnp.float32
            )
            weights = jnp.exp(
                products * score_scale + col_ref[proto_block] + row_ref[row_block]
            ).astype(jnp.bfloat16)
            acc_ref[proto_block] += jnp.dot(weights, rows_here, preferred_element_type=jnp.float32)

    half = TILE // 2
    for block in range(PB_DEV):
        for core in range(2):
            shares_ref[core, block] = acc_ref[block, core * half:(core + 1) * half, :].astype(
                jnp.bfloat16
            )


def final_pass(slots, images, prototypes, col_column, row_pot, col_pot):
    return pl.pallas_call(
        final_kernel,
        out_shape=(
            jax.ShapeDtypeStruct((2, PB_DEV, TILE // 2, E), jnp.bfloat16),
            jax.ShapeDtypeStruct(col_pot.shape, col_pot.dtype),
        ),
        in_specs=slot_specs() + whole_specs(5),
        out_specs=tuple(whole_specs(2)),
        scratch_shapes=[pltpu.VMEM((PB_DEV, TILE, E), jnp.float32)],
    )(*slots, images, prototypes, col_column, row_pot, col_pot)


def to_column(lanes):
    padded = jnp.concatenate(
        [lanes, jnp.zeros((8 - lanes.shape[0], TILE), jnp.float32)], axis=0
    ) if lanes.shape[0] < 8 else lanes
    return jnp.transpose(padded)


def stage_peer(axis, size, stride, step):
    me = lax.axis_index(axis)
    place = lax.rem(me // stride, size)
    return me + (lax.rem(place + step, size) - place) * stride, place


def exchange_stage(axis, size, stride, stage, local, packed, landed, send_sems, recv_sems):
    place = stage_peer(axis, size, stride, 0)[1]
    packed[...] = local
    landed[stage, place] = local

    def peer_copy(step, slot):
        return pltpu.make_async_remote_copy(
            src_ref=packed,
            dst_ref=landed.at[stage, slot],
            send_sem=send_sems.at[stage, lax.rem(place + step, size)],
            recv_sem=recv_sems.at[stage, slot],
            device_id={axis: stage_peer(axis, size, stride, step)[0]},
            device_id_type=pl.DeviceIdType.MESH,
        )

    def send(step, carry):
        peer_copy(step, place).start()
        return carry

    lax.fori_loop(1, size, send, 0)

    def receive(step, carry):
        peer_copy(size - step, lax.rem(place + size - step, size)).wait_recv()
        return carry

    lax.fori_loop(1, size, receive, 0)

    def drain(step, carry):
        peer_copy(step, place).wait_send()
        return carry

    lax.fori_loop(1, size, drain, 0)
    gathered = landed[stage]
    highest = jnp.max(gathered, axis=0)
    return highest + jnp.log(jnp.sum(jnp.exp(gathered - highest[None]), axis=0))


def exchange(axis, groups, stage, local, packed, landed_refs, send_refs, recv_refs):
    for (size, stride), landed, send_sems, recv_sems in zip(groups, landed_refs, send_refs,
                                                           recv_refs):
        local = exchange_stage(axis, size, stride, stage, local, packed, landed, send_sems,
                               recv_sems)
    return local


def pick_column(columns, chosen_block, blocks):
    picked = columns[:, 0:1]
    for block in range(1, blocks):
        picked = jnp.where(chosen_block == block, columns[:, block:block + 1], picked)
    return picked


def local_merge(along_rows, rows_ref, protos_ref, valid_ref, slot_images_ref, slot_protos_ref,
                other_columns):
    blocks = RB_DEV if along_rows else PB_DEV
    other_blocks = PB_DEV if along_rows else RB_DEV
    tops = [jnp.full((1, TILE), far_below, jnp.float32) for _ in range(blocks)]
    masses = [jnp.zeros((1, TILE), jnp.float32) for _ in range(blocks)]
    score_scale = float(E) ** (-0.5)
    for position in range(MAXT):
        row_block = rows_ref[position]
        proto_block = protos_ref[position]
        live = valid_ref[position] == 1
        rows_here = slot_images_ref[position]
        protos_here = slot_protos_ref[position]
        if along_rows:
            first, second, other_block, target = protos_here, rows_here, proto_block, row_block
        else:
            first, second, other_block, target = rows_here, protos_here, row_block, proto_block
        products = lax.dot_general(
            first, second, (((1,), (1,)), ((), ())), preferred_element_type=jnp.float32
        )
        values = products * score_scale + pick_column(other_columns, other_block, other_blocks)
        local_top = jnp.max(values, axis=0, keepdims=True)
        local_mass = jnp.sum(jnp.exp(values - local_top), axis=0, keepdims=True)
        for block in range(blocks):
            chosen = jnp.logical_and(live, target == block)
            new_top = jnp.maximum(tops[block], local_top)
            new_mass = masses[block] * jnp.exp(tops[block] - new_top) + local_mass * jnp.exp(
                local_top - new_top
            )
            tops[block] = jnp.where(chosen, new_top, tops[block])
            masses[block] = jnp.where(chosen, new_mass, masses[block])
    return jnp.maximum(
        jnp.concatenate(tops, axis=0) + jnp.log(jnp.concatenate(masses, axis=0)), far_below
    )


def axis_groups():
    proto_count = lax.axis_size("proto")
    img_count = lax.axis_size("img")
    return {
        "proto": ((PB_DEV, 1), (proto_count // PB_DEV, PB_DEV)),
        "img": ((2, 1), (img_count // 2, 2)),
    }


def sinkhorn_kernel(log_ratio, rows_ref, protos_ref, valid_ref, images_ref, prototypes_ref,
                    row_out, col_out, col_columns_out, row_packed, col_packed, *stage_refs):
    groups = axis_groups()
    row_refs = stage_refs[0:6]
    col_refs = stage_refs[6:12]
    barrier = pltpu.get_barrier_semaphore()
    greeted = 0
    for axis in ("proto", "img"):
        for size, stride in groups[axis]:

            def greet(step, carry):
                peer = stage_peer(axis, size, stride, step)[0]
                pl.semaphore_signal(barrier, inc=1, device_id={axis: peer},
                                    device_id_type=pl.DeviceIdType.MESH)
                return carry

            lax.fori_loop(1, size, greet, 0)
            greeted += size - 1
    pl.semaphore_wait(barrier, greeted)

    col_t = jnp.zeros((TILE, PB_DEV), jnp.float32)
    for iteration in range(ITERS):
        local = local_merge(True, rows_ref, protos_ref, valid_ref, images_ref, prototypes_ref,
                            col_t)
        merged = exchange("proto", groups["proto"], iteration, local, row_packed,
                          row_refs[0:2], row_refs[2:4], row_refs[4:6])
        row_pot = log_ratio - merged
        row_t = to_column(row_pot)
        local = local_merge(False, rows_ref, protos_ref, valid_ref, images_ref, prototypes_ref,
                            row_t)
        merged = exchange("img", groups["img"], iteration, local, col_packed,
                          col_refs[0:2], col_refs[2:4], col_refs[4:6])
        col_pot = -merged
        col_t = to_column(col_pot)
    for block in range(RB_DEV):
        row_out[block] = row_pot[block:block + 1]
    col_out[...] = col_pot
    for block in range(PB_DEV):
        col_columns_out[block] = col_t[:, block:block + 1]


def sinkhorn(slots, slot_images, slot_protos, log_ratio):
    groups = axis_groups()
    vmem = pltpu.VMEM
    stage_scratch = []
    for axis, blocks in (("proto", RB_DEV), ("img", PB_DEV)):
        sizes = [size for size, _ in groups[axis]]
        stage_scratch += [vmem((ITERS, size, blocks, TILE), jnp.float32) for size in sizes]
        stage_scratch += [pltpu.SemaphoreType.DMA((ITERS, size)) for size in sizes]
        stage_scratch += [pltpu.SemaphoreType.DMA((ITERS, size)) for size in sizes]
    return pl.pallas_call(
        functools.partial(sinkhorn_kernel, log_ratio),
        out_shape=(
            jax.ShapeDtypeStruct((RB_DEV, 1, TILE), jnp.float32),
            jax.ShapeDtypeStruct((PB_DEV, TILE), jnp.float32),
            jax.ShapeDtypeStruct((PB_DEV, TILE, 1), jnp.float32),
        ),
        in_specs=slot_specs() + whole_specs(2),
        out_specs=tuple(whole_specs(3)),
        scratch_shapes=[
            vmem((RB_DEV, TILE), jnp.float32),
            vmem((PB_DEV, TILE), jnp.float32),
        ] + stage_scratch,
        compiler_params=pltpu.CompilerParams(collective_id=0, has_side_effects=True),
    )(*slots, slot_images, slot_protos)


def scatter_kernel(shares_ref, out_ref, paired, pair_sums, landed, pair_sems, send_sems,
                   recv_sems):
    count = lax.axis_size("img")
    chips = count // 2
    me = lax.axis_index("img")
    core = lax.rem(me, 2)
    chip = me // 2
    partner = me + 1 - 2 * core
    barrier = pltpu.get_barrier_semaphore()
    pl.semaphore_signal(barrier, inc=1, device_id={"img": partner},
                        device_id_type=pl.DeviceIdType.MESH)

    def greet(step, carry):
        peer = lax.rem(chip + step, chips) * 2 + core
        pl.semaphore_signal(barrier, inc=1, device_id={"img": peer},
                            device_id_type=pl.DeviceIdType.MESH)
        return carry

    lax.fori_loop(1, chips, greet, 0)
    pl.semaphore_wait(barrier, chips)

    def pair_copy(piece):
        return pltpu.make_async_remote_copy(
            src_ref=shares_ref.at[1 - core, piece],
            dst_ref=paired.at[piece],
            send_sem=pair_sems.at[0, piece],
            recv_sem=pair_sems.at[1, piece],
            device_id={"img": partner},
            device_id_type=pl.DeviceIdType.MESH,
        )

    def peer_copy(peer_chip, slot):
        return pltpu.make_async_remote_copy(
            src_ref=pair_sums.at[peer_chip],
            dst_ref=landed.at[slot],
            send_sem=send_sems.at[peer_chip],
            recv_sem=recv_sems.at[slot],
            device_id={"img": peer_chip * 2 + core},
            device_id_type=pl.DeviceIdType.MESH,
        )

    def pair_send(step, carry):
        pair_copy(lax.rem(chip + step, chips)).start()
        return carry

    lax.fori_loop(1, chips + 1, pair_send, 0)

    def add_pair(piece):
        pair_copy(piece).wait_recv()
        pair_sums[piece] = (
            shares_ref[core, piece].astype(jnp.float32) + paired[piece].astype(jnp.float32)
        ).astype(jnp.bfloat16)

    def send(step, carry):
        piece = lax.rem(chip + step, chips)
        add_pair(piece)
        peer_copy(piece, chip).start()
        return carry

    lax.fori_loop(1, chips, send, 0)
    add_pair(chip)
    out_ref[chip] = pair_sums[chip]

    def receive(step, carry):
        source = lax.rem(chip + chips - step, chips)
        peer_copy(source, source).wait_recv()
        out_ref[source] = landed[source]
        return carry

    lax.fori_loop(1, chips, receive, 0)

    def drain(step, carry):
        peer_copy(lax.rem(chip + step, chips), chip).wait_send()
        return carry

    lax.fori_loop(1, chips, drain, 0)

    def pair_drain(step, carry):
        pair_copy(lax.rem(chip + step, chips)).wait_send()
        return carry

    lax.fori_loop(1, chips + 1, pair_drain, 0)


def scatter_sum(shares):
    cores, chips, rows, width = shares.shape
    half = (chips, rows, width)
    return pl.pallas_call(
        scatter_kernel,
        out_shape=jax.ShapeDtypeStruct(half, shares.dtype),
        in_specs=whole_specs(1),
        out_specs=pl.BlockSpec(memory_space=pltpu.VMEM),
        scratch_shapes=[
            pltpu.VMEM(half, shares.dtype),
            pltpu.VMEM(half, shares.dtype),
            pltpu.VMEM(half, shares.dtype),
            pltpu.SemaphoreType.DMA((2, chips)),
            pltpu.SemaphoreType.DMA((chips,)),
            pltpu.SemaphoreType.DMA((chips,)),
        ],
        compiler_params=pltpu.CompilerParams(collective_id=1, has_side_effects=True),
    )(shares)


def shards(images, prototypes, tile_row, tile_proto, tile_valid):
    img_count = lax.axis_size("img")
    proto_count = lax.axis_size("proto")
    slots = (tile_row.reshape(MAXT), tile_proto.reshape(MAXT), tile_valid.reshape(MAXT))
    log_ratio = math.log(PB_DEV * proto_count / (RB_DEV * img_count))
    slot_images = images.reshape(RB_DEV, TILE, E)[slots[0]]
    slot_protos = prototypes.reshape(PB_DEV, TILE, E)[slots[1]]
    row_pot, col_pot, col_columns = sinkhorn(slots, slot_images, slot_protos, log_ratio)
    partial_value, col_pot = final_pass(slots, images, prototypes, col_columns, row_pot, col_pot)
    proto_share = jnp.sum(scatter_sum(partial_value).astype(jnp.float32), axis=0)
    return (proto_share, col_pot.reshape(PB_DEV * TILE))


def solution(mesh):
    return jax.shard_map(
        shards,
        mesh=mesh,
        in_specs=(
            P("img", None),
            P("proto", None),
            P("img", "proto", None),
            P("img", "proto", None),
            P("img", "proto", None),
        ),
        out_specs=(P(("proto", "img"), None), P("proto")),
        check_vma=False,
    )
```

```python
import functools
import math

import jax
import jax.numpy as jnp
from jax import lax
from jax.experimental import pallas as pl
from jax.experimental.pallas import tpu as pltpu
from jax.sharding import PartitionSpec as P

E = 256
TILE = 512
RB_DEV = 4
PB_DEV = 8
MAXT = 6
ITERS = 3


far_below = -1e30


def running_top(values_of, live_slots, reduced, slot_blocks, block_count):

    def advance(position, tops):
        local_top = jnp.max(values_of(position), axis=reduced)
        target = slot_blocks[position]
        old_top = lax.dynamic_index_in_dim(tops, target, 0, keepdims=False)
        return lax.dynamic_update_index_in_dim(tops, jnp.maximum(old_top, local_top), target, 0)

    return lax.fori_loop(
        0, live_slots, advance, jnp.full((block_count, TILE), far_below, jnp.float32)
    )


def running_mass(values_of, live_slots, reduced, slot_blocks, tops):

    def advance(position, masses):
        target = slot_blocks[position]
        top_here = lax.dynamic_index_in_dim(tops, target, 0, keepdims=False)
        local_mass = jnp.sum(
            jnp.exp(values_of(position) - jnp.expand_dims(top_here, reduced)), axis=reduced
        )
        old_mass = lax.dynamic_index_in_dim(masses, target, 0, keepdims=False)
        return lax.dynamic_update_index_in_dim(masses, old_mass + local_mass, target, 0)

    return lax.fori_loop(0, live_slots, advance, jnp.zeros_like(tops))


def gather_kernel(axis, x_ref, out_ref, landed, send_sems, recv_sems):
    count = lax.axis_size(axis)
    me = lax.axis_index(axis)

    def peer_copy(peer, slot):
        return pltpu.make_async_remote_copy(
            src_ref=x_ref,
            dst_ref=landed.at[slot],
            send_sem=send_sems.at[slot],
            recv_sem=recv_sems.at[slot],
            device_id={axis: peer},
            device_id_type=pl.DeviceIdType.MESH,
        )

    landed[me] = x_ref[...]

    def send(step, carry):
        peer = lax.rem(me + step, count)
        peer_copy(peer, me).start()
        return carry

    lax.fori_loop(1, count, send, 0)

    def receive(step, carry):
        peer = lax.rem(me + count - step, count)
        peer_copy(peer, peer).wait_recv()
        return carry

    lax.fori_loop(1, count, receive, 0)

    def drain(step, carry):
        peer = lax.rem(me + step, count)
        peer_copy(peer, me).wait_send()
        return carry

    lax.fori_loop(1, count, drain, 0)
    out_ref[...] = landed[...]


def gather_peers(block, axis):
    count = lax.axis_size(axis)
    shape = (count,) + block.shape
    return pl.pallas_call(
        functools.partial(gather_kernel, axis),
        out_shape=jax.ShapeDtypeStruct(shape, block.dtype),
        in_specs=[pl.BlockSpec(memory_space=pltpu.VMEM)],
        out_specs=pl.BlockSpec(memory_space=pltpu.VMEM),
        scratch_shapes=[
            pltpu.VMEM(shape, block.dtype),
            pltpu.SemaphoreType.DMA((count,)),
            pltpu.SemaphoreType.DMA((count,)),
        ],
        compiler_params=pltpu.CompilerParams(has_side_effects=True),
    )(block)


def merge_tops(local_top, local_mass, axis):
    gathered = gather_peers(jnp.stack([local_top, local_mass]), axis)
    tops, masses = gathered[:, 0], gathered[:, 1]
    highest = jnp.max(tops, axis=0)
    summed = jnp.sum(masses * jnp.exp(tops - highest[None]), axis=0)
    return highest, summed


def slot_specs():
    return [pl.BlockSpec(memory_space=pltpu.SMEM)] * 3


def whole_specs(count):
    return [pl.BlockSpec(memory_space=pltpu.VMEM)] * count


def pass_kernel(along_rows, rows_ref, protos_ref, valid_ref, images_ref, prototypes_ref,
                other_ref, top_ref, mass_ref):
    top_ref[...] = jnp.full(top_ref.shape, far_below, jnp.float32)
    mass_ref[...] = jnp.zeros(mass_ref.shape, jnp.float32)
    score_scale = float(E) ** (-0.5)
    for position in range(MAXT):

        @pl.when(valid_ref[position] == 1)
        def _():
            row_block = rows_ref[position]
            proto_block = protos_ref[position]
            rows_here = images_ref[pl.ds(pl.multiple_of(row_block * TILE, TILE), TILE), :]
            protos_here = prototypes_ref[pl.ds(pl.multiple_of(proto_block * TILE, TILE), TILE), :]
            if along_rows:
                first, second, other_block, target = protos_here, rows_here, proto_block, row_block
            else:
                first, second, other_block, target = rows_here, protos_here, row_block, proto_block
            products = lax.dot_general(
                first, second, (((1,), (1,)), ((), ())), preferred_element_type=jnp.float32
            )
            values = products * score_scale + other_ref[other_block]
            local_top = jnp.max(values, axis=0, keepdims=True)
            old_top = top_ref[target]
            new_top = jnp.maximum(old_top, local_top)
            local_mass = jnp.sum(jnp.exp(values - new_top), axis=0, keepdims=True)
            mass_ref[target] = mass_ref[target] * jnp.exp(old_top - new_top) + local_mass
            top_ref[target] = new_top


def local_pass(along_rows, slots, images, prototypes, other_column):
    blocks = RB_DEV if along_rows else PB_DEV
    shape = jax.ShapeDtypeStruct((blocks, 1, TILE), jnp.float32)
    return pl.pallas_call(
        functools.partial(pass_kernel, along_rows),
        out_shape=(shape, shape),
        in_specs=slot_specs() + whole_specs(3),
        out_specs=tuple(whole_specs(2)),
    )(*slots, images, prototypes, other_column)


def final_kernel(rows_ref, protos_ref, valid_ref, images_ref, prototypes_ref,
                 col_ref, row_ref, shares_ref, acc_ref):
    acc_ref[...] = jnp.zeros(acc_ref.shape, jnp.float32)
    score_scale = float(E) ** (-0.5)
    for position in range(MAXT):

        @pl.when(valid_ref[position] == 1)
        def _():
            row_block = rows_ref[position]
            proto_block = protos_ref[position]
            rows_here = images_ref[pl.ds(pl.multiple_of(row_block * TILE, TILE), TILE), :]
            protos_here = prototypes_ref[pl.ds(pl.multiple_of(proto_block * TILE, TILE), TILE), :]
            products = lax.dot_general(
                protos_here, rows_here, (((1,), (1,)), ((), ())), preferred_element_type=jnp.float32
            )
            weights = jnp.exp(
                products * score_scale + col_ref[proto_block] + row_ref[row_block]
            ).astype(jnp.bfloat16)
            acc_ref[proto_block] += jnp.dot(weights, rows_here, preferred_element_type=jnp.float32)

    half = TILE // 2
    for block in range(PB_DEV):
        for core in range(2):
            shares_ref[core, block] = acc_ref[block, core * half:(core + 1) * half, :].astype(
                jnp.bfloat16
            )


def final_pass(slots, images, prototypes, col_column, row_pot):
    return pl.pallas_call(
        final_kernel,
        out_shape=jax.ShapeDtypeStruct((2, PB_DEV, TILE // 2, E), jnp.bfloat16),
        in_specs=slot_specs() + whole_specs(4),
        out_specs=pl.BlockSpec(memory_space=pltpu.VMEM),
        scratch_shapes=[pltpu.VMEM((PB_DEV, TILE, E), jnp.float32)],
    )(*slots, images, prototypes, col_column, row_pot)


def to_column(lanes):
    padded = jnp.concatenate(
        [lanes, jnp.zeros((8 - lanes.shape[0], TILE), jnp.float32)], axis=0
    ) if lanes.shape[0] < 8 else lanes
    return jnp.transpose(padded)


def stage_peer(axis, size, stride, step):
    me = lax.axis_index(axis)
    place = lax.rem(me // stride, size)
    return me + (lax.rem(place + step, size) - place) * stride, place


def exchange_stage(axis, size, stride, stage, local, packed, landed, send_sems, recv_sems):
    place = stage_peer(axis, size, stride, 0)[1]
    packed[...] = local
    landed[stage, place] = local

    def peer_copy(step, slot):
        return pltpu.make_async_remote_copy(
            src_ref=packed,
            dst_ref=landed.at[stage, slot],
            send_sem=send_sems.at[stage, lax.rem(place + step, size)],
            recv_sem=recv_sems.at[stage, slot],
            device_id={axis: stage_peer(axis, size, stride, step)[0]},
            device_id_type=pl.DeviceIdType.MESH,
        )

    def send(step, carry):
        peer_copy(step, place).start()
        return carry

    lax.fori_loop(1, size, send, 0)

    def receive(step, carry):
        peer_copy(size - step, lax.rem(place + size - step, size)).wait_recv()
        return carry

    lax.fori_loop(1, size, receive, 0)

    def drain(step, carry):
        peer_copy(step, place).wait_send()
        return carry

    lax.fori_loop(1, size, drain, 0)
    gathered = landed[stage]
    highest = jnp.max(gathered, axis=0)
    return highest + jnp.log(jnp.sum(jnp.exp(gathered - highest[None]), axis=0))


def exchange(axis, groups, stage, local, packed, landed_refs, send_refs, recv_refs):
    for (size, stride), landed, send_sems, recv_sems in zip(groups, landed_refs, send_refs,
                                                           recv_refs):
        local = exchange_stage(axis, size, stride, stage, local, packed, landed, send_sems,
                               recv_sems)
    return local


def pick_column(columns, chosen_block, blocks):
    picked = columns[:, 0:1]
    for block in range(1, blocks):
        picked = jnp.where(chosen_block == block, columns[:, block:block + 1], picked)
    return picked


def local_merge(along_rows, rows_ref, protos_ref, valid_ref, slot_images_ref, slot_protos_ref,
                other_columns):
    blocks = RB_DEV if along_rows else PB_DEV
    other_blocks = PB_DEV if along_rows else RB_DEV
    tops = [jnp.full((1, TILE), far_below, jnp.float32) for _ in range(blocks)]
    masses = [jnp.zeros((1, TILE), jnp.float32) for _ in range(blocks)]
    score_scale = float(E) ** (-0.5)
    for position in range(MAXT):
        row_block = rows_ref[position]
        proto_block = protos_ref[position]
        live = valid_ref[position] == 1
        rows_here = slot_images_ref[position]
        protos_here = slot_protos_ref[position]
        if along_rows:
            first, second, other_block, target = protos_here, rows_here, proto_block, row_block
        else:
            first, second, other_block, target = rows_here, protos_here, row_block, proto_block
        products = lax.dot_general(
            first, second, (((1,), (1,)), ((), ())), preferred_element_type=jnp.float32
        )
        values = products * score_scale + pick_column(other_columns, other_block, other_blocks)
        local_top = jnp.max(values, axis=0, keepdims=True)
        local_mass = jnp.sum(jnp.exp(values - local_top), axis=0, keepdims=True)
        for block in range(blocks):
            chosen = jnp.logical_and(live, target == block)
            new_top = jnp.maximum(tops[block], local_top)
            new_mass = masses[block] * jnp.exp(tops[block] - new_top) + local_mass * jnp.exp(
                local_top - new_top
            )
            tops[block] = jnp.where(chosen, new_top, tops[block])
            masses[block] = jnp.where(chosen, new_mass, masses[block])
    return jnp.maximum(
        jnp.concatenate(tops, axis=0) + jnp.log(jnp.concatenate(masses, axis=0)), far_below
    )


def axis_groups():
    proto_count = lax.axis_size("proto")
    img_count = lax.axis_size("img")
    return {
        "proto": ((PB_DEV, 1), (proto_count // PB_DEV, PB_DEV)),
        "img": ((2, 1), (img_count // 2, 2)),
    }


def sinkhorn_kernel(log_ratio, rows_ref, protos_ref, valid_ref, images_ref, prototypes_ref,
                    row_out, col_out, col_columns_out, row_packed, col_packed, *stage_refs):
    groups = axis_groups()
    row_refs = stage_refs[0:6]
    col_refs = stage_refs[6:12]
    barrier = pltpu.get_barrier_semaphore()
    greeted = 0
    for axis in ("proto", "img"):
        for size, stride in groups[axis]:

            def greet(step, carry):
                peer = stage_peer(axis, size, stride, step)[0]
                pl.semaphore_signal(barrier, inc=1, device_id={axis: peer},
                                    device_id_type=pl.DeviceIdType.MESH)
                return carry

            lax.fori_loop(1, size, greet, 0)
            greeted += size - 1

    col_t = jnp.zeros((TILE, PB_DEV), jnp.float32)
    for iteration in range(ITERS):
        local = local_merge(True, rows_ref, protos_ref, valid_ref, images_ref, prototypes_ref,
                            col_t)
        if iteration == 0:
            pl.semaphore_wait(barrier, greeted)
        merged = exchange("proto", groups["proto"], iteration, local, row_packed,
                          row_refs[0:2], row_refs[2:4], row_refs[4:6])
        row_pot = log_ratio - merged
        row_t = to_column(row_pot)
        local = local_merge(False, rows_ref, protos_ref, valid_ref, images_ref, prototypes_ref,
                            row_t)
        merged = exchange("img", groups["img"], iteration, local, col_packed,
                          col_refs[0:2], col_refs[2:4], col_refs[4:6])
        col_pot = -merged
        col_t = to_column(col_pot)
    for block in range(RB_DEV):
        row_out[block] = row_pot[block:block + 1]
    col_out[...] = col_pot
    for block in range(PB_DEV):
        col_columns_out[block] = col_t[:, block:block + 1]


def sinkhorn(slots, slot_images, slot_protos, log_ratio):
    groups = axis_groups()
    vmem = pltpu.VMEM
    stage_scratch = []
    for axis, blocks in (("proto", RB_DEV), ("img", PB_DEV)):
        sizes = [size for size, _ in groups[axis]]
        stage_scratch += [vmem((ITERS, size, blocks, TILE), jnp.float32) for size in sizes]
        stage_scratch += [pltpu.SemaphoreType.DMA((ITERS, size)) for size in sizes]
        stage_scratch += [pltpu.SemaphoreType.DMA((ITERS, size)) for size in sizes]
    return pl.pallas_call(
        functools.partial(sinkhorn_kernel, log_ratio),
        out_shape=(
            jax.ShapeDtypeStruct((RB_DEV, 1, TILE), jnp.float32),
            jax.ShapeDtypeStruct((PB_DEV, TILE), jnp.float32),
            jax.ShapeDtypeStruct((PB_DEV, TILE, 1), jnp.float32),
        ),
        in_specs=slot_specs() + whole_specs(2),
        out_specs=tuple(whole_specs(3)),
        scratch_shapes=[
            vmem((RB_DEV, TILE), jnp.float32),
            vmem((PB_DEV, TILE), jnp.float32),
        ] + stage_scratch,
        compiler_params=pltpu.CompilerParams(collective_id=0, has_side_effects=True),
    )(*slots, slot_images, slot_protos)


def scatter_kernel(shares_ref, out_ref, paired, pair_sums, landed, pair_sems, send_sems,
                   recv_sems):
    count = lax.axis_size("img")
    chips = count // 2
    me = lax.axis_index("img")
    core = lax.rem(me, 2)
    chip = me // 2
    partner = me + 1 - 2 * core
    barrier = pltpu.get_barrier_semaphore()
    pl.semaphore_signal(barrier, inc=1, device_id={"img": partner},
                        device_id_type=pl.DeviceIdType.MESH)

    def greet(step, carry):
        peer = lax.rem(chip + step, chips) * 2 + core
        pl.semaphore_signal(barrier, inc=1, device_id={"img": peer},
                            device_id_type=pl.DeviceIdType.MESH)
        return carry

    lax.fori_loop(1, chips, greet, 0)
    pl.semaphore_wait(barrier, chips)

    def pair_copy(piece):
        return pltpu.make_async_remote_copy(
            src_ref=shares_ref.at[1 - core, piece],
            dst_ref=paired.at[piece],
            send_sem=pair_sems.at[0, piece],
            recv_sem=pair_sems.at[1, piece],
            device_id={"img": partner},
            device_id_type=pl.DeviceIdType.MESH,
        )

    def peer_copy(peer_chip, slot):
        return pltpu.make_async_remote_copy(
            src_ref=pair_sums.at[peer_chip],
            dst_ref=landed.at[slot],
            send_sem=send_sems.at[peer_chip],
            recv_sem=recv_sems.at[slot],
            device_id={"img": peer_chip * 2 + core},
            device_id_type=pl.DeviceIdType.MESH,
        )

    def pair_send(step, carry):
        pair_copy(lax.rem(chip + step, chips)).start()
        return carry

    lax.fori_loop(1, chips + 1, pair_send, 0)

    def add_pair(piece):
        pair_copy(piece).wait_recv()
        pair_sums[piece] = (
            shares_ref[core, piece].astype(jnp.float32) + paired[piece].astype(jnp.float32)
        ).astype(jnp.bfloat16)

    def send(step, carry):
        piece = lax.rem(chip + step, chips)
        add_pair(piece)
        peer_copy(piece, chip).start()
        return carry

    lax.fori_loop(1, chips, send, 0)
    add_pair(chip)
    out_ref[...] = pair_sums[chip].astype(jnp.float32)

    def receive(step, carry):
        source = lax.rem(chip + chips - step, chips)
        peer_copy(source, source).wait_recv()
        out_ref[...] += landed[source].astype(jnp.float32)
        return carry

    lax.fori_loop(1, chips, receive, 0)

    def drain(step, carry):
        peer_copy(lax.rem(chip + step, chips), chip).wait_send()
        return carry

    lax.fori_loop(1, chips, drain, 0)

    def pair_drain(step, carry):
        pair_copy(lax.rem(chip + step, chips)).wait_send()
        return carry

    lax.fori_loop(1, chips + 1, pair_drain, 0)


def scatter_sum(shares):
    cores, chips, rows, width = shares.shape
    half = (chips, rows, width)
    return pl.pallas_call(
        scatter_kernel,
        out_shape=jax.ShapeDtypeStruct((rows, width), jnp.float32),
        in_specs=whole_specs(1),
        out_specs=pl.BlockSpec(memory_space=pltpu.VMEM),
        scratch_shapes=[
            pltpu.VMEM(half, shares.dtype),
            pltpu.VMEM(half, shares.dtype),
            pltpu.VMEM(half, shares.dtype),
            pltpu.SemaphoreType.DMA((2, chips)),
            pltpu.SemaphoreType.DMA((chips,)),
            pltpu.SemaphoreType.DMA((chips,)),
        ],
        compiler_params=pltpu.CompilerParams(collective_id=1, has_side_effects=True),
    )(shares)


def shards(images, prototypes, tile_row, tile_proto, tile_valid):
    img_count = lax.axis_size("img")
    proto_count = lax.axis_size("proto")
    slots = (tile_row.reshape(MAXT), tile_proto.reshape(MAXT), tile_valid.reshape(MAXT))
    log_ratio = math.log(PB_DEV * proto_count / (RB_DEV * img_count))
    slot_images = images.reshape(RB_DEV, TILE, E)[slots[0]]
    slot_protos = prototypes.reshape(PB_DEV, TILE, E)[slots[1]]
    row_pot, col_pot, col_columns = sinkhorn(slots, slot_images, slot_protos, log_ratio)
    partial_value = final_pass(slots, images, prototypes, col_columns, row_pot)
    proto_share = scatter_sum(partial_value)
    return (proto_share, col_pot.reshape(PB_DEV * TILE))


def solution(mesh):
    return jax.shard_map(
        shards,
        mesh=mesh,
        in_specs=(
            P("img", None),
            P("proto", None),
            P("img", "proto", None),
            P("img", "proto", None),
            P("img", "proto", None),
        ),
        out_specs=(P(("proto", "img"), None), P("proto")),
        check_vma=False,
    )
```

```python
import functools
import math

import jax
import jax.numpy as jnp
from jax import lax
from jax.experimental import pallas as pl
from jax.experimental.pallas import tpu as pltpu
from jax.sharding import PartitionSpec as P

E = 256
TILE = 512
RB_DEV = 4
PB_DEV = 8
MAXT = 6
ITERS = 3


far_below = -1e30


def running_top(values_of, live_slots, reduced, slot_blocks, block_count):

    def advance(position, tops):
        local_top = jnp.max(values_of(position), axis=reduced)
        target = slot_blocks[position]
        old_top = lax.dynamic_index_in_dim(tops, target, 0, keepdims=False)
        return lax.dynamic_update_index_in_dim(tops, jnp.maximum(old_top, local_top), target, 0)

    return lax.fori_loop(
        0, live_slots, advance, jnp.full((block_count, TILE), far_below, jnp.float32)
    )


def running_mass(values_of, live_slots, reduced, slot_blocks, tops):

    def advance(position, masses):
        target = slot_blocks[position]
        top_here = lax.dynamic_index_in_dim(tops, target, 0, keepdims=False)
        local_mass = jnp.sum(
            jnp.exp(values_of(position) - jnp.expand_dims(top_here, reduced)), axis=reduced
        )
        old_mass = lax.dynamic_index_in_dim(masses, target, 0, keepdims=False)
        return lax.dynamic_update_index_in_dim(masses, old_mass + local_mass, target, 0)

    return lax.fori_loop(0, live_slots, advance, jnp.zeros_like(tops))


def gather_kernel(axis, x_ref, out_ref, landed, send_sems, recv_sems):
    count = lax.axis_size(axis)
    me = lax.axis_index(axis)

    def peer_copy(peer, slot):
        return pltpu.make_async_remote_copy(
            src_ref=x_ref,
            dst_ref=landed.at[slot],
            send_sem=send_sems.at[slot],
            recv_sem=recv_sems.at[slot],
            device_id={axis: peer},
            device_id_type=pl.DeviceIdType.MESH,
        )

    landed[me] = x_ref[...]

    def send(step, carry):
        peer = lax.rem(me + step, count)
        peer_copy(peer, me).start()
        return carry

    lax.fori_loop(1, count, send, 0)

    def receive(step, carry):
        peer = lax.rem(me + count - step, count)
        peer_copy(peer, peer).wait_recv()
        return carry

    lax.fori_loop(1, count, receive, 0)

    def drain(step, carry):
        peer = lax.rem(me + step, count)
        peer_copy(peer, me).wait_send()
        return carry

    lax.fori_loop(1, count, drain, 0)
    out_ref[...] = landed[...]


def gather_peers(block, axis):
    count = lax.axis_size(axis)
    shape = (count,) + block.shape
    return pl.pallas_call(
        functools.partial(gather_kernel, axis),
        out_shape=jax.ShapeDtypeStruct(shape, block.dtype),
        in_specs=[pl.BlockSpec(memory_space=pltpu.VMEM)],
        out_specs=pl.BlockSpec(memory_space=pltpu.VMEM),
        scratch_shapes=[
            pltpu.VMEM(shape, block.dtype),
            pltpu.SemaphoreType.DMA((count,)),
            pltpu.SemaphoreType.DMA((count,)),
        ],
        compiler_params=pltpu.CompilerParams(has_side_effects=True),
    )(block)


def merge_tops(local_top, local_mass, axis):
    gathered = gather_peers(jnp.stack([local_top, local_mass]), axis)
    tops, masses = gathered[:, 0], gathered[:, 1]
    highest = jnp.max(tops, axis=0)
    summed = jnp.sum(masses * jnp.exp(tops - highest[None]), axis=0)
    return highest, summed


def slot_specs():
    return [pl.BlockSpec(memory_space=pltpu.SMEM)] * 3


def whole_specs(count):
    return [pl.BlockSpec(memory_space=pltpu.VMEM)] * count


def pass_kernel(along_rows, rows_ref, protos_ref, valid_ref, images_ref, prototypes_ref,
                other_ref, top_ref, mass_ref):
    top_ref[...] = jnp.full(top_ref.shape, far_below, jnp.float32)
    mass_ref[...] = jnp.zeros(mass_ref.shape, jnp.float32)
    score_scale = float(E) ** (-0.5)
    for position in range(MAXT):

        @pl.when(valid_ref[position] == 1)
        def _():
            row_block = rows_ref[position]
            proto_block = protos_ref[position]
            rows_here = images_ref[pl.ds(pl.multiple_of(row_block * TILE, TILE), TILE), :]
            protos_here = prototypes_ref[pl.ds(pl.multiple_of(proto_block * TILE, TILE), TILE), :]
            if along_rows:
                first, second, other_block, target = protos_here, rows_here, proto_block, row_block
            else:
                first, second, other_block, target = rows_here, protos_here, row_block, proto_block
            products = lax.dot_general(
                first, second, (((1,), (1,)), ((), ())), preferred_element_type=jnp.float32
            )
            values = products * score_scale + other_ref[other_block]
            local_top = jnp.max(values, axis=0, keepdims=True)
            old_top = top_ref[target]
            new_top = jnp.maximum(old_top, local_top)
            local_mass = jnp.sum(jnp.exp(values - new_top), axis=0, keepdims=True)
            mass_ref[target] = mass_ref[target] * jnp.exp(old_top - new_top) + local_mass
            top_ref[target] = new_top


def local_pass(along_rows, slots, images, prototypes, other_column):
    blocks = RB_DEV if along_rows else PB_DEV
    shape = jax.ShapeDtypeStruct((blocks, 1, TILE), jnp.float32)
    return pl.pallas_call(
        functools.partial(pass_kernel, along_rows),
        out_shape=(shape, shape),
        in_specs=slot_specs() + whole_specs(3),
        out_specs=tuple(whole_specs(2)),
    )(*slots, images, prototypes, other_column)


def final_kernel(rows_ref, protos_ref, valid_ref, images_ref, prototypes_ref,
                 col_ref, row_ref, shares_ref, acc_ref):
    acc_ref[...] = jnp.zeros(acc_ref.shape, jnp.float32)
    score_scale = float(E) ** (-0.5)
    for position in range(MAXT):

        @pl.when(valid_ref[position] == 1)
        def _():
            row_block = rows_ref[position]
            proto_block = protos_ref[position]
            rows_here = images_ref[pl.ds(pl.multiple_of(row_block * TILE, TILE), TILE), :]
            protos_here = prototypes_ref[pl.ds(pl.multiple_of(proto_block * TILE, TILE), TILE), :]
            products = lax.dot_general(
                protos_here, rows_here, (((1,), (1,)), ((), ())), preferred_element_type=jnp.float32
            )
            col_column = pick_column(to_column(col_ref[...]), proto_block, PB_DEV)
            weights = jnp.exp(
                products * score_scale + col_column + row_ref[row_block]
            ).astype(jnp.bfloat16)
            acc_ref[proto_block] += jnp.dot(weights, rows_here, preferred_element_type=jnp.float32)

    half = TILE // 2
    for block in range(PB_DEV):
        for core in range(2):
            shares_ref[core, block] = acc_ref[block, core * half:(core + 1) * half, :].astype(
                jnp.bfloat16
            )


def final_pass(slots, images, prototypes, col_column, row_pot):
    return pl.pallas_call(
        final_kernel,
        out_shape=jax.ShapeDtypeStruct((2, PB_DEV, TILE // 2, E), jnp.bfloat16),
        in_specs=slot_specs() + whole_specs(4),
        out_specs=pl.BlockSpec(memory_space=pltpu.VMEM),
        scratch_shapes=[pltpu.VMEM((PB_DEV, TILE, E), jnp.float32)],
    )(*slots, images, prototypes, col_column, row_pot)


def to_column(lanes):
    padded = jnp.concatenate(
        [lanes, jnp.zeros((8 - lanes.shape[0], TILE), jnp.float32)], axis=0
    ) if lanes.shape[0] < 8 else lanes
    return jnp.transpose(padded)


def stage_peer(axis, size, stride, step):
    me = lax.axis_index(axis)
    place = lax.rem(me // stride, size)
    return me + (lax.rem(place + step, size) - place) * stride, place


def exchange_stage(axis, size, stride, stage, local, packed, landed, send_sems, recv_sems):
    place = stage_peer(axis, size, stride, 0)[1]
    packed[...] = local
    landed[stage, place] = local

    def peer_copy(step, slot):
        return pltpu.make_async_remote_copy(
            src_ref=packed,
            dst_ref=landed.at[stage, slot],
            send_sem=send_sems.at[stage, lax.rem(place + step, size)],
            recv_sem=recv_sems.at[stage, slot],
            device_id={axis: stage_peer(axis, size, stride, step)[0]},
            device_id_type=pl.DeviceIdType.MESH,
        )

    def send(step, carry):
        peer_copy(step, place).start()
        return carry

    lax.fori_loop(1, size, send, 0)

    def receive(step, carry):
        peer_copy(size - step, lax.rem(place + size - step, size)).wait_recv()
        return carry

    lax.fori_loop(1, size, receive, 0)

    def drain(step, carry):
        peer_copy(step, place).wait_send()
        return carry

    lax.fori_loop(1, size, drain, 0)
    gathered = landed[stage]
    highest = jnp.max(gathered, axis=0)
    return highest + jnp.log(jnp.sum(jnp.exp(gathered - highest[None]), axis=0))


def exchange(axis, groups, stage, local, packed, landed_refs, send_refs, recv_refs):
    for (size, stride), landed, send_sems, recv_sems in zip(groups, landed_refs, send_refs,
                                                           recv_refs):
        local = exchange_stage(axis, size, stride, stage, local, packed, landed, send_sems,
                               recv_sems)
    return local


def pick_column(columns, chosen_block, blocks):
    picked = columns[:, 0:1]
    for block in range(1, blocks):
        picked = jnp.where(chosen_block == block, columns[:, block:block + 1], picked)
    return picked


def local_merge(along_rows, rows_ref, protos_ref, valid_ref, slot_images_ref, slot_protos_ref,
                other_columns):
    blocks = RB_DEV if along_rows else PB_DEV
    other_blocks = PB_DEV if along_rows else RB_DEV
    tops = [jnp.full((1, TILE), far_below, jnp.float32) for _ in range(blocks)]
    masses = [jnp.zeros((1, TILE), jnp.float32) for _ in range(blocks)]
    score_scale = float(E) ** (-0.5)
    for position in range(MAXT):
        row_block = rows_ref[position]
        proto_block = protos_ref[position]
        live = valid_ref[position] == 1
        rows_here = slot_images_ref[position]
        protos_here = slot_protos_ref[position]
        if along_rows:
            first, second, other_block, target = protos_here, rows_here, proto_block, row_block
        else:
            first, second, other_block, target = rows_here, protos_here, row_block, proto_block
        products = lax.dot_general(
            first, second, (((1,), (1,)), ((), ())), preferred_element_type=jnp.float32
        )
        values = products * score_scale + pick_column(other_columns, other_block, other_blocks)
        local_top = jnp.max(values, axis=0, keepdims=True)
        local_mass = jnp.sum(jnp.exp(values - local_top), axis=0, keepdims=True)
        for block in range(blocks):
            chosen = jnp.logical_and(live, target == block)
            new_top = jnp.maximum(tops[block], local_top)
            new_mass = masses[block] * jnp.exp(tops[block] - new_top) + local_mass * jnp.exp(
                local_top - new_top
            )
            tops[block] = jnp.where(chosen, new_top, tops[block])
            masses[block] = jnp.where(chosen, new_mass, masses[block])
    return jnp.maximum(
        jnp.concatenate(tops, axis=0) + jnp.log(jnp.concatenate(masses, axis=0)), far_below
    )


def axis_groups():
    proto_count = lax.axis_size("proto")
    img_count = lax.axis_size("img")
    return {
        "proto": ((PB_DEV, 1), (proto_count // PB_DEV, PB_DEV)),
        "img": ((2, 1), (img_count // 2, 2)),
    }


def sinkhorn_kernel(log_ratio, rows_ref, protos_ref, valid_ref, images_ref, prototypes_ref,
                    row_out, col_out, col_columns_out, row_packed, col_packed, *stage_refs):
    groups = axis_groups()
    row_refs = stage_refs[0:6]
    col_refs = stage_refs[6:12]
    barrier = pltpu.get_barrier_semaphore()
    greeted = 0
    for axis in ("proto", "img"):
        for size, stride in groups[axis]:

            def greet(step, carry):
                peer = stage_peer(axis, size, stride, step)[0]
                pl.semaphore_signal(barrier, inc=1, device_id={axis: peer},
                                    device_id_type=pl.DeviceIdType.MESH)
                return carry

            lax.fori_loop(1, size, greet, 0)
            greeted += size - 1
    pl.semaphore_wait(barrier, greeted)

    col_t = jnp.zeros((TILE, PB_DEV), jnp.float32)
    for iteration in range(ITERS):
        local = local_merge(True, rows_ref, protos_ref, valid_ref, images_ref, prototypes_ref,
                            col_t)
        merged = exchange("proto", groups["proto"], iteration, local, row_packed,
                          row_refs[0:2], row_refs[2:4], row_refs[4:6])
        row_pot = log_ratio - merged
        row_t = to_column(row_pot)
        local = local_merge(False, rows_ref, protos_ref, valid_ref, images_ref, prototypes_ref,
                            row_t)
        merged = exchange("img", groups["img"], iteration, local, col_packed,
                          col_refs[0:2], col_refs[2:4], col_refs[4:6])
        col_pot = -merged
        col_t = to_column(col_pot)
    for block in range(RB_DEV):
        row_out[block] = row_pot[block:block + 1]
    col_out[...] = col_pot
    col_columns_out[...] = jnp.zeros(col_columns_out.shape, jnp.float32)


def sinkhorn(slots, slot_images, slot_protos, log_ratio):
    groups = axis_groups()
    vmem = pltpu.VMEM
    stage_scratch = []
    for axis, blocks in (("proto", RB_DEV), ("img", PB_DEV)):
        sizes = [size for size, _ in groups[axis]]
        stage_scratch += [vmem((ITERS, size, blocks, TILE), jnp.float32) for size in sizes]
        stage_scratch += [pltpu.SemaphoreType.DMA((ITERS, size)) for size in sizes]
        stage_scratch += [pltpu.SemaphoreType.DMA((ITERS, size)) for size in sizes]
    return pl.pallas_call(
        functools.partial(sinkhorn_kernel, log_ratio),
        out_shape=(
            jax.ShapeDtypeStruct((RB_DEV, 1, TILE), jnp.float32),
            jax.ShapeDtypeStruct((PB_DEV, TILE), jnp.float32),
            jax.ShapeDtypeStruct((1, TILE), jnp.float32),
        ),
        in_specs=slot_specs() + whole_specs(2),
        out_specs=tuple(whole_specs(3)),
        scratch_shapes=[
            vmem((RB_DEV, TILE), jnp.float32),
            vmem((PB_DEV, TILE), jnp.float32),
        ] + stage_scratch,
        compiler_params=pltpu.CompilerParams(collective_id=0, has_side_effects=True),
    )(*slots, slot_images, slot_protos)


def scatter_kernel(shares_ref, out_ref, paired, pair_sums, landed, pair_sems, send_sems,
                   recv_sems):
    count = lax.axis_size("img")
    chips = count // 2
    me = lax.axis_index("img")
    core = lax.rem(me, 2)
    chip = me // 2
    partner = me + 1 - 2 * core
    barrier = pltpu.get_barrier_semaphore()
    pl.semaphore_signal(barrier, inc=1, device_id={"img": partner},
                        device_id_type=pl.DeviceIdType.MESH)

    def greet(step, carry):
        peer = lax.rem(chip + step, chips) * 2 + core
        pl.semaphore_signal(barrier, inc=1, device_id={"img": peer},
                            device_id_type=pl.DeviceIdType.MESH)
        return carry

    lax.fori_loop(1, chips, greet, 0)
    pl.semaphore_wait(barrier, chips)

    def pair_copy(piece):
        return pltpu.make_async_remote_copy(
            src_ref=shares_ref.at[1 - core, piece],
            dst_ref=paired.at[piece],
            send_sem=pair_sems.at[0, piece],
            recv_sem=pair_sems.at[1, piece],
            device_id={"img": partner},
            device_id_type=pl.DeviceIdType.MESH,
        )

    def peer_copy(peer_chip, slot):
        return pltpu.make_async_remote_copy(
            src_ref=pair_sums.at[peer_chip],
            dst_ref=landed.at[slot],
            send_sem=send_sems.at[peer_chip],
            recv_sem=recv_sems.at[slot],
            device_id={"img": peer_chip * 2 + core},
            device_id_type=pl.DeviceIdType.MESH,
        )

    def pair_send(step, carry):
        pair_copy(lax.rem(chip + step, chips)).start()
        return carry

    lax.fori_loop(1, chips + 1, pair_send, 0)

    def add_pair(piece):
        pair_copy(piece).wait_recv()
        pair_sums[piece] = (
            shares_ref[core, piece].astype(jnp.float32) + paired[piece].astype(jnp.float32)
        ).astype(jnp.bfloat16)

    def send(step, carry):
        piece = lax.rem(chip + step, chips)
        add_pair(piece)
        peer_copy(piece, chip).start()
        return carry

    lax.fori_loop(1, chips, send, 0)
    add_pair(chip)
    out_ref[...] = pair_sums[chip].astype(jnp.float32)

    def receive(step, carry):
        source = lax.rem(chip + chips - step, chips)
        peer_copy(source, source).wait_recv()
        out_ref[...] += landed[source].astype(jnp.float32)
        return carry

    lax.fori_loop(1, chips, receive, 0)

    def drain(step, carry):
        peer_copy(lax.rem(chip + step, chips), chip).wait_send()
        return carry

    lax.fori_loop(1, chips, drain, 0)

    def pair_drain(step, carry):
        pair_copy(lax.rem(chip + step, chips)).wait_send()
        return carry

    lax.fori_loop(1, chips + 1, pair_drain, 0)


def scatter_sum(shares):
    cores, chips, rows, width = shares.shape
    half = (chips, rows, width)
    return pl.pallas_call(
        scatter_kernel,
        out_shape=jax.ShapeDtypeStruct((rows, width), jnp.float32),
        in_specs=whole_specs(1),
        out_specs=pl.BlockSpec(memory_space=pltpu.VMEM),
        scratch_shapes=[
            pltpu.VMEM(half, shares.dtype),
            pltpu.VMEM(half, shares.dtype),
            pltpu.VMEM(half, shares.dtype),
            pltpu.SemaphoreType.DMA((2, chips)),
            pltpu.SemaphoreType.DMA((chips,)),
            pltpu.SemaphoreType.DMA((chips,)),
        ],
        compiler_params=pltpu.CompilerParams(collective_id=1, has_side_effects=True),
    )(shares)


def shards(images, prototypes, tile_row, tile_proto, tile_valid):
    img_count = lax.axis_size("img")
    proto_count = lax.axis_size("proto")
    slots = (tile_row.reshape(MAXT), tile_proto.reshape(MAXT), tile_valid.reshape(MAXT))
    log_ratio = math.log(PB_DEV * proto_count / (RB_DEV * img_count))
    slot_images = images.reshape(RB_DEV, TILE, E)[slots[0]]
    slot_protos = prototypes.reshape(PB_DEV, TILE, E)[slots[1]]
    row_pot, col_pot, col_columns = sinkhorn(slots, slot_images, slot_protos, log_ratio)
    partial_value = final_pass(slots, images, prototypes, col_pot, row_pot)
    proto_share = scatter_sum(partial_value)
    return (proto_share, col_pot.reshape(PB_DEV * TILE))


def solution(mesh):
    return jax.shard_map(
        shards,
        mesh=mesh,
        in_specs=(
            P("img", None),
            P("proto", None),
            P("img", "proto", None),
            P("img", "proto", None),
            P("img", "proto", None),
        ),
        out_specs=(P(("proto", "img"), None), P("proto")),
        check_vma=False,
    )
```
